32 devices in a mesh: branch: 2 (over x), dp: 16 (over z, y, core).
Axes of the slice: x: 2, y: 2, z: 4, core: 2. Of those that a mesh axis runs over, the one named last changes fastest.
Arguments:
- inputs: bfloat16 [96, 816, 512], P('dp'), may hold values from -6 to 6
- window_count: int32 [16], P('dp'), may hold values from 1 to 6, as said below
- branch_blocks: bfloat16 [2, 2, 23552, 512], P('branch', None, 'dp')
- branch_gains: float32 [2, 512], P('branch'), may hold values from 0.1 to 1.9
- branch_biases: float32 [2, 4, 512], P('branch'), may hold values from -2.5 to 2.5
- merge_weight: bfloat16 [1024, 512], replicated, may hold values from -0.1875 to 0.1875
- ff_in: bfloat16 [512, 2048], replicated, may hold values from -0.25 to 0.25
- ff_in_bias: float32 [2048], replicated, may hold values from -2.5 to 2.5
- ff_out: bfloat16 [2048, 512], replicated, may hold values from -0.25 to 0.25
- shared_biases: float32 [4, 512], replicated, may hold values from -2.5 to 2.5
- shared_gains: float32 [2, 512], replicated, may hold values from 0.1 to 1.9
- d_out: bfloat16 [48, 2, 1, 816, 512], P('dp', 'branch'), may hold values from -6 to 6
Outputs:
- layer_out: bfloat16 [48, 2, 1, 816, 512], P('dp', 'branch')
- grad_inputs: bfloat16 [48, 2, 1, 816, 512], P('dp', 'branch')
- grad_branch_blocks: float32 [2, 2, 23552, 512], P('branch', None, 'dp')
- grad_branch_gains: float32 [2, 512], P('branch')
- grad_branch_biases: float32 [2, 4, 512], P('branch')
- grad_merge_weight: float32 [1024, 512], replicated
- grad_ff_in: float32 [512, 2048], replicated
- grad_ff_in_bias: float32 [2048], replicated
- grad_ff_out: float32 [2048, 512], replicated
- grad_shared_biases: float32 [4, 512], replicated
- grad_shared_gains: float32 [2, 512], replicated
The draws below stay inside these ranges and needn't reach their ends.
Inputs may be any that keep to these rules, and one draw needn't show every extreme that they name: window_count[j] is the number of live windows among windows j * 6 to (j + 1) * 6 - 1, the live ones first; at least one entry equals 6.
All inputs are finite; a program needn't handle non-finite values.
Results may differ from the reference program's by a relative error of at most 0.015.
Values may be sent and summed in bfloat16 or wider, within the bound.
A program may use at most 512 MiB of HBM per device.

```python
import jax
import jax.numpy as jnp
from jax import lax

D = 512
FF = 2048
SCALE_A = 12
SCALE_B = 16
SEQ = 816
MICRO = 3
WIN_MICRO = 2
GRAD_GROUPS = 2
BLOCKS = 92
GROUP_ROWS = 23552
SLOTS = 6
WINDOWS = 96
OUT_GROUPS = 48
N_DP = 16


def draw_window_count(key, part):
    left_key, right_key, peak_key = jax.random.split(key, 3)
    left_draw = jax.random.randint(left_key, (N_DP,), 0, SLOTS)
    right_draw = jax.random.randint(right_key, (N_DP,), 0, SLOTS)
    counts = 1 + left_draw * right_draw // SLOTS
    peak_index = jax.random.randint(peak_key, (), 0, N_DP)
    return jnp.where(jnp.arange(N_DP) == peak_index, SLOTS, counts).astype(jnp.int32)


def region_scale(block_ids, stride):
    tap_count = SEQ // stride
    return jnp.where(block_ids < stride, (stride * D) ** (-0.5), jnp.where(block_ids < stride + tap_count, 1.5 * (tap_count * D) ** (-0.5), jnp.where(block_ids < 2 * stride + tap_count, 1.5 * D ** (-0.5), 0.02)))


def draw_branch_blocks(key, part):
    gaussian = jnp.clip(jax.random.normal(key, (2, GRAD_GROUPS, GROUP_ROWS, D), jnp.float32), -6.0, 6.0)
    group_ids = jnp.arange(GRAD_GROUPS)[:, None]
    row_ids = jnp.arange(GROUP_ROWS)[None, :]
    block_ids = group_ids * (GROUP_ROWS // D) + row_ids // D
    factor = jnp.stack([region_scale(block_ids, SCALE_A), region_scale(block_ids, SCALE_B)])
    return (gaussian * factor[:, :, :, None]).astype(jnp.bfloat16)


def level_of(own_key, extent, cuts, low, high):
    factor_of, own = 1.0, jax.random.fold_in(own_key, 6)
    for position, blocks in cuts:
        draws = jnp.exp(jax.random.uniform(jax.random.fold_in(own, position), (blocks,), jnp.float32, low / len(cuts), high / len(cuts)))
        factor_of = factor_of * jnp.repeat(draws, extent[position] // blocks).reshape([-1 if axis == position else 1 for axis in range(len(extent))])
    return factor_of


def bell_draw(rng, shape, width, reach, cuts=(), kind=jnp.bfloat16):
    factor_of = level_of(rng, shape, cuts, -0.22, 0.18) if cuts else 1.0
    array = jax.random.normal(rng, shape, jnp.float32) * width * factor_of
    return jnp.minimum(jnp.maximum(array, -reach), reach).astype(kind)


def setup_inputs(seed: int = 0) -> dict:
    arg_keys = jax.random.split(jax.random.key(seed), 13)
    inputs = bell_draw(arg_keys[0], (WINDOWS, SEQ, D), 1.0, 6.0, ((0, 16),))
    window_count = draw_window_count(jax.random.fold_in(arg_keys[12], 71), 0)
    branch_blocks = draw_branch_blocks(jax.random.fold_in(arg_keys[12], 71), 0)
    branch_gains = jnp.clip(1.0 + 0.18 * jax.random.normal(arg_keys[3], (2, D), jnp.float32), 0.1, 1.9)
    branch_biases = bell_draw(arg_keys[4], (2, 4, D), 0.3, 2.5, ((0, 2),), jnp.float32)
    merge_weight = bell_draw(arg_keys[5], (2 * D, D), (2 * D) ** -0.5, 0.1875)
    ff_in = bell_draw(arg_keys[6], (D, FF), D ** -0.5, 0.25)
    ff_in_bias = bell_draw(arg_keys[7], (FF,), 0.3, 2.5, (), jnp.float32)
    ff_out = bell_draw(arg_keys[8], (FF, D), (FF // 4) ** -0.5, 0.25)
    shared_biases = bell_draw(arg_keys[9], (4, D), 0.3, 2.5, (), jnp.float32)
    shared_gains = jnp.clip(1.0 + 0.18 * jax.random.normal(arg_keys[10], (2, D), jnp.float32), 0.1, 1.9)
    d_out = bell_draw(arg_keys[11], (OUT_GROUPS, 2, WIN_MICRO // 2, SEQ, D), 1.0, 6.0, ((0, 16), (1, 2)))
    return {"inputs": inputs, "window_count": window_count, "branch_blocks": branch_blocks, "branch_gains": branch_gains, "branch_biases": branch_biases, "merge_weight": merge_weight, "ff_in": ff_in, "ff_in_bias": ff_in_bias, "ff_out": ff_out, "shared_biases": shared_biases, "shared_gains": shared_gains, "d_out": d_out}


PRECISE = lax.Precision.HIGHEST
EPSILON = 1e-05

@jax.custom_vjp
def low(v):
    return lax.optimization_barrier(v.astype(jnp.bfloat16)).astype(jnp.float32)

@jax.custom_vjp
def low_back(v):
    return v

def low_keep(v):
    return (low(v), None)

def low_pass(kept, grad):
    return (grad,)

def back_keep(v):
    return (v, None)

def back_low(kept, grad):
    return (low(grad),)
low.defvjp(low_keep, low_pass)
low_back.defvjp(back_keep, back_low)

def layer_norm(values, norm_gain, norm_shift):
    centre = values - lax.optimization_barrier(jnp.mean(values, axis=-1, keepdims=True))
    spread = lax.optimization_barrier(jnp.mean(centre * centre, axis=-1, keepdims=True))
    return centre * lax.rsqrt(spread + EPSILON) * norm_gain + norm_shift

def gelu_exact(values):
    return jax.nn.gelu(values, approximate=False)

def past_windows(values, tap_count):
    batch_size = values.shape[0]
    channels = values.shape[2]
    padded = jnp.concatenate([jnp.zeros((batch_size, tap_count - 1, channels), jnp.float32), values], axis=1)
    offsets = (jnp.arange(tap_count)[:, None] + jnp.arange(tap_count)[None, :]).astype(jnp.int32)
    return padded[:, offsets, :]

def branch(values, blocks, norm_gain, biases, stride):
    batch_size = values.shape[0]
    tap_count = SEQ // stride
    down_weight = blocks[:stride]
    iso_weight = blocks[stride:stride + tap_count]
    up_weight = blocks[stride + tap_count:2 * stride + tap_count]
    tap_rows = values.reshape(batch_size, tap_count, stride, D)
    pre_down = low_back(jnp.einsum('btrd,rdo->bto', tap_rows, down_weight, precision=PRECISE) + biases[0])
    activation = low(jnp.tanh(pre_down))
    windows = past_windows(activation, tap_count)
    pre_iso = low_back(jnp.einsum('btsd,sdo->bto', windows, iso_weight, precision=PRECISE) + biases[1])
    isometric = low(jnp.tanh(pre_iso))
    expanded = jnp.einsum('bte,red->btrd', isometric, up_weight, precision=PRECISE).reshape(batch_size, SEQ, D)
    expanded = low_back(expanded + biases[2])
    return layer_norm(expanded + values, norm_gain, biases[3])

def block_layer(weights, values):
    blocks, branch_gains, branch_biases, merge_weight, ff_in, ff_in_bias, ff_out, shared_biases, shared_gains = weights
    first_out = low_back(low(branch(values, blocks[0], branch_gains[0], branch_biases[0], SCALE_A)))
    second_out = low_back(low(branch(values, blocks[1], branch_gains[1], branch_biases[1], SCALE_B)))
    joined = jnp.concatenate([first_out, second_out], axis=-1)
    merged = low_back(jnp.einsum('btk,ko->bto', joined, merge_weight, precision=PRECISE) + shared_biases[0])
    normed = low(layer_norm(merged, shared_gains[0], shared_biases[1]))
    inner_pre = low_back(jnp.einsum('btd,df->btf', normed, ff_in, precision=PRECISE) + ff_in_bias)
    hidden = low(gelu_exact(inner_pre))
    outer_pre = low_back(jnp.einsum('btf,fd->btd', hidden, ff_out, precision=PRECISE) + shared_biases[2])
    return layer_norm(merged + outer_pre, shared_gains[1], shared_biases[3])

def reference(inputs, window_count, branch_blocks, branch_gains, branch_biases, merge_weight, ff_in, ff_in_bias, ff_out, shared_biases, shared_gains, d_out):
    params = (branch_blocks.astype(jnp.float32).reshape(2, BLOCKS, D, D), branch_gains.astype(jnp.float32), branch_biases.astype(jnp.float32), merge_weight.astype(jnp.float32), ff_in.astype(jnp.float32), ff_in_bias.astype(jnp.float32), ff_out.astype(jnp.float32), shared_biases.astype(jnp.float32), shared_gains.astype(jnp.float32))
    window_ids = jnp.arange(WINDOWS).astype(jnp.int32)
    owners = (window_ids // SLOTS).astype(jnp.int32)
    alive_all = (window_ids % SLOTS < window_count[owners]).astype(jnp.float32)
    values_all = inputs.astype(jnp.float32).reshape(N_DP, SLOTS, SEQ, D)
    cotangent_all = d_out.astype(jnp.float32).reshape(N_DP, SLOTS, SEQ, D)
    alive_blocks = alive_all.reshape(N_DP, SLOTS)
    initial = jax.tree.map(jnp.zeros_like, params)

    def step_block(running, block):
        block_values, block_cotangent, block_alive = block

        def forward(weights, inputs_now):
            return block_layer(weights, inputs_now) * block_alive[:, None, None]
        result, pullback = jax.vjp(forward, params, block_values)
        weight_grads, value_grads = pullback(block_cotangent)
        return (jax.tree.map(jnp.add, running, weight_grads), (result, value_grads))
    totals, (results, value_grads) = lax.scan(step_block, initial, (values_all, cotangent_all, alive_blocks))
    out_shape = (N_DP * MICRO, 2, WIN_MICRO // 2, SEQ, D)
    return (results.reshape(out_shape).astype(jnp.bfloat16), value_grads.reshape(out_shape).astype(jnp.bfloat16), totals[0].reshape(2, GRAD_GROUPS, GROUP_ROWS, D), totals[1], totals[2], totals[3], totals[4], totals[5], totals[6], totals[7], totals[8])
```

```python
import functools
import jax, jax.numpy as jnp
from jax import lax
from jax.experimental import pallas as pl
from jax.experimental.pallas import tpu as pltpu

MESH = pl.DeviceIdType.MESH
ANY = pl.BlockSpec(memory_space=pl.ANY)


def place():
    me = lax.axis_index("dp")
    return lax.axis_index("branch"), me, me // 4, (me // 2) % 2, me % 2


def meet(depth, b, me, z):
    barrier = pltpu.get_barrier_semaphore()
    y, c = (me // 2) % 2, me % 2
    pl.semaphore_signal(barrier, 1, device_id=(b, me + 1 - 2 * c), device_id_type=MESH)
    pl.semaphore_signal(barrier, 1, device_id=(b, me + 2 - 4 * y), device_id_type=MESH)

    @pl.when(z > 0)
    def _():
        pl.semaphore_signal(barrier, 1, device_id=(b, me - 4), device_id_type=MESH)

    @pl.when(z < depth - 1)
    def _():
        pl.semaphore_signal(barrier, 1, device_id=(b, me + 4), device_id_type=MESH)

    count = 2 + jnp.where(z > 0, 1, 0) + jnp.where(z < depth - 1, 1, 0)
    pl.semaphore_wait(barrier, count)


def gather_body(depth, npd, rows, base, ranges, swaps, src, dst, hold, local_sem, recv_sem, send_sem):
    b, me, z, y, c = place()
    meet(depth, b, me, z)
    (a0, a1), (b0, b1) = ranges
    q0 = jnp.where(b == 0, a0, b0)
    q1 = jnp.where(b == 0, a1, b1)
    swap = jnp.where(b == 0, swaps[0], swaps[1])
    core_peer, y_peer = (b, me + 1 - 2 * c), (b, me + 2 - 4 * y)

    def chunk(ref, index):
        return ref.at[pl.ds(pl.multiple_of(index * rows, 8), rows), :]

    def own(i):
        return src.at[pl.ds(pl.multiple_of(base + i * rows, 8), rows), :]

    def remote(kind, q, device, from_own=False):
        k = q - q0
        return pltpu.make_async_remote_copy(
            own(q - me * npd) if from_own else chunk(dst, k), chunk(dst, k), send_sem.at[kind, k], recv_sem.at[k],
            device_id=device, device_id_type=MESH,
        )

    def each_own(what):
        for i in range(npd):
            q = me * npd + i

            @pl.when(jnp.logical_and(q >= q0, q < q1))
            def _():
                what(q, i)

    def take(q, i):
        return pltpu.make_async_copy(own(i), hold.at[i], local_sem.at[0, i])

    def put(q, i):
        return pltpu.make_async_copy(hold.at[i], chunk(dst, q - q0), local_sem.at[1, i])

    each_own(lambda q, i: take(q, i).start())

    def column(j):
        ys = (j // 2) % 2
        return jnp.where(j == swap, 1 - ys, ys)

    def each(core, steps, what):
        def over(zs, t, s):
            for ys in (y, 1 - y):
                j = (zs * 2 + ys) * 2 + core
                col = column(j)
                i = s - t - jnp.where(ys != col, 1, 0) - jnp.where(y != col, 1, 0)
                i = jnp.where(jnp.logical_and(t == 0, ys == y), s, i)
                q = j * npd + i

                @pl.when(jnp.logical_and(jnp.logical_and(i >= 0, i < npd), jnp.logical_and(q >= q0, q < q1)))
                def _():
                    what(q, j)

        def over_steps(s, carry):
            def over_far(t, inner):
                @pl.when(z >= t)
                def _():
                    over(z - t, t, s)

                @pl.when(jnp.logical_and(z + t < depth, t > 0))
                def _():
                    over(z + t, t, s)

                return inner

            return lax.fori_loop(0, depth, over_far, carry)

        lax.fori_loop(0, npd + depth + 1, over_steps, 0)

    def sends(q, j, act, from_own=False):
        zs, ys = j // 4, (j // 2) % 2
        col = column(j)
        chain = y == col

        @pl.when(jnp.logical_and(chain, jnp.logical_and(z >= zs, z < depth - 1)))
        def _():
            act(remote(0, q, (b, me + 4), from_own))

        @pl.when(jnp.logical_and(chain, jnp.logical_and(z <= zs, z > 0)))
        def _():
            act(remote(1, q, (b, me - 4), from_own))

        start_here = jnp.logical_and(z == zs, ys != col)

        @pl.when(chain != start_here)
        def _():
            act(remote(2, q, y_peer, from_own))

        act(remote(3, q, core_peer, from_own))

    def forward(q, j):
        @pl.when(me == j)
        def _():
            sends(q, j, lambda copy: copy.start(), True)

        @pl.when(me != j)
        def _():
            remote(3, q, core_peer).wait_recv()
            sends(q, j, lambda copy: copy.start())

    each(c, npd + depth + 1, forward)

    def swap_own(q, i):
        take(q, i).wait()
        put(q, i).start()

    each_own(swap_own)

    def finish(q, carry):
        j = q // npd

        @pl.when(c == j % 2)
        def _():
            sends(q, j, lambda copy: copy.wait_send())

        @pl.when(c != j % 2)
        def _():
            remote(3, q, core_peer).wait_recv()

        return carry

    lax.fori_loop(q0, q1, finish, 0)
    each_own(lambda q, i: put(q, i).wait())


def gather_rows(mesh, src, base, rows, npd, ranges, collective_id, swaps=(-1, -1)):
    depth = mesh.shape["dp"] // 4
    count = max(r[1] - r[0] for r in ranges)
    return pl.pallas_call(
        functools.partial(gather_body, depth, npd, rows, base, ranges, swaps),
        out_shape=jax.ShapeDtypeStruct((count * rows, src.shape[1]), src.dtype),
        in_specs=[ANY],
        out_specs=ANY,
        scratch_shapes=[
            pltpu.VMEM((npd, rows, src.shape[1]), src.dtype),
            pltpu.SemaphoreType.DMA((2, npd)),
            pltpu.SemaphoreType.DMA((count,)),
            pltpu.SemaphoreType.DMA((4, count)),
        ],
        compiler_params=pltpu.CompilerParams(collective_id=collective_id, has_side_effects=True),
    )(src)


def reduce_body(depth, npd, rows, ranges, swaps, lag, src, out, own, rc, ry, rz, fin, acc, own_sem, rc_sem, ry_sem, rz_sem, fin_sem, send_sem, fin_send):
    b, me, z, y, c = place()
    meet(depth, b, me, z)
    (a0, a1), (b0, b1) = ranges
    q0 = jnp.where(b == 0, a0, b0)
    q1 = jnp.where(b == 0, a1, b1)
    swap = jnp.where(b == 0, swaps[0], swaps[1])
    pair0 = q0 // npd // 2
    core_peer, y_peer = (b, me + 1 - 2 * c), (b, me + 2 - 4 * y)
    up, down = (b, jnp.minimum(me + 4, 4 * depth - 1)), (b, jnp.maximum(me - 4, 0))

    def column(j):
        ys = (j // 2) % 2
        return jnp.where(j == swap, 1 - ys, ys)

    def slot(j, i):
        return (j // 2 - pair0) * npd + i

    def part(j, i):
        return src.at[pl.ds(pl.multiple_of((j * npd + i - q0) * rows, 8), rows), :]

    def keep(j, i):
        return pltpu.make_async_copy(part(j, i), own.at[slot(j, i)], own_sem.at[slot(j, i)])

    def remote(kind, frm, to, sem, k, device):
        return pltpu.make_async_remote_copy(
            frm, to, send_sem.at[kind, k], sem, device_id=device, device_id_type=MESH
        )

    def to_core(j, i):
        k = slot(j, i)
        return remote(0, part(j, i), rc.at[k], rc_sem.at[k], k, core_peer)

    def to_y(j, i):
        k = slot(j, i)
        return remote(1, own.at[k], ry.at[k], ry_sem.at[k], k, y_peer)

    def to_z(j, i, way):
        k = slot(j, i)
        return remote(2, own.at[k], rz.at[way, k], rz_sem.at[way, k], k, (up, down)[way])

    def to_owner(j, i):
        return pltpu.make_async_remote_copy(
            own.at[slot(j, i)], fin.at[i], fin_send.at[i], fin_sem.at[i], device_id=y_peer, device_id_type=MESH
        )

    def owners(n, core, what):
        pos, i = n // npd, n % npd
        rising = pos + jnp.where(pos >= z, 1, 0)
        falling = depth - 1 - pos
        falling = falling - jnp.where(falling <= z, 1, 0)
        zs = jnp.where(pos == depth - 1, z, jnp.where(z >= depth // 2, rising, falling))
        for ys in (0, 1):
            j = (zs * 2 + ys) * 2 + core
            q = j * npd + i

            @pl.when(jnp.logical_and(q >= q0, q < q1))
            def _():
                what(j, i, zs, ys)

    total = depth * npd

    def begin(n, carry):
        owners(n, 1 - c, lambda j, i, zs, ys: to_core(j, i).start())
        owners(n, c, lambda j, i, zs, ys: keep(j, i).start())
        return carry

    lax.fori_loop(0, total, begin, 0)

    def cross(j, i, zs, ys):
        @pl.when(column(j) != y)
        def _():
            k = slot(j, i)
            keep(j, i).wait()
            to_core(j, i).wait_recv()
            own[k] = (own[k].astype(jnp.float32) + rc[k].astype(jnp.float32)).astype(own.dtype)
            to_y(j, i).start()

    def chain(j, i, zs, ys):
        @pl.when(column(j) == y)
        def _():
            k = slot(j, i)
            keep(j, i).wait()
            to_core(j, i).wait_recv()
            to_y(j, i).wait_recv()
            acc[...] = own[k].astype(jnp.float32) + rc[k].astype(jnp.float32) + ry[k].astype(jnp.float32)

            @pl.when(jnp.logical_and(z >= zs, z < depth - 1))
            def _():
                to_z(j, i, 1).wait_recv()
                acc[...] += rz[1, k].astype(jnp.float32)

            @pl.when(jnp.logical_and(z <= zs, z > 0))
            def _():
                to_z(j, i, 0).wait_recv()
                acc[...] += rz[0, k].astype(jnp.float32)

            @pl.when(jnp.logical_and(z == zs, ys == y))
            def _():
                out[i] = acc[...].astype(out.dtype)

            @pl.when(jnp.logical_not(jnp.logical_and(z == zs, ys == y)))
            def _():
                own[k] = acc[...].astype(own.dtype)

            @pl.when(z > zs)
            def _():
                to_z(j, i, 1).start()

            @pl.when(z < zs)
            def _():
                to_z(j, i, 0).start()

            @pl.when(jnp.logical_and(z == zs, ys != y))
            def _():
                to_owner(j, i).start()

    def step(s, carry):
        @pl.when(s < total)
        def _():
            owners(s, c, cross)

        @pl.when(s >= lag)
        def _():
            owners(s - lag, c, chain)

        return carry

    lax.fori_loop(0, total + lag, step, 0)

    def sent(j, i, zs, ys):
        @pl.when(column(j) != y)
        def _():
            to_y(j, i).wait_send()

            @pl.when(me == j)
            def _():
                to_owner(j, i).wait_recv()
                out[i] = fin[i].astype(out.dtype)

        @pl.when(column(j) == y)
        def _():
            @pl.when(z != zs)
            def _():
                to_z(j, i, 0).wait_send()

            @pl.when(jnp.logical_and(z == zs, ys != y))
            def _():
                to_owner(j, i).wait_send()

    def end(n, carry):
        owners(n, 1 - c, lambda j, i, zs, ys: to_core(j, i).wait_send())
        owners(n, c, sent)
        return carry

    lax.fori_loop(0, total, end, 0)


def reduce_rows(mesh, src, rows, npd, ranges, collective_id, dtype, swaps=(-1, -1), lag=2):
    depth = mesh.shape["dp"] // 4
    pairs = max((r[1] + npd - 1) // npd // 2 + (r[1] + npd - 1) // npd % 2 - r[0] // npd // 2 for r in ranges)
    held, width = pairs * npd, src.shape[1]
    block = (held, rows, width)
    return pl.pallas_call(
        functools.partial(reduce_body, depth, npd, rows, ranges, swaps, lag),
        out_shape=jax.ShapeDtypeStruct((npd, rows, width), dtype),
        in_specs=[ANY],
        out_specs=pl.BlockSpec(memory_space=pltpu.VMEM),
        scratch_shapes=[
            pltpu.VMEM(block, src.dtype),
            pltpu.VMEM(block, src.dtype),
            pltpu.VMEM(block, src.dtype),
            pltpu.VMEM((2, *block), src.dtype),
            pltpu.VMEM((npd, rows, width), src.dtype),
            pltpu.VMEM((rows, width), jnp.float32),
            pltpu.SemaphoreType.DMA((held,)),
            pltpu.SemaphoreType.DMA((held,)),
            pltpu.SemaphoreType.DMA((held,)),
            pltpu.SemaphoreType.DMA((2, held)),
            pltpu.SemaphoreType.DMA((npd,)),
            pltpu.SemaphoreType.DMA((3, held)),
            pltpu.SemaphoreType.DMA((npd,)),
        ],
        compiler_params=pltpu.CompilerParams(
            collective_id=collective_id, has_side_effects=True, vmem_limit_bytes=50 * 2**20
        ),
    )(src)
SCALES = (12, 16)
MICRO = 3
GROUPS = 2
EPSILON = 1e-05
BF, F32 = jnp.bfloat16, jnp.float32
MIB = 2**20


def up_to(value, step):
    return (value + step - 1) // step * step


def dot(a, b):
    return jnp.dot(a, b, preferred_element_type=F32)


def dot_bt(a, b):
    return lax.dot_general(a, b, (((1,), (1,)), ((), ())), preferred_element_type=F32)


def dot_at(a, b):
    return lax.dot_general(a, b, (((0,), (0,)), ((), ())), preferred_element_type=F32)


def mean(values):
    return jnp.mean(values, axis=-1, keepdims=True)


def normalise(values):
    centre = values - mean(values)
    rho = lax.rsqrt(mean(centre * centre) + EPSILON)
    return centre * rho, rho


def norm_back(q_gain, xhat, rho):
    return rho * (q_gain - mean(q_gain) - xhat * mean(q_gain * xhat))


def column_sum(values):
    return jnp.sum(values, axis=0, keepdims=True)


VMEM = pl.BlockSpec(memory_space=pltpu.VMEM)


def whole_call(body, out_shape, scratch, limit, cost=None):
    return pl.pallas_call(
        body,
        out_shape=out_shape,
        out_specs=jax.tree.map(lambda _: VMEM, out_shape),
        scratch_shapes=scratch,
        compiler_params=pltpu.CompilerParams(vmem_limit_bytes=limit * MIB),
        cost_estimate=cost,
    )


LANES = 128


def panels(ref, lead, rows):
    return jnp.concatenate([ref[(*lead, p, rows, slice(None))] for p in range(ref.shape[-3])], axis=1)


def set_panels(ref, lead, rows, values):
    for p in range(ref.shape[-3]):
        ref[(*lead, p, rows, slice(None))] = values[:, p * LANES : (p + 1) * LANES]


def down_body(k, n, pitch, off, x, weight, bias, pre, act, taps, spread):
    slots, length, width = x.shape
    many = slots * pitch
    spread[:, length:, :] = jnp.zeros((spread.shape[0], spread.shape[1] - length, LANES), F32)

    def window(w, carry):
        set_panels(spread, (), slice(0, length), x[w].astype(F32))
        for r in range(k):
            taps[pl.ds(pl.multiple_of(w * pitch, 16), pitch), r * width : (r + 1) * width] = panels(
                spread, (), pl.ds(r, pitch, stride=k)
            ).astype(BF)
        return carry

    lax.fori_loop(0, slots, window, 0)
    total = dot(taps[:many, : k * width], weight[off : off + k * width, :]) + bias[0:1, :]
    tall = pre.shape[1]
    for w in range(slots):
        rows = fit(total[w * pitch : (w + 1) * pitch], tall)
        pre[w] = rows
        step = lax.broadcasted_iota(jnp.int32, rows.shape, 0)
        act[w] = jnp.where(step < n, jnp.tanh(rows), 0.0).astype(BF)


def fit(values, tall):
    rows = values.shape[0]
    if rows >= tall:
        return values[:tall]
    return jnp.concatenate([values, jnp.zeros((tall - rows, values.shape[1]), values.dtype)], axis=0)


def expand(k, n, pitch, off, iso_rows, weight, spread):
    width = iso_rows.shape[1]
    slots = spread.shape[0]

    def tap(r, carry):
        rows = dot(iso_rows[...], weight[pl.ds(pl.multiple_of(off + r * width, 16), width), :])
        for w in range(slots):
            set_panels(spread, (w,), pl.ds(r, pitch, stride=k), rows[w * pitch : (w + 1) * pitch])
        return carry

    lax.fori_loop(0, k, tap, 0)


def iso_of(n, pitch, pre_iso, bias):
    rows = fit(jnp.tanh(pre_iso + bias[1:2, :]), pitch)
    step = lax.broadcasted_iota(jnp.int32, rows.shape, 0)
    return jnp.where(step < n, rows, 0.0)


def up_body(k, n, pitch, off, live, pre_iso, weight, x, gain, bias, out, iso_rows, spread):
    slots, length, width = x.shape
    for w in range(slots):
        iso = iso_of(n, pitch, pre_iso[w], bias)
        iso_rows[w * pitch : (w + 1) * pitch, :] = jnp.where(w < live[0], iso, 0.0).astype(BF)
    expand(k, n, pitch, off, iso_rows, weight, spread)

    def window(w, carry):
        values = panels(spread, (w,), slice(0, length)) + bias[2:3, :] + x[w].astype(F32)
        xhat, _ = normalise(values)
        out[w] = (xhat * gain[0:1, :] + bias[3:4, :]).astype(BF)
        return carry

    lax.fori_loop(0, slots, window, 0)


def up_back_body(k, n, pitch, off, live, grad, pre_iso, weight, x, gain, bias, grad_iso, vectors, grad_taps, part, iso_rows, spread):
    slots, length, width = x.shape
    for w in range(slots):
        iso = iso_of(n, pitch, pre_iso[w], bias)
        iso_rows[w * pitch : (w + 1) * pitch, :] = jnp.where(w < live[0], iso, 0.0).astype(BF)
    expand(k, n, pitch, off, iso_rows, weight, spread)
    vectors[...] = jnp.zeros_like(vectors)

    def window(w, carry):
        values = panels(spread, (w,), slice(0, length)) + bias[2:3, :] + x[w].astype(F32)
        xhat, rho = normalise(values)
        q = grad[w].astype(F32)
        residual = norm_back(q * gain[0:1, :], xhat, rho)
        set_panels(spread, (w,), slice(0, length), residual)
        vectors[0:1, :] += column_sum(q * xhat)
        vectors[3:4, :] += column_sum(residual.astype(BF).astype(F32))
        vectors[4:5, :] += column_sum(q)
        return carry

    lax.fori_loop(0, slots, window, 0)

    def tap(w, carry):
        for r in range(k):
            grad_taps[pl.ds(pl.multiple_of(w * pitch, 16), pitch), r * width : (r + 1) * width] = panels(
                spread, (w,), pl.ds(r, pitch, stride=k)
            ).astype(BF)
        return carry

    lax.fori_loop(0, slots, tap, 0)
    total = jnp.zeros((slots * pitch, width), F32)
    for r in range(k):
        rows = grad_taps[: slots * pitch, r * width : (r + 1) * width]
        total += dot_bt(rows, weight[off + r * width : off + (r + 1) * width, :])
        part[off + r * width : off + (r + 1) * width, :] = dot_at(iso_rows[...], rows).astype(BF)
    tall = grad_iso.shape[1]
    for w in range(slots):
        iso = iso_of(n, pitch, pre_iso[w], bias)
        slope = jnp.where(lax.broadcasted_iota(jnp.int32, iso.shape, 0) < n, 1.0 - iso * iso, 0.0)
        back = total[w * pitch : (w + 1) * pitch] * slope
        back = jnp.where(w < live[0], back, 0.0).astype(BF)
        vectors[2:3, :] += column_sum(back.astype(F32))
        grad_iso[w] = fit(back.astype(F32), tall).astype(BF)


def down_back_body(k, n, pitch, off, live, grad_act, pre, grad_taps, taps, weight, out, vector, part, rows, spread):
    slots, length, width = out.shape
    vector[...] = jnp.zeros_like(vector)
    for w in range(slots):
        act = jnp.tanh(fit(pre[w], pitch))
        step = lax.broadcasted_iota(jnp.int32, act.shape, 0)
        back = fit(grad_act[w], pitch) * (1.0 - act * act)
        back = jnp.where(jnp.logical_and(step < n, w < live[0]), back, 0.0).astype(BF)
        vector[...] += column_sum(back.astype(F32))
        rows[w * pitch : (w + 1) * pitch, :] = back
    for r in range(k):
        back = dot_bt(rows[...], weight[off + r * width : off + (r + 1) * width, :])
        back += grad_taps[: slots * pitch, r * width : (r + 1) * width].astype(F32)
        for w in range(slots):
            set_panels(spread, (w,), pl.ds(r, pitch, stride=k), back[w * pitch : (w + 1) * pitch])
        part[off + r * width : off + (r + 1) * width, :] = dot_at(
            taps[: slots * pitch, r * width : (r + 1) * width], rows[...]
        ).astype(BF)

    def window(w, carry):
        out[w] = panels(spread, (w,), slice(0, length)).astype(BF)
        return carry

    lax.fori_loop(0, slots, window, 0)


SUBLANES = 8


def shifted(copies, start, tall):
    rows = pl.multiple_of(start // SUBLANES * SUBLANES, SUBLANES)
    return copies[start % SUBLANES, pl.ds(rows, tall), :].astype(BF)


def late_copies(copies, values):
    tall = values.shape[0]
    for b in range(SUBLANES):
        copies[b, tall - b : 2 * tall - b, :] = values


def early_copies(copies, values):
    tall = values.shape[0]
    for b in range(SUBLANES):
        copies[b, : tall - b, :] = values[b:]


PACK = 8


def iso_specs(tall, width, pieces):
    def spec(e):
        def at(step, order, count, shift):
            last = jnp.maximum(count[0] - 1, 0) // PACK
            return order[jnp.minimum(step, last) * PACK + e], 0, 0

        return pl.BlockSpec((1, tall, width), at)

    return [spec(e) for e in range(PACK)]


def scatter_out(order, count, slots_ref, sem, out, tall, step, steps):
    def copy(at, e):
        where = jnp.minimum(at * PACK + e, order.shape[0] - 1)
        return pltpu.make_async_copy(
            slots_ref.at[at % 2, e], out.at[order[where]], sem.at[at % 2, e]
        )

    live = pl.cdiv(count[0], PACK)

    @pl.when(step < live)
    def _():
        for e in range(PACK):
            @pl.when(step * PACK + e < count[0])
            def _():
                copy(step, e).start()

    @pl.when(jnp.logical_and(step >= 1, step <= live))
    def _():
        for e in range(PACK):
            @pl.when((step - 1) * PACK + e < count[0])
            def _():
                copy(step - 1, e).wait()

    @pl.when(jnp.logical_and(step == steps - 1, live == steps))
    def _():
        for e in range(PACK):
            @pl.when(step * PACK + e < count[0])
            def _():
                copy(step, e).wait()


def iso_forward_body(tall, pitch, blocks, steps, order, count, shift, *refs):
    acts, (weight, out, buffer, columns, ready, sem) = refs[:PACK], refs[PACK:]
    step = pl.program_id(0)
    width = weight.shape[1]

    @pl.when(step == 0)
    def _():
        buffer[...] = jnp.zeros_like(buffer)
        columns[...] = jnp.zeros_like(columns)

    @pl.when(step * PACK < count[0])
    def _():
        for e in range(PACK):
            late_copies(buffer, jnp.where(step * PACK + e < count[0], acts[e][0].astype(F32), 0.0))
            for m in range(blocks):
                columns[e * pitch : e * pitch + tall, m * width : (m + 1) * width] = shifted(buffer, tall - shift[m], tall)
        total = dot(columns[...], weight[...])
        for e in range(PACK):
            ready[step % 2, e] = total[e * pitch : e * pitch + tall].astype(BF)

    scatter_out(order, count, ready, sem, out, tall, step, steps)


def iso_back_body(tall, pitch, blocks, steps, order, count, shift, *refs):
    acts, grads = refs[:PACK], refs[PACK : 2 * PACK]
    weight, out, kernel_grad, buffer, columns, gathered, ahead, ready, sem = refs[2 * PACK :]
    step = pl.program_id(0)
    width = weight.shape[1]

    @pl.when(step == 0)
    def _():
        buffer[...] = jnp.zeros_like(buffer)
        columns[...] = jnp.zeros_like(columns)
        gathered[...] = jnp.zeros_like(gathered)
        ahead[...] = jnp.zeros_like(ahead)
        kernel_grad[...] = jnp.zeros_like(kernel_grad)

    @pl.when(step * PACK < count[0])
    def _():
        for e in range(PACK):
            alive = step * PACK + e < count[0]
            late_copies(buffer, jnp.where(alive, acts[e][0].astype(F32), 0.0))
            for m in range(blocks):
                columns[e * pitch : e * pitch + tall, m * width : (m + 1) * width] = shifted(buffer, tall - shift[m], tall)
            gathered[e * pitch : e * pitch + tall, :] = jnp.where(alive, grads[e][0].astype(F32), 0.0).astype(BF)
        for m in range(blocks):
            kernel_grad[m * width : (m + 1) * width, :] += dot_at(columns[:, m * width : (m + 1) * width], gathered[...])
        for e in range(PACK):
            alive = step * PACK + e < count[0]
            early_copies(ahead, jnp.where(alive, grads[e][0].astype(F32), 0.0))
            for m in range(blocks):
                columns[e * pitch : e * pitch + tall, m * width : (m + 1) * width] = shifted(ahead, shift[m], tall)
        total = dot_bt(columns[:, :width], weight[:width, :])
        for m in range(1, blocks):
            total += dot_bt(columns[:, m * width : (m + 1) * width], weight[m * width : (m + 1) * width, :])
        for e in range(PACK):
            ready[step % 2, e] = total[e * pitch : e * pitch + tall].astype(BF)

    scatter_out(order, count, ready, sem, out, tall, step, steps)


def iso_call(back, order, count, shift, weight, *windows):
    many, tall, width = windows[0].shape
    blocks = weight.shape[0] // width
    pitch = up_to(tall, 16)
    steps = many // PACK
    held = pl.BlockSpec(weight.shape, lambda step, *_: (0, 0))
    out_shape = [jax.ShapeDtypeStruct((many, tall, width), BF)]
    out_specs = [ANY]
    copies = pltpu.VMEM((SUBLANES, 2 * tall, width), F32)
    scratch = [copies, pltpu.VMEM((PACK * pitch, blocks * width), BF)]
    if back:
        out_shape.append(jax.ShapeDtypeStruct(weight.shape, F32))
        out_specs.append(held)
        scratch += [pltpu.VMEM((PACK * pitch, width), BF), copies]
    scratch += [pltpu.VMEM((2, PACK, tall, width), BF), pltpu.SemaphoreType.DMA((2, PACK))]
    body = iso_back_body if back else iso_forward_body
    flops = 2 * many * tall * weight.size * (2 if back else 1) // 3
    return pl.pallas_call(
        functools.partial(body, tall, pitch, blocks, steps),
        out_shape=out_shape,
        grid_spec=pltpu.PrefetchScalarGridSpec(
            num_scalar_prefetch=3,
            grid=(steps,),
            in_specs=[s for _ in windows for s in iso_specs(tall, width, steps)] + [held],
            out_specs=out_specs,
            scratch_shapes=scratch,
        ),
        compiler_params=pltpu.CompilerParams(vmem_limit_bytes=56 * MIB),
        cost_estimate=pl.CostEstimate(flops=flops, bytes_accessed=4 * MIB, transcendentals=0),
    )(order, count, shift, *[v for v in windows for _ in range(PACK)], weight)


def feed_body(per_window, tile, live, half, own, other, d_out, merge_own, merge_other, ff_in, ff_in_bias, ff_out, biases, gains,
              layer_out, grad_own, grad_other, normed_out, hidden_out, inner_out, outer_out, merged_out, bias_grad, sums, slope):
    step = pl.program_id(0)
    alive = jnp.where(2 * (step // per_window) + half[0] < live[0], 1.0, 0.0)

    @pl.when(step == 0)
    def _():
        bias_grad[...] = jnp.zeros_like(bias_grad)
        sums[...] = jnp.zeros_like(sums)

    merged = dot(own[...], merge_own[...]) + dot(other[...], merge_other[...]) + biases[0:1, :]
    xhat_one, rho_one = normalise(merged)
    normed = (xhat_one * gains[0:1, :] + biases[1:2, :]).astype(BF)
    normed_out[...] = normed
    units = ff_in.shape[1]
    total = merged + biases[2:3, :]
    for u in range(0, units, tile):
        inner = dot(normed, ff_in[:, u : u + tile]) + ff_in_bias[:, u : u + tile]
        phi_total = 0.5 * (1.0 + lax.erf(inner * 0.7071067811865476))
        hidden = (inner * phi_total).astype(BF)
        slope[:, u : u + tile] = phi_total + inner * (jnp.exp(-0.5 * inner * inner) * 0.3989422804014327)
        hidden_out[:, u : u + tile] = hidden
        total += dot(hidden, ff_out[u : u + tile, :])
    xhat_two, rho_two = normalise(total)
    layer_out[...] = ((xhat_two * gains[1:2, :] + biases[3:4, :]) * alive).astype(BF)
    q = d_out[...].astype(F32) * alive
    grad_sum = norm_back(q * gains[1:2, :], xhat_two, rho_two)
    grad_outer = grad_sum.astype(BF)
    outer_out[...] = grad_outer
    back = jnp.zeros_like(merged)
    for u in range(0, units, tile):
        grad_inner = (dot_bt(grad_outer, ff_out[u : u + tile, :]) * slope[:, u : u + tile]).astype(BF)
        inner_out[:, u : u + tile] = grad_inner
        bias_grad[:, u : u + tile] += column_sum(grad_inner.astype(F32))
        back += dot_bt(grad_inner, ff_in[:, u : u + tile])
    grad_merged = (grad_sum + norm_back(back * gains[0:1, :], xhat_one, rho_one)).astype(BF)
    merged_out[...] = grad_merged
    grad_own[...] = dot_bt(grad_merged, merge_own[...]).astype(BF)
    grad_other[...] = dot_bt(grad_merged, merge_other[...]).astype(BF)
    sums[0:1, :] += column_sum(grad_merged.astype(F32))
    sums[1:2, :] += column_sum(back)
    sums[2:3, :] += column_sum(grad_outer.astype(F32))
    sums[3:4, :] += column_sum(q)
    sums[4:5, :] += column_sum(back * xhat_one)
    sums[5:6, :] += column_sum(q * xhat_two)


def feed_call(live, half, own, other, d_out, merge_own, merge_other, ff_in, ff_in_bias, ff_out, biases, gains, per_window):
    rows, width = own.shape
    units = ff_in.shape[1]
    block = rows // (MICRO * per_window)
    steps = rows // block

    def rowed(columns):
        return pl.BlockSpec((block, columns), lambda step, *_: (step, 0))

    def held(shape):
        return pl.BlockSpec(shape, lambda step, *_: (0, 0))

    def shaped(columns):
        return jax.ShapeDtypeStruct((rows, columns), BF)

    weights = (merge_own, merge_other, ff_in, ff_in_bias, ff_out, biases, gains)
    return pl.pallas_call(
        functools.partial(feed_body, per_window, 512),
        out_shape=[shaped(width), shaped(width), shaped(width), shaped(width), shaped(units), shaped(units), shaped(width),
                   shaped(width), jax.ShapeDtypeStruct((1, units), F32), jax.ShapeDtypeStruct((8, width), F32)],
        grid_spec=pltpu.PrefetchScalarGridSpec(
            num_scalar_prefetch=2,
            grid=(steps,),
            in_specs=[rowed(width)] * 3 + [held(v.shape) for v in weights],
            out_specs=[rowed(width)] * 4 + [rowed(units)] * 2 + [rowed(width)] * 2 + [held((1, units)), held((8, width))],
            scratch_shapes=[pltpu.VMEM((block, units), F32)],
        ),
        compiler_params=pltpu.CompilerParams(vmem_limit_bytes=56 * MIB),
        cost_estimate=pl.CostEstimate(flops=rows * width * units * 2 * 5, bytes_accessed=40 * MIB, transcendentals=rows * units),
    )(live, half, own, other, d_out, *weights)


def branch_index_pair(branch, first, second, *operands):
    return lax.cond(branch == 0, first, second, *operands)


def solution(mesh):
    def per_device(inputs, window_count, branch_blocks, branch_gains, branch_biases, merge_weight, ff_in, ff_in_bias, ff_out,
                   shared_biases, shared_gains, d_out):
        members = mesh.shape["dp"]
        branch, me = lax.axis_index("branch"), lax.axis_index("dp")
        slots, length, width = inputs.shape
        group_rows = branch_blocks.shape[2] * members
        share = branch_blocks.shape[2]
        taps_of = [length // k for k in SCALES]
        tall = up_to(max(taps_of), 8)
        pitches = [up_to(n, 16) for n in taps_of]
        reach = max(SCALES)
        most = slots * max(pitches)
        live = window_count.astype(jnp.int32)
        half = branch.astype(jnp.int32)[None]
        gain, bias = branch_gains, branch_biases[0]

        npd = 8 if share % 64 == 0 else 1
        chunk = share // npd
        down_ranges = tuple((0, -(-k * width // chunk)) for k in SCALES)
        up_starts = [(k + n) * width - group_rows for k, n in zip(SCALES, taps_of)]
        up_ranges = tuple((s // chunk, -(-(s + k * width) // chunk)) for s, k in zip(up_starts, SCALES))
        up_offs = [s - r[0] * chunk for s, r in zip(up_starts, up_ranges)]
        swaps = (-1, 1) if members == 16 else (-1, -1)
        own_blocks = branch_blocks[0]

        down_weight = gather_rows(mesh, own_blocks[0], 0, chunk, npd, down_ranges, 1, swaps)
        up_weight = gather_rows(mesh, own_blocks[1], 0, chunk, npd, up_ranges, 2)

        blocks = (share + width - 1) // width + 1
        k_of = jnp.where(branch == 0, SCALES[0], SCALES[1])
        n_of = jnp.where(branch == 0, taps_of[0], taps_of[1])
        rows_at = jnp.arange(share)
        padded, shifts, insides, lead = [], [], [], []
        for g in range(GROUPS):
            first = g * group_rows + me * share - k_of * width
            inside = jnp.logical_and(first + rows_at >= 0, first + rows_at < n_of * width)
            start = first // width
            shifts.append(jnp.clip(n_of - 1 - start - jnp.arange(blocks), 0, tall))
            lead.append(first - start * width)
            insides.append(inside)
            kept = jnp.where(inside[:, None], own_blocks[g], 0)
            padded.append(lax.dynamic_update_slice(jnp.zeros((blocks * width, width), BF), kept, (lead[g], 0)))
        iso_weight = jnp.concatenate(padded, axis=0)
        shift = jnp.concatenate(shifts).astype(jnp.int32)

        counts = lax.all_gather(live, "dp", axis=0, tiled=True)
        alive = (jnp.arange(slots)[None, :] < counts[:, None]).reshape(-1)
        places = jnp.arange(members * slots)
        rank = jnp.sum(jnp.logical_and(alive[None, :], places[None, :] < places[:, None]).astype(jnp.int32), axis=1)
        order = jnp.sum(
            jnp.where(jnp.logical_and(alive[:, None], rank[:, None] == places[None, :]), places[:, None], 0), axis=0
        ).astype(jnp.int32)
        count = jnp.sum(counts)[None].astype(jnp.int32)

        def windows_shape(kind):
            return jax.ShapeDtypeStruct((slots, tall, width), kind)

        full = jax.ShapeDtypeStruct((slots, length, width), BF)
        taps_shape = jax.ShapeDtypeStruct((most, reach * width), BF)
        part_shape = jax.ShapeDtypeStruct((max(r[1] - r[0] for r in down_ranges) * chunk, width), BF)
        up_part_shape = jax.ShapeDtypeStruct((max(r[1] - r[0] for r in up_ranges) * chunk, width), BF)
        sm = pl.BlockSpec(memory_space=pltpu.SMEM)

        def call(body, index, off, outs, scratch, scalars, *operands):
            k, n, pitch = SCALES[index], taps_of[index], pitches[index]
            return pl.pallas_call(
                functools.partial(body, k, n, pitch, off),
                out_shape=outs,
                in_specs=[sm] * scalars + [VMEM] * (len(operands) - scalars),
                out_specs=jax.tree.map(lambda _: VMEM, outs),
                scratch_shapes=scratch,
                compiler_params=pltpu.CompilerParams(vmem_limit_bytes=60 * MIB),
            )(*operands)

        def rows_scratch(index):
            return pltpu.VMEM((slots * pitches[index], width), BF)

        def spread_scratch(index, count_of=slots):
            return pltpu.VMEM((count_of, width // LANES, pitches[index] * SCALES[index], LANES), F32)

        def down_of(index):
            def run(x, weight, bias):
                return call(down_body, index, 0, (windows_shape(F32), windows_shape(BF), taps_shape),
                            [pltpu.VMEM((width // LANES, pitches[index] * SCALES[index], LANES), F32)], 0, x, weight, bias)
            return run

        pre, act, taps = branch_index_pair(branch, down_of(0), down_of(1), inputs, down_weight, bias)

        passes = 1 if members <= 32 else slots
        per = slots // passes
        pieces = 2 if per % 2 == 0 else 1

        def spread_windows(values, collective_id):
            flat = values.reshape(slots * tall, width)
            return gather_rows(mesh, flat, 0, slots * tall // 2, 2, ((0, 2 * members),) * 2, collective_id).reshape(
                members * slots, tall, width
            )

        def sum_windows(values, collective_id):
            parts = values.reshape(members, passes, per, tall, width)
            results = [
                reduce_rows(mesh, parts[:, p].reshape(-1, width), per * tall // pieces, pieces,
                            ((0, pieces * members),) * 2, collective_id + p, F32)
                for p in range(passes)
            ]
            return jnp.concatenate([r.reshape(per, tall, width) for r in results], axis=0)

        acts = spread_windows(act, 3)
        [terms] = iso_call(False, order, count, shift, iso_weight, acts)
        pre_iso = sum_windows(terms, 16)

        def up_of(index):
            def run(*operands):
                return call(up_body, index, up_offs[index], full, [rows_scratch(index), spread_scratch(index)], 1, *operands)
            return run

        branch_out = branch_index_pair(branch, up_of(0), up_of(1), live, pre_iso, up_weight, inputs, gain, bias)

        def swap(values):
            return lax.ppermute(values, "branch", [(0, 1), (1, 0)])

        def part_at(values, which):
            return lax.dynamic_index_in_dim(values.reshape(MICRO, 2, length, width), which, 1, keepdims=False)

        own = part_at(branch_out, branch).reshape(-1, width)
        other = swap(part_at(branch_out, 1 - branch)).reshape(-1, width)
        merge_own = lax.dynamic_slice_in_dim(merge_weight, branch * width, width, 0)
        merge_other = lax.dynamic_slice_in_dim(merge_weight, (1 - branch) * width, width, 0)
        (layer_out, grad_own, grad_other, normed, hidden, grad_inner, grad_outer, grad_merged, bias_grad, sums) = feed_call(
            live, half, own, other, d_out.reshape(-1, width), merge_own, merge_other, ff_in, ff_in_bias[None], ff_out,
            shared_biases, shared_gains, 3,
        )
        arrived = swap(grad_other.reshape(MICRO, length, width))
        kept = grad_own.reshape(MICRO, length, width)
        grad_branch = jnp.where(
            branch == 0, jnp.stack([kept, arrived], axis=1), jnp.stack([arrived, kept], axis=1)
        ).reshape(slots, length, width)
        ff_in_grad = dot_at(normed, grad_inner)
        ff_out_grad = dot_at(hidden, grad_outer)
        merge_own_grad, merge_other_grad = dot_at(own, grad_merged), dot_at(other, grad_merged)
        merge_grad = jnp.where(
            branch == 0, jnp.concatenate([merge_own_grad, merge_other_grad]), jnp.concatenate([merge_other_grad, merge_own_grad])
        )
        wide = lax.psum((merge_grad.astype(BF), ff_in_grad.astype(BF), ff_out_grad.astype(BF)), ("branch", "dp"))

        def up_back_of(index):
            def run(*operands):
                return call(up_back_body, index, up_offs[index],
                            (windows_shape(BF), jax.ShapeDtypeStruct((8, width), F32), taps_shape, up_part_shape),
                            [rows_scratch(index), spread_scratch(index)], 1, *operands)
            return run

        grad_iso, vectors, grad_taps, up_part = branch_index_pair(
            branch, up_back_of(0), up_back_of(1), live, grad_branch, pre_iso, up_weight, inputs, gain, bias
        )
        grads = spread_windows(grad_iso, 4)
        back_terms, kernel_grad = iso_call(True, order, count, shift, iso_weight, acts, grads)
        grad_act = sum_windows(back_terms, 32)

        def down_back_of(index):
            def run(*operands):
                return call(down_back_body, index, 0, (full, jax.ShapeDtypeStruct((1, width), F32), part_shape),
                            [rows_scratch(index), spread_scratch(index)], 1, *operands)
            return run

        grad_values, down_vector, down_part = branch_index_pair(
            branch, down_back_of(0), down_back_of(1), live, grad_act, pre, grad_taps, taps, down_weight
        )
        arrived_values = swap(part_at(grad_values, 1 - branch))
        grad_inputs = (part_at(grad_values, branch).astype(F32) + arrived_values.astype(F32)).astype(BF)

        vectors = vectors.at[1].set(down_vector[0])
        both = jnp.where((jnp.arange(2) == branch)[:, None, None], vectors[None, :5], 0.0)
        small = lax.psum((both, bias_grad, sums), ("branch", "dp"))
        own_vectors = lax.dynamic_slice_in_dim(small[0], branch, 1, 0)

        up_sum = reduce_rows(mesh, up_part, chunk, npd, up_ranges, 5, F32).reshape(share, width)
        down_sum = reduce_rows(mesh, down_part, chunk, npd, down_ranges, 6, F32, swaps).reshape(share, width)
        group_grads = []
        for g, side in enumerate((down_sum, up_sum)):
            at = g * group_rows + me * share + rows_at
            low, high = (0, k_of * width) if g == 0 else ((k_of + n_of) * width, (2 * k_of + n_of) * width)
            iso_rows = lax.dynamic_slice(kernel_grad, (g * blocks * width + lead[g], 0), (share, width))
            outside = jnp.where(jnp.logical_and(at >= low, at < high)[:, None], side, 0.0)
            group_grads.append(jnp.where(insides[g][:, None], iso_rows, outside))
        grad_blocks = jnp.stack(group_grads)[None]
        return (
            layer_out.reshape(MICRO, 1, 1, length, width), grad_inputs[:, None, None], grad_blocks,
            own_vectors[:, 0], own_vectors[:, 1:], wide[0].astype(F32), wide[1].astype(F32), small[1][0],
            wide[2].astype(F32), small[2][:4], small[2][4:6],
        )

    from jax.sharding import PartitionSpec as P

    placed = (P("dp", None, None), P("dp"), P("branch", None, "dp", None), P("branch", None), P("branch", None, None), P(), P(), P(),
              P(), P(), P(), P("dp", "branch", None, None, None))
    return jax.shard_map(
        per_device, mesh=mesh, in_specs=placed,
        out_specs=(P("dp", "branch", None, None, None), P("dp", "branch", None, None, None), P("branch", None, "dp", None),
                   P("branch", None), P("branch", None, None), P(), P(), P(), P(), P(), P()),
        check_vma=False,
    )
```

```python
import functools
import jax, jax.numpy as jnp
from jax import lax
from jax.experimental import pallas as pl
from jax.experimental.pallas import tpu as pltpu

MESH = pl.DeviceIdType.MESH
ANY = pl.BlockSpec(memory_space=pl.ANY)


def place():
    me = lax.axis_index("dp")
    return lax.axis_index("branch"), me, me // 4, (me // 2) % 2, me % 2


def meet(depth, b, me, z):
    barrier = pltpu.get_barrier_semaphore()
    y, c = (me // 2) % 2, me % 2
    pl.semaphore_signal(barrier, 1, device_id=(b, me + 1 - 2 * c), device_id_type=MESH)
    pl.semaphore_signal(barrier, 1, device_id=(b, me + 2 - 4 * y), device_id_type=MESH)

    @pl.when(z > 0)
    def _():
        pl.semaphore_signal(barrier, 1, device_id=(b, me - 4), device_id_type=MESH)

    @pl.when(z < depth - 1)
    def _():
        pl.semaphore_signal(barrier, 1, device_id=(b, me + 4), device_id_type=MESH)

    count = 2 + jnp.where(z > 0, 1, 0) + jnp.where(z < depth - 1, 1, 0)
    pl.semaphore_wait(barrier, count)


def gather_body(depth, npd, rows, base, ranges, swaps, src, dst, hold, local_sem, recv_sem, send_sem):
    b, me, z, y, c = place()
    meet(depth, b, me, z)
    (a0, a1), (b0, b1) = ranges
    q0 = jnp.where(b == 0, a0, b0)
    q1 = jnp.where(b == 0, a1, b1)
    swap = jnp.where(b == 0, swaps[0], swaps[1])
    core_peer, y_peer = (b, me + 1 - 2 * c), (b, me + 2 - 4 * y)

    def chunk(ref, index):
        return ref.at[pl.ds(pl.multiple_of(index * rows, 8), rows), :]

    def own(i):
        return src.at[pl.ds(pl.multiple_of(base + i * rows, 8), rows), :]

    def remote(kind, q, device, from_own=False):
        k = q - q0
        return pltpu.make_async_remote_copy(
            own(q - me * npd) if from_own else chunk(dst, k), chunk(dst, k), send_sem.at[kind, k], recv_sem.at[k],
            device_id=device, device_id_type=MESH,
        )

    def each_own(what):
        for i in range(npd):
            q = me * npd + i

            @pl.when(jnp.logical_and(q >= q0, q < q1))
            def _():
                what(q, i)

    def take(q, i):
        return pltpu.make_async_copy(own(i), hold.at[i], local_sem.at[0, i])

    def put(q, i):
        return pltpu.make_async_copy(hold.at[i], chunk(dst, q - q0), local_sem.at[1, i])

    each_own(lambda q, i: take(q, i).start())

    def column(j):
        ys = (j // 2) % 2
        return jnp.where(j == swap, 1 - ys, ys)

    def each(core, steps, what):
        def over(zs, t, s):
            for ys in (y, 1 - y):
                j = (zs * 2 + ys) * 2 + core
                col = column(j)
                i = s - t - jnp.where(ys != col, 1, 0) - jnp.where(y != col, 1, 0)
                i = jnp.where(jnp.logical_and(t == 0, ys == y), s, i)
                q = j * npd + i

                @pl.when(jnp.logical_and(jnp.logical_and(i >= 0, i < npd), jnp.logical_and(q >= q0, q < q1)))
                def _():
                    what(q, j)

        def over_steps(s, carry):
            def over_far(t, inner):
                @pl.when(z >= t)
                def _():
                    over(z - t, t, s)

                @pl.when(jnp.logical_and(z + t < depth, t > 0))
                def _():
                    over(z + t, t, s)

                return inner

            return lax.fori_loop(0, depth, over_far, carry)

        lax.fori_loop(0, npd + depth + 1, over_steps, 0)

    def sends(q, j, act, from_own=False):
        zs, ys = j // 4, (j // 2) % 2
        col = column(j)
        chain = y == col

        @pl.when(jnp.logical_and(chain, jnp.logical_and(z >= zs, z < depth - 1)))
        def _():
            act(remote(0, q, (b, me + 4), from_own))

        @pl.when(jnp.logical_and(chain, jnp.logical_and(z <= zs, z > 0)))
        def _():
            act(remote(1, q, (b, me - 4), from_own))

        start_here = jnp.logical_and(z == zs, ys != col)

        @pl.when(chain != start_here)
        def _():
            act(remote(2, q, y_peer, from_own))

        act(remote(3, q, core_peer, from_own))

    def forward(q, j):
        @pl.when(me == j)
        def _():
            sends(q, j, lambda copy: copy.start(), True)

        @pl.when(me != j)
        def _():
            remote(3, q, core_peer).wait_recv()
            sends(q, j, lambda copy: copy.start())

    each(c, npd + depth + 1, forward)

    def swap_own(q, i):
        take(q, i).wait()
        put(q, i).start()

    each_own(swap_own)

    def finish(q, carry):
        j = q // npd

        @pl.when(c == j % 2)
        def _():
            sends(q, j, lambda copy: copy.wait_send())

        @pl.when(c != j % 2)
        def _():
            remote(3, q, core_peer).wait_recv()

        return carry

    lax.fori_loop(q0, q1, finish, 0)
    each_own(lambda q, i: put(q, i).wait())


def gather_rows(mesh, src, base, rows, npd, ranges, collective_id, swaps=(-1, -1)):
    depth = mesh.shape["dp"] // 4
    count = max(r[1] - r[0] for r in ranges)
    return pl.pallas_call(
        functools.partial(gather_body, depth, npd, rows, base, ranges, swaps),
        out_shape=jax.ShapeDtypeStruct((count * rows, src.shape[1]), src.dtype),
        in_specs=[ANY],
        out_specs=ANY,
        scratch_shapes=[
            pltpu.VMEM((npd, rows, src.shape[1]), src.dtype),
            pltpu.SemaphoreType.DMA((2, npd)),
            pltpu.SemaphoreType.DMA((count,)),
            pltpu.SemaphoreType.DMA((4, count)),
        ],
        compiler_params=pltpu.CompilerParams(collective_id=collective_id, has_side_effects=True),
    )(src)


def reduce_body(depth, npd, rows, ranges, swaps, lag, src, out, own, rc, ry, rz, fin, acc, own_sem, rc_sem, ry_sem, rz_sem, fin_sem, send_sem, fin_send):
    b, me, z, y, c = place()
    meet(depth, b, me, z)
    (a0, a1), (b0, b1) = ranges
    q0 = jnp.where(b == 0, a0, b0)
    q1 = jnp.where(b == 0, a1, b1)
    swap = jnp.where(b == 0, swaps[0], swaps[1])
    pair0 = q0 // npd // 2
    core_peer, y_peer = (b, me + 1 - 2 * c), (b, me + 2 - 4 * y)
    up, down = (b, jnp.minimum(me + 4, 4 * depth - 1)), (b, jnp.maximum(me - 4, 0))

    def column(j):
        ys = (j // 2) % 2
        return jnp.where(j == swap, 1 - ys, ys)

    def slot(j, i):
        return (j // 2 - pair0) * npd + i

    def part(j, i):
        return src.at[pl.ds(pl.multiple_of((j * npd + i - q0) * rows, 8), rows), :]

    def keep(j, i):
        return pltpu.make_async_copy(part(j, i), own.at[slot(j, i)], own_sem.at[slot(j, i)])

    def remote(kind, frm, to, sem, k, device):
        return pltpu.make_async_remote_copy(
            frm, to, send_sem.at[kind, k], sem, device_id=device, device_id_type=MESH
        )

    def to_core(j, i):
        k = slot(j, i)
        return remote(0, part(j, i), rc.at[k], rc_sem.at[k], k, core_peer)

    def to_y(j, i):
        k = slot(j, i)
        return remote(1, own.at[k], ry.at[k], ry_sem.at[k], k, y_peer)

    def to_z(j, i, way):
        k = slot(j, i)
        return remote(2, own.at[k], rz.at[way, k], rz_sem.at[way, k], k, (up, down)[way])

    def to_owner(j, i):
        return pltpu.make_async_remote_copy(
            own.at[slot(j, i)], fin.at[i], fin_send.at[i], fin_sem.at[i], device_id=y_peer, device_id_type=MESH
        )

    def owners(n, core, what):
        pos, i = n // npd, n % npd
        rising = pos + jnp.where(pos >= z, 1, 0)
        falling = depth - 1 - pos
        falling = falling - jnp.where(falling <= z, 1, 0)
        zs = jnp.where(pos == depth - 1, z, jnp.where(z >= depth // 2, rising, falling))
        for ys in (0, 1):
            j = (zs * 2 + ys) * 2 + core
            q = j * npd + i

            @pl.when(jnp.logical_and(q >= q0, q < q1))
            def _():
                what(j, i, zs, ys)

    total = depth * npd

    def begin(n, carry):
        owners(n, 1 - c, lambda j, i, zs, ys: to_core(j, i).start())
        owners(n, c, lambda j, i, zs, ys: keep(j, i).start())
        return carry

    lax.fori_loop(0, total, begin, 0)

    def cross(j, i, zs, ys):
        @pl.when(column(j) != y)
        def _():
            k = slot(j, i)
            keep(j, i).wait()
            to_core(j, i).wait_recv()
            own[k] = (own[k].astype(jnp.float32) + rc[k].astype(jnp.float32)).astype(own.dtype)
            to_y(j, i).start()

    def chain(j, i, zs, ys):
        @pl.when(column(j) == y)
        def _():
            k = slot(j, i)
            keep(j, i).wait()
            to_core(j, i).wait_recv()
            to_y(j, i).wait_recv()
            acc[...] = own[k].astype(jnp.float32) + rc[k].astype(jnp.float32) + ry[k].astype(jnp.float32)

            @pl.when(jnp.logical_and(z >= zs, z < depth - 1))
            def _():
                to_z(j, i, 1).wait_recv()
                acc[...] += rz[1, k].astype(jnp.float32)

            @pl.when(jnp.logical_and(z <= zs, z > 0))
            def _():
                to_z(j, i, 0).wait_recv()
                acc[...] += rz[0, k].astype(jnp.float32)

            @pl.when(jnp.logical_and(z == zs, ys == y))
            def _():
                out[i] = acc[...].astype(out.dtype)

            @pl.when(jnp.logical_not(jnp.logical_and(z == zs, ys == y)))
            def _():
                own[k] = acc[...].astype(own.dtype)

            @pl.when(z > zs)
            def _():
                to_z(j, i, 1).start()

            @pl.when(z < zs)
            def _():
                to_z(j, i, 0).start()

            @pl.when(jnp.logical_and(z == zs, ys != y))
            def _():
                to_owner(j, i).start()

    def step(s, carry):
        @pl.when(s < total)
        def _():
            owners(s, c, cross)

        @pl.when(s >= lag)
        def _():
            owners(s - lag, c, chain)

        return carry

    lax.fori_loop(0, total + lag, step, 0)

    def sent(j, i, zs, ys):
        @pl.when(column(j) != y)
        def _():
            to_y(j, i).wait_send()

            @pl.when(me == j)
            def _():
                to_owner(j, i).wait_recv()
                out[i] = fin[i].astype(out.dtype)

        @pl.when(column(j) == y)
        def _():
            @pl.when(z != zs)
            def _():
                to_z(j, i, 0).wait_send()

            @pl.when(jnp.logical_and(z == zs, ys != y))
            def _():
                to_owner(j, i).wait_send()

    def end(n, carry):
        owners(n, 1 - c, lambda j, i, zs, ys: to_core(j, i).wait_send())
        owners(n, c, sent)
        return carry

    lax.fori_loop(0, total, end, 0)


def reduce_rows(mesh, src, rows, npd, ranges, collective_id, dtype, swaps=(-1, -1), lag=2):
    depth = mesh.shape["dp"] // 4
    pairs = max((r[1] + npd - 1) // npd // 2 + (r[1] + npd - 1) // npd % 2 - r[0] // npd // 2 for r in ranges)
    held, width = pairs * npd, src.shape[1]
    block = (held, rows, width)
    return pl.pallas_call(
        functools.partial(reduce_body, depth, npd, rows, ranges, swaps, lag),
        out_shape=jax.ShapeDtypeStruct((npd, rows, width), dtype),
        in_specs=[ANY],
        out_specs=pl.BlockSpec(memory_space=pltpu.VMEM),
        scratch_shapes=[
            pltpu.VMEM(block, src.dtype),
            pltpu.VMEM(block, src.dtype),
            pltpu.VMEM(block, src.dtype),
            pltpu.VMEM((2, *block), src.dtype),
            pltpu.VMEM((npd, rows, width), src.dtype),
            pltpu.VMEM((rows, width), jnp.float32),
            pltpu.SemaphoreType.DMA((held,)),
            pltpu.SemaphoreType.DMA((held,)),
            pltpu.SemaphoreType.DMA((held,)),
            pltpu.SemaphoreType.DMA((2, held)),
            pltpu.SemaphoreType.DMA((npd,)),
            pltpu.SemaphoreType.DMA((3, held)),
            pltpu.SemaphoreType.DMA((npd,)),
        ],
        compiler_params=pltpu.CompilerParams(
            collective_id=collective_id, has_side_effects=True, vmem_limit_bytes=50 * 2**20
        ),
    )(src)
SCALES = (12, 16)
MICRO = 3
GROUPS = 2
EPSILON = 1e-05
BF, F32 = jnp.bfloat16, jnp.float32
MIB = 2**20


def up_to(value, step):
    return (value + step - 1) // step * step


def dot(a, b):
    return jnp.dot(a, b, preferred_element_type=F32)


def dot_bt(a, b):
    return lax.dot_general(a, b, (((1,), (1,)), ((), ())), preferred_element_type=F32)


def dot_at(a, b):
    return lax.dot_general(a, b, (((0,), (0,)), ((), ())), preferred_element_type=F32)


def mean(values):
    return jnp.mean(values, axis=-1, keepdims=True)


def normalise(values):
    centre = values - mean(values)
    rho = lax.rsqrt(mean(centre * centre) + EPSILON)
    return centre * rho, rho


def norm_back(q_gain, xhat, rho):
    return rho * (q_gain - mean(q_gain) - xhat * mean(q_gain * xhat))


def column_sum(values):
    return jnp.sum(values, axis=0, keepdims=True)


VMEM = pl.BlockSpec(memory_space=pltpu.VMEM)


def whole_call(body, out_shape, scratch, limit, cost=None):
    return pl.pallas_call(
        body,
        out_shape=out_shape,
        out_specs=jax.tree.map(lambda _: VMEM, out_shape),
        scratch_shapes=scratch,
        compiler_params=pltpu.CompilerParams(vmem_limit_bytes=limit * MIB),
        cost_estimate=cost,
    )


LANES = 128


def panels(ref, lead, rows):
    return jnp.concatenate([ref[(*lead, p, rows, slice(None))] for p in range(ref.shape[-3])], axis=1)


def set_panels(ref, lead, rows, values):
    for p in range(ref.shape[-3]):
        ref[(*lead, p, rows, slice(None))] = values[:, p * LANES : (p + 1) * LANES]


def down_body(k, n, pitch, off, live, x, weight, bias, pre, act, taps, spread):
    slots, length, width = x.shape
    many = slots * pitch
    spread[:, length:, :] = jnp.zeros((spread.shape[0], spread.shape[1] - length, LANES), F32)

    def window(w, carry):
        set_panels(spread, (), slice(0, length), x[w].astype(F32))
        for r in range(k):
            taps[pl.ds(pl.multiple_of(w * pitch, 16), pitch), r * width : (r + 1) * width] = panels(
                spread, (), pl.ds(r, pitch, stride=k)
            ).astype(BF)
        return carry

    lax.fori_loop(0, slots, window, 0)
    total = dot(taps[:many, : k * width], weight[off : off + k * width, :]) + bias[0:1, :]
    tall = pre.shape[1]
    for w in range(slots):
        rows = fit(total[w * pitch : (w + 1) * pitch], tall)
        pre[w] = rows
        step = lax.broadcasted_iota(jnp.int32, rows.shape, 0)
        flag = jnp.where(step == tall - 1, jnp.where(w < live[0], 1.0, 0.0), 0.0)
        act[w] = jnp.where(step < n, jnp.tanh(rows), flag).astype(BF)


def fit(values, tall):
    rows = values.shape[0]
    if rows >= tall:
        return values[:tall]
    return jnp.concatenate([values, jnp.zeros((tall - rows, values.shape[1]), values.dtype)], axis=0)


def expand(k, n, pitch, off, iso_rows, weight, spread):
    width = iso_rows.shape[1]
    slots = spread.shape[0]

    def tap(r, carry):
        rows = dot(iso_rows[...], weight[pl.ds(pl.multiple_of(off + r * width, 16), width), :])
        for w in range(slots):
            set_panels(spread, (w,), pl.ds(r, pitch, stride=k), rows[w * pitch : (w + 1) * pitch])
        return carry

    lax.fori_loop(0, k, tap, 0)


def iso_of(n, pitch, pre_iso, bias):
    rows = fit(jnp.tanh(pre_iso + bias[1:2, :]), pitch)
    step = lax.broadcasted_iota(jnp.int32, rows.shape, 0)
    return jnp.where(step < n, rows, 0.0)


def up_body(k, n, pitch, off, live, half, pre_iso, weight, x, gain, bias, own, send, iso_rows, spread):
    slots, length, width = x.shape
    for w in range(slots):
        iso = iso_of(n, pitch, pre_iso[w], bias)
        iso_rows[w * pitch : (w + 1) * pitch, :] = jnp.where(w < live[0], iso, 0.0).astype(BF)
    expand(k, n, pitch, off, iso_rows, weight, spread)

    def window(m, carry):
        for out, w in ((send, 2 * m + 1 - half[0]), (own, 2 * m + half[0])):
            values = panels(spread, (w,), slice(0, length)) + bias[2:3, :] + x[w].astype(F32)
            xhat, _ = normalise(values)
            out[m] = (xhat * gain[0:1, :] + bias[3:4, :]).astype(BF)
        return carry

    lax.fori_loop(0, slots // 2, window, 0)


def up_back_body(k, n, pitch, off, live, half, grad_own, grad_arrived, pre_iso, weight, x, gain, bias, grad_iso, vectors, grad_taps, part, iso_rows, spread):
    slots, length, width = x.shape
    for w in range(slots):
        iso = iso_of(n, pitch, pre_iso[w], bias)
        iso_rows[w * pitch : (w + 1) * pitch, :] = jnp.where(w < live[0], iso, 0.0).astype(BF)
    expand(k, n, pitch, off, iso_rows, weight, spread)
    vectors[...] = jnp.zeros_like(vectors)

    def window(m, carry):
        for grad, w in ((grad_own, 2 * m + half[0]), (grad_arrived, 2 * m + 1 - half[0])):
            values = panels(spread, (w,), slice(0, length)) + bias[2:3, :] + x[w].astype(F32)
            xhat, rho = normalise(values)
            q = grad[m].astype(F32)
            residual = norm_back(q * gain[0:1, :], xhat, rho)
            set_panels(spread, (w,), slice(0, length), residual)
            vectors[0:1, :] += column_sum(q * xhat)
            vectors[3:4, :] += column_sum(residual.astype(BF).astype(F32))
            vectors[4:5, :] += column_sum(q)
        return carry

    lax.fori_loop(0, slots // 2, window, 0)

    def tap(w, carry):
        for r in range(k):
            grad_taps[pl.ds(pl.multiple_of(w * pitch, 16), pitch), r * width : (r + 1) * width] = panels(
                spread, (w,), pl.ds(r, pitch, stride=k)
            ).astype(BF)
        return carry

    lax.fori_loop(0, slots, tap, 0)
    total = jnp.zeros((slots * pitch, width), F32)
    for r in range(k):
        rows = grad_taps[: slots * pitch, r * width : (r + 1) * width]
        total += dot_bt(rows, weight[off + r * width : off + (r + 1) * width, :])
        part[off + r * width : off + (r + 1) * width, :] = dot_at(iso_rows[...], rows).astype(BF)
    tall = grad_iso.shape[1]
    for w in range(slots):
        iso = iso_of(n, pitch, pre_iso[w], bias)
        slope = jnp.where(lax.broadcasted_iota(jnp.int32, iso.shape, 0) < n, 1.0 - iso * iso, 0.0)
        back = total[w * pitch : (w + 1) * pitch] * slope
        back = jnp.where(w < live[0], back, 0.0).astype(BF)
        vectors[2:3, :] += column_sum(back.astype(F32))
        grad_iso[w] = fit(back.astype(F32), tall).astype(BF)


def down_back_body(k, n, pitch, off, live, half, grad_act, pre, grad_taps, taps, weight, keep, send, vector, part, rows, spread):
    slots, (length, width) = pre.shape[0], keep.shape[1:]
    vector[...] = jnp.zeros_like(vector)
    for w in range(slots):
        act = jnp.tanh(fit(pre[w], pitch))
        step = lax.broadcasted_iota(jnp.int32, act.shape, 0)
        back = fit(grad_act[w], pitch) * (1.0 - act * act)
        back = jnp.where(jnp.logical_and(step < n, w < live[0]), back, 0.0).astype(BF)
        vector[...] += column_sum(back.astype(F32))
        rows[w * pitch : (w + 1) * pitch, :] = back
    for r in range(k):
        back = dot_bt(rows[...], weight[off + r * width : off + (r + 1) * width, :])
        back += grad_taps[: slots * pitch, r * width : (r + 1) * width].astype(F32)
        for w in range(slots):
            set_panels(spread, (w,), pl.ds(r, pitch, stride=k), back[w * pitch : (w + 1) * pitch])
        part[off + r * width : off + (r + 1) * width, :] = dot_at(
            taps[: slots * pitch, r * width : (r + 1) * width], rows[...]
        ).astype(BF)

    def window(m, carry):
        send[m] = panels(spread, (2 * m + 1 - half[0],), slice(0, length)).astype(BF)
        keep[m] = panels(spread, (2 * m + half[0],), slice(0, length)).astype(BF)
        return carry

    lax.fori_loop(0, slots // 2, window, 0)


SUBLANES = 8


def shifted(copies, start, tall):
    rows = pl.multiple_of(start // SUBLANES * SUBLANES, SUBLANES)
    return copies[start % SUBLANES, pl.ds(rows, tall), :].astype(BF)


def late_copies(copies, values):
    tall = values.shape[0]
    for b in range(SUBLANES):
        copies[b, tall - b : 2 * tall - b, :] = values


def early_copies(copies, values):
    tall = values.shape[0]
    for b in range(SUBLANES):
        copies[b, : tall - b, :] = values[b:]


PACK = 8


def iso_specs(tall, width, pieces):
    def spec(e):
        def at(step, order, count, shift):
            last = jnp.maximum(count[0] - 1, 0) // PACK
            return order[jnp.minimum(step, last) * PACK + e], 0, 0

        return pl.BlockSpec((1, tall, width), at)

    return [spec(e) for e in range(PACK)]


def scatter_out(order, count, slots_ref, sem, out, tall, step, steps):
    def copy(at, e):
        where = jnp.minimum(at * PACK + e, order.shape[0] - 1)
        return pltpu.make_async_copy(
            slots_ref.at[at % 2, e], out.at[order[where]], sem.at[at % 2, e]
        )

    live = pl.cdiv(count[0], PACK)

    @pl.when(step < live)
    def _():
        for e in range(PACK):
            @pl.when(step * PACK + e < count[0])
            def _():
                copy(step, e).start()

    @pl.when(jnp.logical_and(step >= 1, step <= live))
    def _():
        for e in range(PACK):
            @pl.when((step - 1) * PACK + e < count[0])
            def _():
                copy(step - 1, e).wait()

    @pl.when(jnp.logical_and(step == steps - 1, live == steps))
    def _():
        for e in range(PACK):
            @pl.when(step * PACK + e < count[0])
            def _():
                copy(step, e).wait()


def iso_forward_body(tall, pitch, blocks, steps, order, count, shift, *refs):
    acts, (weight, out, buffer, columns, ready, sem) = refs[:PACK], refs[PACK:]
    step = pl.program_id(0)
    width = weight.shape[1]

    @pl.when(step == 0)
    def _():
        buffer[...] = jnp.zeros_like(buffer)
        columns[...] = jnp.zeros_like(columns)

    @pl.when(step * PACK < count[0])
    def _():
        for e in range(PACK):
            late_copies(buffer, jnp.where(step * PACK + e < count[0], acts[e][0].astype(F32), 0.0))
            for m in range(blocks):
                columns[e * pitch : e * pitch + tall, m * width : (m + 1) * width] = shifted(buffer, tall - shift[m], tall)
        total = dot(columns[...], weight[...])
        for e in range(PACK):
            ready[step % 2, e] = total[e * pitch : e * pitch + tall].astype(BF)

    scatter_out(order, count, ready, sem, out, tall, step, steps)


def iso_back_body(tall, pitch, blocks, steps, order, count, shift, *refs):
    acts, grads = refs[:PACK], refs[PACK : 2 * PACK]
    weight, out, kernel_grad, buffer, columns, gathered, ahead, ready, sem = refs[2 * PACK :]
    step = pl.program_id(0)
    width = weight.shape[1]

    @pl.when(step == 0)
    def _():
        buffer[...] = jnp.zeros_like(buffer)
        columns[...] = jnp.zeros_like(columns)
        gathered[...] = jnp.zeros_like(gathered)
        ahead[...] = jnp.zeros_like(ahead)
        kernel_grad[...] = jnp.zeros_like(kernel_grad)

    @pl.when(step * PACK < count[0])
    def _():
        for e in range(PACK):
            alive = step * PACK + e < count[0]
            late_copies(buffer, jnp.where(alive, acts[e][0].astype(F32), 0.0))
            for m in range(blocks):
                columns[e * pitch : e * pitch + tall, m * width : (m + 1) * width] = shifted(buffer, tall - shift[m], tall)
            gathered[e * pitch : e * pitch + tall, :] = jnp.where(alive, grads[e][0].astype(F32), 0.0).astype(BF)
        for m in range(blocks):
            kernel_grad[m * width : (m + 1) * width, :] += dot_at(columns[:, m * width : (m + 1) * width], gathered[...])
        for e in range(PACK):
            alive = step * PACK + e < count[0]
            early_copies(ahead, jnp.where(alive, grads[e][0].astype(F32), 0.0))
            for m in range(blocks):
                columns[e * pitch : e * pitch + tall, m * width : (m + 1) * width] = shifted(ahead, shift[m], tall)
        total = dot_bt(columns[:, :width], weight[:width, :])
        for m in range(1, blocks):
            total += dot_bt(columns[:, m * width : (m + 1) * width], weight[m * width : (m + 1) * width, :])
        for e in range(PACK):
            ready[step % 2, e] = total[e * pitch : e * pitch + tall].astype(BF)

    scatter_out(order, count, ready, sem, out, tall, step, steps)


def iso_call(back, order, count, shift, weight, *windows):
    many, tall, width = windows[0].shape
    blocks = weight.shape[0] // width
    pitch = up_to(tall, 16)
    steps = many // PACK
    held = pl.BlockSpec(weight.shape, lambda step, *_: (0, 0))
    out_shape = [jax.ShapeDtypeStruct((many, tall, width), BF)]
    out_specs = [ANY]
    copies = pltpu.VMEM((SUBLANES, 2 * tall, width), F32)
    scratch = [copies, pltpu.VMEM((PACK * pitch, blocks * width), BF)]
    if back:
        out_shape.append(jax.ShapeDtypeStruct(weight.shape, F32))
        out_specs.append(held)
        scratch += [pltpu.VMEM((PACK * pitch, width), BF), copies]
    scratch += [pltpu.VMEM((2, PACK, tall, width), BF), pltpu.SemaphoreType.DMA((2, PACK))]
    body = iso_back_body if back else iso_forward_body
    flops = 2 * many * tall * weight.size * (2 if back else 1) // 3
    return pl.pallas_call(
        functools.partial(body, tall, pitch, blocks, steps),
        out_shape=out_shape,
        grid_spec=pltpu.PrefetchScalarGridSpec(
            num_scalar_prefetch=3,
            grid=(steps,),
            in_specs=[s for _ in windows for s in iso_specs(tall, width, steps)] + [held],
            out_specs=out_specs,
            scratch_shapes=scratch,
        ),
        compiler_params=pltpu.CompilerParams(vmem_limit_bytes=56 * MIB),
        cost_estimate=pl.CostEstimate(flops=flops, bytes_accessed=4 * MIB, transcendentals=0),
    )(order, count, shift, *[v for v in windows for _ in range(PACK)], weight)


def feed_body(per_window, tile, live, own, bo_send, d_out, merge_weight, ff_in, ff_in_bias, ff_out, biases, gains,
              layer_out, grad_own, arrived, merge_grad, in_grad, out_grad, bias_grad, sums,
              slope, hidden_kept, other_slots, grad_slots, merge_sum, in_sum, out_sum, bo_sent, bo_come, back_sent, back_come):
    step, steps = pl.program_id(0), pl.num_programs(0)
    branch, me = lax.axis_index("branch"), lax.axis_index("dp")
    partner = (1 - branch, me)
    block, width = own.shape

    def forth(at):
        return pltpu.make_async_remote_copy(
            bo_send.at[pl.ds(pl.multiple_of(at * block, 8), block), :], other_slots.at[at], bo_sent.at[at], bo_come.at[at],
            device_id=partner, device_id_type=MESH,
        )

    def back_copy(at):
        return pltpu.make_async_remote_copy(
            grad_slots.at[at], arrived.at[pl.ds(pl.multiple_of(at * block, 8), block), :], back_sent.at[at], back_come.at[at],
            device_id=partner, device_id_type=MESH,
        )

    @pl.when(step == 0)
    def _():
        barrier = pltpu.get_barrier_semaphore()
        pl.semaphore_signal(barrier, 1, device_id=partner, device_id_type=MESH)
        pl.semaphore_wait(barrier, 1)
        forth(0).start()
        forth(1).start()
        bias_grad[...] = jnp.zeros_like(bias_grad)
        sums[...] = jnp.zeros_like(sums)
        merge_sum[...] = jnp.zeros_like(merge_sum)
        in_sum[...] = jnp.zeros_like(in_sum)
        out_sum[...] = jnp.zeros_like(out_sum)

    forth(step).wait_recv()

    @pl.when(step + 2 < steps)
    def _():
        forth(step + 2).start()

    alive = jnp.where(2 * (step // per_window) + branch < live[0], 1.0, 0.0)
    own_rows, other_rows = own[...], other_slots[step]
    own_at = pl.ds(pl.multiple_of(branch * width, width), width)
    other_at = pl.ds(pl.multiple_of((1 - branch) * width, width), width)
    merged = dot(own_rows, merge_weight[own_at, :]) + dot(other_rows, merge_weight[other_at, :]) + biases[0:1, :]
    xhat_one, rho_one = normalise(merged)
    normed = (xhat_one * gains[0:1, :] + biases[1:2, :]).astype(BF)
    units = ff_in.shape[1]
    total = merged + biases[2:3, :]
    for u in range(0, units, tile):
        inner = dot(normed, ff_in[:, u : u + tile]) + ff_in_bias[:, u : u + tile]
        phi_total = 0.5 * (1.0 + lax.erf(inner * 0.7071067811865476))
        hidden = (inner * phi_total).astype(BF)
        slope[:, u : u + tile] = phi_total + inner * (jnp.exp(-0.5 * inner * inner) * 0.3989422804014327)
        hidden_kept[:, u : u + tile] = hidden
        total += dot(hidden, ff_out[u : u + tile, :])
    xhat_two, rho_two = normalise(total)
    layer_out[...] = ((xhat_two * gains[1:2, :] + biases[3:4, :]) * alive).astype(BF)
    q = d_out[...].astype(F32) * alive
    grad_sum = norm_back(q * gains[1:2, :], xhat_two, rho_two)
    grad_outer = grad_sum.astype(BF)
    back = jnp.zeros_like(merged)
    for u in range(0, units, tile):
        grad_inner = (dot_bt(grad_outer, ff_out[u : u + tile, :]) * slope[:, u : u + tile]).astype(BF)
        bias_grad[:, u : u + tile] += column_sum(grad_inner.astype(F32))
        back += dot_bt(grad_inner, ff_in[:, u : u + tile])
        in_sum[:, u : u + tile] += dot_at(normed, grad_inner)
        out_sum[u : u + tile, :] += dot_at(hidden_kept[:, u : u + tile], grad_outer)
    grad_merged = (grad_sum + norm_back(back * gains[0:1, :], xhat_one, rho_one)).astype(BF)
    grad_slots[step] = dot_bt(grad_merged, merge_weight[other_at, :]).astype(BF)
    back_copy(step).start()
    grad_own[...] = dot_bt(grad_merged, merge_weight[own_at, :]).astype(BF)
    merge_sum[own_at, :] += dot_at(own_rows, grad_merged)
    merge_sum[other_at, :] += dot_at(other_rows, grad_merged)
    sums[0:1, :] += column_sum(grad_merged.astype(F32))
    sums[1:2, :] += column_sum(back)
    sums[2:3, :] += column_sum(grad_outer.astype(F32))
    sums[3:4, :] += column_sum(q)
    sums[4:5, :] += column_sum(back * xhat_one)
    sums[5:6, :] += column_sum(q * xhat_two)

    @pl.when(step == steps - 1)
    def _():
        merge_grad[...] = merge_sum[...].astype(BF)
        in_grad[...] = in_sum[...].astype(BF)
        out_grad[...] = out_sum[...].astype(BF)

        def finish(at, carry):
            forth(at).wait_send()
            back_copy(at).wait_send()
            back_copy(at).wait_recv()
            return carry

        lax.fori_loop(0, steps, finish, 0)


def feed_call(live, own, bo_send, d_out, merge_weight, ff_in, ff_in_bias, ff_out, biases, gains, per_window, collective_id):
    rows, width = own.shape
    units = ff_in.shape[1]
    steps = MICRO * per_window
    block = rows // steps

    def rowed(columns):
        return pl.BlockSpec((block, columns), lambda step, *_: (step, 0))

    def held(shape):
        return pl.BlockSpec(shape, lambda step, *_: (0, 0), pipeline_mode=pl.Buffered(1))

    def shaped(*shape):
        return jax.ShapeDtypeStruct(shape, BF)

    weights = (merge_weight, ff_in, ff_in_bias, ff_out, biases, gains)
    outs = [(rows, width), (rows, width), (rows, width), merge_weight.shape, ff_in.shape, ff_out.shape]
    return pl.pallas_call(
        functools.partial(feed_body, per_window, 512),
        out_shape=[shaped(*s) for s in outs] + [jax.ShapeDtypeStruct((1, units), F32), jax.ShapeDtypeStruct((8, width), F32)],
        grid_spec=pltpu.PrefetchScalarGridSpec(
            num_scalar_prefetch=1,
            grid=(steps,),
            in_specs=[rowed(width), ANY, rowed(width)] + [held(v.shape) for v in weights],
            out_specs=[rowed(width), rowed(width), ANY] + [held(s) for s in outs[3:]] + [held((1, units)), held((8, width))],
            scratch_shapes=[
                pltpu.VMEM((block, units), F32), pltpu.VMEM((block, units), BF), pltpu.VMEM((steps, block, width), BF),
                pltpu.VMEM((steps, block, width), BF), pltpu.VMEM(merge_weight.shape, F32), pltpu.VMEM(ff_in.shape, F32),
                pltpu.VMEM(ff_out.shape, F32), pltpu.SemaphoreType.DMA((steps,)), pltpu.SemaphoreType.DMA((steps,)),
                pltpu.SemaphoreType.DMA((steps,)), pltpu.SemaphoreType.DMA((steps,)),
            ],
        ),
        compiler_params=pltpu.CompilerParams(vmem_limit_bytes=58 * MIB, collective_id=collective_id, has_side_effects=True),
        cost_estimate=pl.CostEstimate(flops=rows * width * units * 2 * 8, bytes_accessed=40 * MIB, transcendentals=rows * units),
    )(live, own, bo_send, d_out, *weights)


def total_body(depth, values, out, pair, come, far, sent_sem, come_sem, far_sent, far_come):
    b, me, z, y, c = place()
    peers = ((b, me + 1 - 2 * c), (1 - b, me), (b, me + 2 - 4 * y))
    barrier = pltpu.get_barrier_semaphore()
    for peer in peers:
        pl.semaphore_signal(barrier, 1, device_id=peer, device_id_type=MESH)

    def along(what):
        def each(other, carry):
            @pl.when(other != z)
            def _():
                what(other)

            return carry

        lax.fori_loop(0, depth, each, 0)

    def at_row(other):
        return b, me + 4 * (other - z)

    along(lambda other: pl.semaphore_signal(barrier, 1, device_id=at_row(other), device_id_type=MESH))
    pl.semaphore_wait(barrier, len(peers) + depth - 1)
    pair[0] = values[...]
    for step, peer in enumerate(peers):
        copy = pltpu.make_async_remote_copy(
            pair.at[step], come.at[step], sent_sem.at[step], come_sem.at[step], device_id=peer, device_id_type=MESH
        )
        copy.start()
        copy.wait()
        pair[step + 1] = pair[step] + come[step]

    def outward(other):
        return pltpu.make_async_remote_copy(
            pair.at[len(peers)], far.at[z], far_sent.at[other], far_come.at[z], device_id=at_row(other), device_id_type=MESH
        )

    def inward(other):
        return pltpu.make_async_remote_copy(
            pair.at[len(peers)], far.at[other], far_sent.at[other], far_come.at[other], device_id=at_row(other), device_id_type=MESH
        )

    along(lambda other: outward(other).start())
    far[z] = pair[len(peers)]
    along(lambda other: outward(other).wait_send())
    along(lambda other: inward(other).wait_recv())
    out[...] = far[0]

    def add(other, carry):
        out[...] += far[other]
        return carry

    lax.fori_loop(1, depth, add, 0)


def total_over(mesh, values, collective_id):
    depth = mesh.shape["dp"] // 4
    return pl.pallas_call(
        functools.partial(total_body, depth),
        out_shape=jax.ShapeDtypeStruct(values.shape, F32),
        in_specs=[VMEM],
        out_specs=VMEM,
        scratch_shapes=[
            pltpu.VMEM((4, *values.shape), F32), pltpu.VMEM((3, *values.shape), F32), pltpu.VMEM((depth, *values.shape), F32),
            pltpu.SemaphoreType.DMA((3,)), pltpu.SemaphoreType.DMA((3,)), pltpu.SemaphoreType.DMA((depth,)),
            pltpu.SemaphoreType.DMA((depth,)),
        ],
        compiler_params=pltpu.CompilerParams(collective_id=collective_id, has_side_effects=True),
    )(values)


def branch_index_pair(branch, first, second, *operands):
    return lax.cond(branch == 0, first, second, *operands)


def solution(mesh):
    def per_device(inputs, window_count, branch_blocks, branch_gains, branch_biases, merge_weight, ff_in, ff_in_bias, ff_out,
                   shared_biases, shared_gains, d_out):
        members = mesh.shape["dp"]
        branch, me = lax.axis_index("branch"), lax.axis_index("dp")
        slots, length, width = inputs.shape
        group_rows = branch_blocks.shape[2] * members
        share = branch_blocks.shape[2]
        taps_of = [length // k for k in SCALES]
        tall = up_to(max(taps_of) + 1, 8)
        pitches = [up_to(n, 16) for n in taps_of]
        reach = max(SCALES)
        most = slots * max(pitches)
        live = window_count.astype(jnp.int32)
        half = branch.astype(jnp.int32)[None]
        gain, bias = branch_gains, branch_biases[0]

        npd = 8 if share % 64 == 0 else 1
        chunk = share // npd
        down_ranges = tuple((0, -(-k * width // chunk)) for k in SCALES)
        up_starts = [(k + n) * width - group_rows for k, n in zip(SCALES, taps_of)]
        up_ranges = tuple((s // chunk, -(-(s + k * width) // chunk)) for s, k in zip(up_starts, SCALES))
        up_offs = [s - r[0] * chunk for s, r in zip(up_starts, up_ranges)]
        swaps = (-1, 1) if members == 16 else (-1, -1)
        own_blocks = branch_blocks[0]

        down_weight = gather_rows(mesh, own_blocks[0], 0, chunk, npd, down_ranges, 1, swaps)
        up_weight = gather_rows(mesh, own_blocks[1], 0, chunk, npd, up_ranges, 2)

        blocks = (share + width - 1) // width + 1
        k_of = jnp.where(branch == 0, SCALES[0], SCALES[1])
        n_of = jnp.where(branch == 0, taps_of[0], taps_of[1])
        rows_at = jnp.arange(share)
        padded, shifts, insides, lead = [], [], [], []
        for g in range(GROUPS):
            first = g * group_rows + me * share - k_of * width
            inside = jnp.logical_and(first + rows_at >= 0, first + rows_at < n_of * width)
            start = first // width
            shifts.append(jnp.clip(n_of - 1 - start - jnp.arange(blocks), 0, tall))
            lead.append(first - start * width)
            insides.append(inside)
            kept = jnp.where(inside[:, None], own_blocks[g], 0)
            padded.append(lax.dynamic_update_slice(jnp.zeros((blocks * width, width), BF), kept, (lead[g], 0)))
        iso_weight = jnp.concatenate(padded, axis=0)
        shift = jnp.concatenate(shifts).astype(jnp.int32)

        def windows_shape(kind):
            return jax.ShapeDtypeStruct((slots, tall, width), kind)

        full = jax.ShapeDtypeStruct((slots // 2, length, width), BF)
        taps_shape = jax.ShapeDtypeStruct((most, reach * width), BF)
        part_shape = jax.ShapeDtypeStruct((max(r[1] - r[0] for r in down_ranges) * chunk, width), BF)
        up_part_shape = jax.ShapeDtypeStruct((max(r[1] - r[0] for r in up_ranges) * chunk, width), BF)
        sm = pl.BlockSpec(memory_space=pltpu.SMEM)

        def call(body, index, off, outs, scratch, scalars, *operands):
            k, n, pitch = SCALES[index], taps_of[index], pitches[index]
            return pl.pallas_call(
                functools.partial(body, k, n, pitch, off),
                out_shape=outs,
                in_specs=[sm] * scalars + [VMEM] * (len(operands) - scalars),
                out_specs=jax.tree.map(lambda _: VMEM, outs),
                scratch_shapes=scratch,
                compiler_params=pltpu.CompilerParams(vmem_limit_bytes=60 * MIB),
            )(*operands)

        def rows_scratch(index):
            return pltpu.VMEM((slots * pitches[index], width), BF)

        def spread_scratch(index, count_of=slots):
            return pltpu.VMEM((count_of, width // LANES, pitches[index] * SCALES[index], LANES), F32)

        def down_of(index):
            def run(*operands):
                return call(down_body, index, 0, (windows_shape(F32), windows_shape(BF), taps_shape),
                            [pltpu.VMEM((width // LANES, pitches[index] * SCALES[index], LANES), F32)], 1, *operands)
            return run

        pre, act, taps = branch_index_pair(branch, down_of(0), down_of(1), live, inputs, down_weight, bias)

        passes = 1 if members <= 32 else slots
        per = slots // passes
        pieces = 2 if per % 2 == 0 else 1

        def spread_windows(values, collective_id):
            flat = values.reshape(slots * tall, width)
            return gather_rows(mesh, flat, 0, slots * tall // 2, 2, ((0, 2 * members),) * 2, collective_id).reshape(
                members * slots, tall, width
            )

        def sum_windows(values, collective_id):
            parts = values.reshape(members, passes, per, tall, width)
            results = [
                reduce_rows(mesh, parts[:, p].reshape(-1, width), per * tall // pieces, pieces,
                            ((0, pieces * members),) * 2, collective_id + p, F32)
                for p in range(passes)
            ]
            return jnp.concatenate([r.reshape(per, tall, width) for r in results], axis=0)

        acts = spread_windows(act, 3)
        alive = acts[:, tall - 1, 0] > 0.5
        places = jnp.arange(members * slots)
        rank = jnp.sum(jnp.logical_and(alive[None, :], places[None, :] < places[:, None]).astype(jnp.int32), axis=1)
        order = jnp.sum(
            jnp.where(jnp.logical_and(alive[:, None], rank[:, None] == places[None, :]), places[:, None], 0), axis=0
        ).astype(jnp.int32)
        count = jnp.sum(alive.astype(jnp.int32))[None]
        [terms] = iso_call(False, order, count, shift, iso_weight, acts)
        pre_iso = sum_windows(terms, 16)

        def up_of(index):
            def run(*operands):
                return call(up_body, index, up_offs[index], (full, full), [rows_scratch(index), spread_scratch(index)], 2, *operands)
            return run

        bo_own, bo_send = branch_index_pair(branch, up_of(0), up_of(1), live, half, pre_iso, up_weight, inputs, gain, bias)
        (layer_out, grad_own, arrived, merge_grad, ff_in_grad, ff_out_grad, bias_grad, sums) = feed_call(
            live, bo_own.reshape(-1, width), bo_send.reshape(-1, width), d_out.reshape(-1, width), merge_weight, ff_in,
            ff_in_bias[None], ff_out, shared_biases, shared_gains, 3, 7,
        )
        wide = lax.psum((merge_grad, ff_in_grad, ff_out_grad), ("branch", "dp"))

        def up_back_of(index):
            def run(*operands):
                return call(up_back_body, index, up_offs[index],
                            (windows_shape(BF), jax.ShapeDtypeStruct((8, width), F32), taps_shape, up_part_shape),
                            [rows_scratch(index), spread_scratch(index)], 2, *operands)
            return run

        grad_iso, vectors, grad_taps, up_part = branch_index_pair(
            branch, up_back_of(0), up_back_of(1), live, half, grad_own.reshape(full.shape), arrived.reshape(full.shape), pre_iso, up_weight, inputs, gain, bias
        )
        grads = spread_windows(grad_iso, 4)
        back_terms, kernel_grad = iso_call(True, order, count, shift, iso_weight, acts, grads)
        grad_act = sum_windows(back_terms, 32)

        def down_back_of(index):
            def run(*operands):
                return call(down_back_body, index, 0, (full, full, jax.ShapeDtypeStruct((1, width), F32), part_shape),
                            [rows_scratch(index), spread_scratch(index)], 2, *operands)
            return run

        values_keep, values_send, down_vector, down_part = branch_index_pair(
            branch, down_back_of(0), down_back_of(1), live, half, grad_act, pre, grad_taps, taps, down_weight
        )
        arrived_values = lax.ppermute(values_send, "branch", [(0, 1), (1, 0)])
        grad_inputs = (values_keep.astype(F32) + arrived_values.astype(F32)).astype(BF)

        vectors = jnp.concatenate([vectors[:1], down_vector, vectors[2:5]], axis=0)
        both = jnp.where((jnp.arange(2) == branch)[:, None, None], vectors[None], 0.0).reshape(10, width)
        pieces_of = bias_grad.shape[1] // width
        small = total_over(mesh, jnp.concatenate([sums, bias_grad.reshape(pieces_of, width), both, jnp.zeros((2, width), F32)]), 8)
        own_vectors = lax.dynamic_slice_in_dim(small[8 + pieces_of :], 5 * branch, 5, 0)[None]
        bias_total = small[8 : 8 + pieces_of].reshape(-1)

        up_sum = reduce_rows(mesh, up_part, chunk, npd, up_ranges, 5, F32).reshape(share, width)
        down_sum = reduce_rows(mesh, down_part, chunk, npd, down_ranges, 6, F32, swaps).reshape(share, width)
        group_grads = []
        for g, side in enumerate((down_sum, up_sum)):
            at = g * group_rows + me * share + rows_at
            low, high = (0, k_of * width) if g == 0 else ((k_of + n_of) * width, (2 * k_of + n_of) * width)
            iso_rows = lax.dynamic_slice(kernel_grad, (g * blocks * width + lead[g], 0), (share, width))
            outside = jnp.where(jnp.logical_and(at >= low, at < high)[:, None], side, 0.0)
            group_grads.append(jnp.where(insides[g][:, None], iso_rows, outside))
        grad_blocks = jnp.stack(group_grads)[None]
        return (
            layer_out.reshape(MICRO, 1, 1, length, width), grad_inputs[:, None, None], grad_blocks,
            own_vectors[:, 0], own_vectors[:, 1:], wide[0].astype(F32), wide[1].astype(F32), bias_total,
            wide[2].astype(F32), small[:4], small[4:6],
        )

    from jax.sharding import PartitionSpec as P

    placed = (P("dp", None, None), P("dp"), P("branch", None, "dp", None), P("branch", None), P("branch", None, None), P(), P(), P(),
              P(), P(), P(), P("dp", "branch", None, None, None))
    return jax.shard_map(
        per_device, mesh=mesh, in_specs=placed,
        out_specs=(P("dp", "branch", None, None, None), P("dp", "branch", None, None, None), P("branch", None, "dp", None),
                   P("branch", None), P("branch", None, None), P(), P(), P(), P(), P(), P()),
        check_vma=False,
    )
```

```python
import functools
import jax, jax.numpy as jnp
from jax import lax
from jax.experimental import pallas as pl
from jax.experimental.pallas import tpu as pltpu

MESH = pl.DeviceIdType.MESH
ANY = pl.BlockSpec(memory_space=pl.ANY)


def place():
    me = lax.axis_index("dp")
    return lax.axis_index("branch"), me, me // 4, (me // 2) % 2, me % 2


def listed(j, b, lists):
    found = jnp.bool_(False)
    for which, owners in enumerate(lists):
        for owner in owners:
            found = jnp.logical_or(found, jnp.logical_and(b == which, j == owner))
    return found


def meet(depth, b, me, z):
    barrier = pltpu.get_barrier_semaphore()
    y, c = (me // 2) % 2, me % 2
    pl.semaphore_signal(barrier, 1, device_id=(b, me + 1 - 2 * c), device_id_type=MESH)
    pl.semaphore_signal(barrier, 1, device_id=(b, me + 2 - 4 * y), device_id_type=MESH)

    @pl.when(z > 0)
    def _():
        pl.semaphore_signal(barrier, 1, device_id=(b, me - 4), device_id_type=MESH)

    @pl.when(z < depth - 1)
    def _():
        pl.semaphore_signal(barrier, 1, device_id=(b, me + 4), device_id_type=MESH)

    count = 2 + jnp.where(z > 0, 1, 0) + jnp.where(z < depth - 1, 1, 0)
    pl.semaphore_wait(barrier, count)


def gather_region(depth, npd, rows, base, ranges, swaps, duals, src, dst, hold, local_sem, recv_sem, send_sem):
    b, me, z, y, c = place()
    (a0, a1), (b0, b1) = ranges
    q0 = jnp.where(b == 0, a0, b0)
    q1 = jnp.where(b == 0, a1, b1)
    swap = jnp.where(b == 0, swaps[0], swaps[1])
    core_peer, y_peer = (b, me + 1 - 2 * c), (b, me + 2 - 4 * y)

    def chunk(ref, index):
        return ref.at[pl.ds(pl.multiple_of(index * rows, 8), rows), :]

    def own(i):
        return src.at[pl.ds(pl.multiple_of(base + i * rows, 8), rows), :]

    def remote(kind, q, device, from_own=False):
        k = q - q0
        return pltpu.make_async_remote_copy(
            own(q - me * npd) if from_own else chunk(dst, k), chunk(dst, k), send_sem.at[kind, k], recv_sem.at[k],
            device_id=device, device_id_type=MESH,
        )

    def each_own(what):
        for i in range(npd):
            q = me * npd + i

            @pl.when(jnp.logical_and(q >= q0, q < q1))
            def _():
                what(q, i)

    def take(q, i):
        return pltpu.make_async_copy(own(i), hold.at[i], local_sem.at[0, i])

    def put(q, i):
        return pltpu.make_async_copy(hold.at[i], chunk(dst, q - q0), local_sem.at[1, i])

    def column(j):
        ys = (j // 2) % 2
        return jnp.where(j == swap, 1 - ys, ys)

    def each(core, what):
        def over(zs, t, s):
            for ys in (y, 1 - y):
                j = (zs * 2 + ys) * 2 + core
                col = column(j)
                i = s - t - jnp.where(ys != col, 1, 0) - jnp.where(y != col, 1, 0)
                i = jnp.where(jnp.logical_and(t == 0, ys == y), s, i)
                q = j * npd + i

                @pl.when(jnp.logical_and(jnp.logical_and(i >= 0, i < npd), jnp.logical_and(q >= q0, q < q1)))
                def _():
                    what(q, j)

        def over_step(s):
            def over_far(t, inner):
                @pl.when(z >= t)
                def _():
                    over(z - t, t, s)

                @pl.when(jnp.logical_and(z + t < depth, t > 0))
                def _():
                    over(z + t, t, s)

                return inner

            lax.fori_loop(0, depth, over_far, 0)

        return over_step

    def sends(q, j, act, from_own=False):
        zs, ys = j // 4, (j // 2) % 2
        col, dual = column(j), listed(j, b, duals)
        chain = y == col
        along = jnp.logical_or(chain, dual)

        @pl.when(jnp.logical_and(along, jnp.logical_and(z >= zs, z < depth - 1)))
        def _():
            act(remote(0, q, (b, me + 4), from_own))

        @pl.when(jnp.logical_and(along, jnp.logical_and(z <= zs, z > 0)))
        def _():
            act(remote(1, q, (b, me - 4), from_own))

        start_here = jnp.logical_and(z == zs, ys != col)

        @pl.when(jnp.logical_and(chain != start_here, jnp.logical_or(jnp.logical_not(dual), me == j)))
        def _():
            act(remote(2, q, y_peer, from_own))

        act(remote(3, q, core_peer, from_own))

    def forward(q, j):
        @pl.when(me == j)
        def _():
            sends(q, j, lambda copy: copy.start(), True)

        @pl.when(me != j)
        def _():
            remote(3, q, core_peer).wait_recv()
            sends(q, j, lambda copy: copy.start())

    def begin():
        each_own(lambda q, i: take(q, i).start())

    def swap_own(q, i):
        take(q, i).wait()
        put(q, i).start()

    work = each(c, forward)

    def finish(q, carry):
        j = q // npd

        @pl.when(c == j % 2)
        def _():
            sends(q, j, lambda copy: copy.wait_send())

        @pl.when(c != j % 2)
        def _():
            remote(3, q, core_peer).wait_recv()

        return carry

    def end():
        each_own(swap_own)
        lax.fori_loop(q0, q1, finish, 0)
        each_own(lambda q, i: put(q, i).wait())

    return begin, work, end, npd + depth + 1


def gather_body(depth, regions, *refs):
    count = len(regions)
    src, dsts, scratch = refs[0], refs[1 : 1 + count], refs[1 + count :]
    b, me, z, y, c = place()
    meet(depth, b, me, z)
    phases = [
        gather_region(depth, *region, src, dsts[r], *scratch[4 * r : 4 * r + 4]) for r, region in enumerate(regions)
    ]
    for begin, *_ in phases:
        begin()

    def step(s, carry):
        for phase in phases:
            phase[1](s)
        return carry

    lax.fori_loop(0, max(phase[3] for phase in phases), step, 0)
    for phase in phases:
        phase[2]()


def gather_rows(mesh, src, regions, collective_id):
    depth, width = mesh.shape["dp"] // 4, src.shape[1]
    shapes, scratch = [], []
    for npd, rows, _, ranges, *_ in regions:
        count = max(r[1] - r[0] for r in ranges)
        shapes.append(jax.ShapeDtypeStruct((count * rows, width), src.dtype))
        scratch += [
            pltpu.VMEM((npd, rows, width), src.dtype),
            pltpu.SemaphoreType.DMA((2, npd)),
            pltpu.SemaphoreType.DMA((count,)),
            pltpu.SemaphoreType.DMA((4, count)),
        ]
    return pl.pallas_call(
        functools.partial(gather_body, depth, regions),
        out_shape=shapes,
        in_specs=[ANY],
        out_specs=[ANY] * len(shapes),
        scratch_shapes=scratch,
        compiler_params=pltpu.CompilerParams(collective_id=collective_id, has_side_effects=True),
        cost_estimate=pl.CostEstimate(flops=5 * 10**10, bytes_accessed=2**24, transcendentals=0),
    )(src)


def reduce_region(depth, npd, rows, ranges, swaps, duals, lag, src, out, own, rc, ry, rz, acc, own_sem, rc_sem, ry_sem, rz_sem, send_sem):
    b, me, z, y, c = place()
    (a0, a1), (b0, b1) = ranges
    q0 = jnp.where(b == 0, a0, b0)
    q1 = jnp.where(b == 0, a1, b1)
    swap = jnp.where(b == 0, swaps[0], swaps[1])
    pair0 = q0 // npd // 2
    core_peer, y_peer = (b, me + 1 - 2 * c), (b, me + 2 - 4 * y)
    up, down = (b, jnp.minimum(me + 4, 4 * depth - 1)), (b, jnp.maximum(me - 4, 0))

    def column(j):
        ys = (j // 2) % 2
        return jnp.where(j == swap, 1 - ys, ys)

    def slot(j, i):
        return (j // 2 - pair0) * npd + i

    def part(j, i):
        return src.at[pl.ds(pl.multiple_of((j * npd + i - q0) * rows, 8), rows), :]

    def keep(j, i):
        return pltpu.make_async_copy(part(j, i), own.at[slot(j, i)], own_sem.at[slot(j, i)])

    def remote(kind, frm, to, sem, k, device):
        return pltpu.make_async_remote_copy(
            frm, to, send_sem.at[kind, k], sem, device_id=device, device_id_type=MESH
        )

    def to_core(j, i):
        k = slot(j, i)
        return remote(0, part(j, i), rc.at[k], rc_sem.at[k], k, core_peer)

    def to_y(j, i):
        k = slot(j, i)
        return remote(1, own.at[k], ry.at[k], ry_sem.at[k], k, y_peer)

    def to_z(j, i, way):
        k = slot(j, i)
        return remote(2, own.at[k], rz.at[way, k], rz_sem.at[way, k], k, (up, down)[way])

    def to_owner(j, i):
        k = slot(j, i)
        return remote(2, own.at[k], ry.at[k], ry_sem.at[k], k, y_peer)

    def owners(n, core, what):
        pos, i = n // npd, n % npd
        rising = pos + jnp.where(pos >= z, 1, 0)
        falling = depth - 1 - pos
        falling = falling - jnp.where(falling <= z, 1, 0)
        zs = jnp.where(pos == depth - 1, z, jnp.where(z >= depth // 2, rising, falling))
        for ys in (0, 1):
            j = (zs * 2 + ys) * 2 + core
            q = j * npd + i

            @pl.when(jnp.logical_and(q >= q0, q < q1))
            def _():
                what(j, i, zs, ys)

    total = depth * npd

    def first(n, carry):
        owners(n, 1 - c, lambda j, i, zs, ys: to_core(j, i).start())
        owners(n, c, lambda j, i, zs, ys: keep(j, i).start())
        return carry

    def cross(j, i, zs, ys):
        @pl.when(jnp.logical_and(column(j) != y, jnp.logical_not(listed(j, b, duals))))
        def _():
            k = slot(j, i)
            keep(j, i).wait()
            to_core(j, i).wait_recv()
            own[k] = (own[k].astype(jnp.float32) + rc[k].astype(jnp.float32)).astype(own.dtype)
            to_y(j, i).start()

    def chain(j, i, zs, ys):
        dual = listed(j, b, duals)

        @pl.when(jnp.logical_or(column(j) == y, dual))
        def _():
            k = slot(j, i)
            keep(j, i).wait()
            to_core(j, i).wait_recv()
            acc[...] = own[k].astype(jnp.float32) + rc[k].astype(jnp.float32)

            @pl.when(jnp.logical_or(jnp.logical_not(dual), jnp.logical_and(z == zs, ys == y)))
            def _():
                to_y(j, i).wait_recv()
                acc[...] += ry[k].astype(jnp.float32)

            @pl.when(jnp.logical_and(z >= zs, z < depth - 1))
            def _():
                to_z(j, i, 1).wait_recv()
                acc[...] += rz[1, k].astype(jnp.float32)

            @pl.when(jnp.logical_and(z <= zs, z > 0))
            def _():
                to_z(j, i, 0).wait_recv()
                acc[...] += rz[0, k].astype(jnp.float32)

            @pl.when(jnp.logical_and(z == zs, ys == y))
            def _():
                out[i] = acc[...].astype(out.dtype)

            @pl.when(jnp.logical_not(jnp.logical_and(z == zs, ys == y)))
            def _():
                own[k] = acc[...].astype(own.dtype)

            @pl.when(z > zs)
            def _():
                to_z(j, i, 1).start()

            @pl.when(z < zs)
            def _():
                to_z(j, i, 0).start()

            @pl.when(jnp.logical_and(z == zs, ys != y))
            def _():
                @pl.when(dual)
                def _():
                    to_y(j, i).start()

                @pl.when(jnp.logical_not(dual))
                def _():
                    to_owner(j, i).start()

    def step(s):
        @pl.when(s < total)
        def _():
            owners(s, c, cross)

        @pl.when(jnp.logical_and(s >= lag, s < total + lag))
        def _():
            owners(s - lag, c, chain)

    def sent(j, i, zs, ys):
        dual = listed(j, b, duals)

        @pl.when(jnp.logical_and(column(j) != y, jnp.logical_not(dual)))
        def _():
            to_y(j, i).wait_send()

            @pl.when(me == j)
            def _():
                to_owner(j, i).wait_recv()
                out[i] = ry[slot(j, i)].astype(out.dtype)

        @pl.when(jnp.logical_or(column(j) == y, dual))
        def _():
            @pl.when(z != zs)
            def _():
                to_z(j, i, 0).wait_send()

            @pl.when(jnp.logical_and(z == zs, ys != y))
            def _():
                @pl.when(dual)
                def _():
                    to_y(j, i).wait_send()

                @pl.when(jnp.logical_not(dual))
                def _():
                    to_owner(j, i).wait_send()

    def last(n, carry):
        owners(n, 1 - c, lambda j, i, zs, ys: to_core(j, i).wait_send())
        owners(n, c, sent)
        return carry

    return (
        lambda: lax.fori_loop(0, total, first, 0),
        step,
        lambda: lax.fori_loop(0, total, last, 0),
        total + lag,
    )


def reduce_body(depth, regions, *refs):
    count = len(regions)
    srcs, outs, scratch = refs[:count], refs[count : 2 * count], refs[2 * count :]
    b, me, z, y, c = place()
    meet(depth, b, me, z)
    size = len(scratch) // count
    phases = [
        reduce_region(depth, *region, srcs[r], outs[r], *scratch[size * r : size * (r + 1)]) for r, region in enumerate(regions)
    ]
    for begin, *_ in phases:
        begin()

    def step(s, carry):
        for phase in phases:
            phase[1](s)
        return carry

    lax.fori_loop(0, max(phase[3] for phase in phases), step, 0)
    for phase in phases:
        phase[2]()


def reduce_rows(mesh, srcs, regions, collective_id, dtype, lag=2):
    depth, width = mesh.shape["dp"] // 4, srcs[0].shape[1]
    kind = srcs[0].dtype
    shapes, scratch = [], []
    for npd, rows, ranges, *_ in regions:
        pairs = max((r[1] + npd - 1) // npd // 2 + (r[1] + npd - 1) // npd % 2 - r[0] // npd // 2 for r in ranges)
        held = pairs * npd
        block = (held, rows, width)
        shapes.append(jax.ShapeDtypeStruct((npd, rows, width), dtype))
        scratch += [
            pltpu.VMEM(block, kind),
            pltpu.VMEM(block, kind),
            pltpu.VMEM(block, kind),
            pltpu.VMEM((2, *block), kind),
            pltpu.VMEM((rows, width), jnp.float32),
            pltpu.SemaphoreType.DMA((held,)),
            pltpu.SemaphoreType.DMA((held,)),
            pltpu.SemaphoreType.DMA((held,)),
            pltpu.SemaphoreType.DMA((2, held)),
            pltpu.SemaphoreType.DMA((3, held)),
        ]
    return pl.pallas_call(
        functools.partial(reduce_body, depth, tuple((*region, lag) for region in regions)),
        out_shape=shapes,
        in_specs=[ANY] * len(srcs),
        out_specs=[pl.BlockSpec(memory_space=pltpu.VMEM)] * len(shapes),
        scratch_shapes=scratch,
        compiler_params=pltpu.CompilerParams(
            collective_id=collective_id, has_side_effects=True, vmem_limit_bytes=60 * 2**20
        ),
        cost_estimate=pl.CostEstimate(flops=5 * 10**10, bytes_accessed=2**24, transcendentals=0),
    )(*srcs)
SCALES = (12, 16)
MICRO = 3
GROUPS = 2
EPSILON = 1e-05
BF, F32 = jnp.bfloat16, jnp.float32
MIB = 2**20


def up_to(value, step):
    return (value + step - 1) // step * step


def dot(a, b):
    return jnp.dot(a, b, preferred_element_type=F32)


def dot_bt(a, b):
    return lax.dot_general(a, b, (((1,), (1,)), ((), ())), preferred_element_type=F32)


def dot_at(a, b):
    return lax.dot_general(a, b, (((0,), (0,)), ((), ())), preferred_element_type=F32)


def mean(values):
    return jnp.mean(values, axis=-1, keepdims=True)


def normalise(values):
    centre = values - mean(values)
    rho = lax.rsqrt(mean(centre * centre) + EPSILON)
    return centre * rho, rho


def norm_back(q_gain, xhat, rho):
    return rho * (q_gain - mean(q_gain) - xhat * mean(q_gain * xhat))


def column_sum(values):
    return jnp.sum(values, axis=0, keepdims=True)


VMEM = pl.BlockSpec(memory_space=pltpu.VMEM)


def whole_call(body, out_shape, scratch, limit, cost=None):
    return pl.pallas_call(
        body,
        out_shape=out_shape,
        out_specs=jax.tree.map(lambda _: VMEM, out_shape),
        scratch_shapes=scratch,
        compiler_params=pltpu.CompilerParams(vmem_limit_bytes=limit * MIB),
        cost_estimate=cost,
    )


LANES = 128


def panels(ref, lead, rows):
    return jnp.concatenate([ref[(*lead, p, rows, slice(None))] for p in range(ref.shape[-3])], axis=1)


def set_panels(ref, lead, rows, values):
    for p in range(ref.shape[-3]):
        ref[(*lead, p, rows, slice(None))] = values[:, p * LANES : (p + 1) * LANES]


def down_body(k, n, pitch, off, live, x, weight, bias, pre, act, taps, spread):
    slots, length, width = x.shape
    many = slots * pitch
    spread[:, length:, :] = jnp.zeros((spread.shape[0], spread.shape[1] - length, LANES), F32)

    def window(w, carry):
        set_panels(spread, (), slice(0, length), x[w].astype(F32))
        for r in range(k):
            taps[pl.ds(pl.multiple_of(w * pitch, 16), pitch), r * width : (r + 1) * width] = panels(
                spread, (), pl.ds(r, pitch, stride=k)
            ).astype(BF)
        return carry

    lax.fori_loop(0, slots, window, 0)
    total = dot(taps[:many, : k * width], weight[off : off + k * width, :]) + bias[0:1, :]
    tall = pre.shape[1]
    for w in range(slots):
        rows = fit(total[w * pitch : (w + 1) * pitch], tall)
        pre[w] = rows
        step = lax.broadcasted_iota(jnp.int32, rows.shape, 0)
        flag = jnp.where(step == tall - 1, jnp.where(w < live[0], 1.0, 0.0), 0.0)
        act[w] = jnp.where(step < n, jnp.tanh(rows), flag).astype(BF)


def fit(values, tall):
    rows = values.shape[0]
    if rows >= tall:
        return values[:tall]
    return jnp.concatenate([values, jnp.zeros((tall - rows, values.shape[1]), values.dtype)], axis=0)


def expand(k, n, pitch, off, iso_rows, weight, spread):
    width = iso_rows.shape[1]
    slots = spread.shape[0]

    def tap(r, carry):
        rows = dot(iso_rows[...], weight[pl.ds(pl.multiple_of(off + r * width, 16), width), :])
        for w in range(slots):
            set_panels(spread, (w,), pl.ds(r, pitch, stride=k), rows[w * pitch : (w + 1) * pitch])
        return carry

    lax.fori_loop(0, k, tap, 0)


def iso_of(n, pitch, pre_iso, bias):
    rows = fit(jnp.tanh(pre_iso + bias[1:2, :]), pitch)
    step = lax.broadcasted_iota(jnp.int32, rows.shape, 0)
    return jnp.where(step < n, rows, 0.0)


def up_body(k, n, pitch, off, live, half, pre_iso, weight, x, gain, bias, own, send, iso_rows, spread):
    slots, length, width = x.shape
    for w in range(slots):
        iso = iso_of(n, pitch, pre_iso[w], bias)
        iso_rows[w * pitch : (w + 1) * pitch, :] = jnp.where(w < live[0], iso, 0.0).astype(BF)
    expand(k, n, pitch, off, iso_rows, weight, spread)

    def window(m, carry):
        for out, w in ((send, 2 * m + 1 - half[0]), (own, 2 * m + half[0])):
            values = panels(spread, (w,), slice(0, length)) + bias[2:3, :] + x[w].astype(F32)
            xhat, _ = normalise(values)
            out[m] = (xhat * gain[0:1, :] + bias[3:4, :]).astype(BF)
        return carry

    lax.fori_loop(0, slots // 2, window, 0)


def up_back_body(k, n, pitch, off, live, half, grad_own, grad_arrived, pre_iso, weight, x, gain, bias, grad_iso, vectors, grad_taps, part, iso_rows, spread):
    slots, length, width = x.shape
    for w in range(slots):
        iso = iso_of(n, pitch, pre_iso[w], bias)
        iso_rows[w * pitch : (w + 1) * pitch, :] = jnp.where(w < live[0], iso, 0.0).astype(BF)
    expand(k, n, pitch, off, iso_rows, weight, spread)
    vectors[...] = jnp.zeros_like(vectors)

    def window(m, carry):
        for grad, w in ((grad_own, 2 * m + half[0]), (grad_arrived, 2 * m + 1 - half[0])):
            values = panels(spread, (w,), slice(0, length)) + bias[2:3, :] + x[w].astype(F32)
            xhat, rho = normalise(values)
            q = grad[m].astype(F32)
            residual = norm_back(q * gain[0:1, :], xhat, rho)
            set_panels(spread, (w,), slice(0, length), residual)
            vectors[0:1, :] += column_sum(q * xhat)
            vectors[3:4, :] += column_sum(residual.astype(BF).astype(F32))
            vectors[4:5, :] += column_sum(q)
        return carry

    lax.fori_loop(0, slots // 2, window, 0)

    def tap(w, carry):
        for r in range(k):
            grad_taps[pl.ds(pl.multiple_of(w * pitch, 16), pitch), r * width : (r + 1) * width] = panels(
                spread, (w,), pl.ds(r, pitch, stride=k)
            ).astype(BF)
        return carry

    lax.fori_loop(0, slots, tap, 0)
    total = jnp.zeros((slots * pitch, width), F32)
    for r in range(k):
        rows = grad_taps[: slots * pitch, r * width : (r + 1) * width]
        total += dot_bt(rows, weight[off + r * width : off + (r + 1) * width, :])
        part[off + r * width : off + (r + 1) * width, :] = dot_at(iso_rows[...], rows).astype(BF)
    tall = grad_iso.shape[1]
    for w in range(slots):
        iso = iso_of(n, pitch, pre_iso[w], bias)
        slope = jnp.where(lax.broadcasted_iota(jnp.int32, iso.shape, 0) < n, 1.0 - iso * iso, 0.0)
        back = total[w * pitch : (w + 1) * pitch] * slope
        back = jnp.where(w < live[0], back, 0.0).astype(BF)
        vectors[2:3, :] += column_sum(back.astype(F32))
        grad_iso[w] = fit(back.astype(F32), tall).astype(BF)


def down_back_body(k, n, pitch, off, live, half, grad_act, pre, grad_taps, taps, weight, keep, send, vector, part, rows, spread):
    slots, (length, width) = pre.shape[0], keep.shape[1:]
    vector[...] = jnp.zeros_like(vector)
    for w in range(slots):
        act = jnp.tanh(fit(pre[w], pitch))
        step = lax.broadcasted_iota(jnp.int32, act.shape, 0)
        back = fit(grad_act[w], pitch) * (1.0 - act * act)
        back = jnp.where(jnp.logical_and(step < n, w < live[0]), back, 0.0).astype(BF)
        vector[...] += column_sum(back.astype(F32))
        rows[w * pitch : (w + 1) * pitch, :] = back
    for r in range(k):
        back = dot_bt(rows[...], weight[off + r * width : off + (r + 1) * width, :])
        back += grad_taps[: slots * pitch, r * width : (r + 1) * width].astype(F32)
        for w in range(slots):
            set_panels(spread, (w,), pl.ds(r, pitch, stride=k), back[w * pitch : (w + 1) * pitch])
        part[off + r * width : off + (r + 1) * width, :] = dot_at(
            taps[: slots * pitch, r * width : (r + 1) * width], rows[...]
        ).astype(BF)

    def window(m, carry):
        send[m] = panels(spread, (2 * m + 1 - half[0],), slice(0, length)).astype(BF)
        keep[m] = panels(spread, (2 * m + half[0],), slice(0, length)).astype(BF)
        return carry

    lax.fori_loop(0, slots // 2, window, 0)


SUBLANES = 8


def shifted(ref, start, tall):
    width = ref.shape[1]
    first = pl.multiple_of(start // SUBLANES * SUBLANES, SUBLANES)
    ahead = start % SUBLANES
    tiles = ref[pl.ds(first, tall + SUBLANES), :].reshape(tall // SUBLANES + 1, SUBLANES, width)
    turned = pltpu.roll(tiles, (SUBLANES - ahead) % SUBLANES, 1)
    row = lax.broadcasted_iota(jnp.int32, (tall // SUBLANES, SUBLANES, width), 1)
    return jnp.where(row < SUBLANES - ahead, turned[:-1], turned[1:]).reshape(tall, width).astype(BF)


PACK = 8


def iso_specs(tall, width, pieces):
    def spec(e):
        def at(step, order, count, shift):
            last = jnp.maximum(count[0] - 1, 0) // PACK
            return order[jnp.minimum(step, last) * PACK + e], 0, 0

        return pl.BlockSpec((1, tall, width), at)

    return [spec(e) for e in range(PACK)]


def scatter_out(order, count, slots_ref, sem, out, tall, step, steps):
    def copy(at, e):
        where = jnp.minimum(at * PACK + e, order.shape[0] - 1)
        return pltpu.make_async_copy(
            slots_ref.at[at % 2, e], out.at[order[where]], sem.at[at % 2, e]
        )

    live = pl.cdiv(count[0], PACK)

    @pl.when(step < live)
    def _():
        for e in range(PACK):
            @pl.when(step * PACK + e < count[0])
            def _():
                copy(step, e).start()

    @pl.when(jnp.logical_and(step >= 1, step <= live))
    def _():
        for e in range(PACK):
            @pl.when((step - 1) * PACK + e < count[0])
            def _():
                copy(step - 1, e).wait()

    @pl.when(jnp.logical_and(step == steps - 1, live == steps))
    def _():
        for e in range(PACK):
            @pl.when(step * PACK + e < count[0])
            def _():
                copy(step, e).wait()


def iso_forward_body(tall, pitch, blocks, steps, order, count, shift, *refs):
    acts, (weight, out, buffer, columns, ready, sem) = refs[:PACK], refs[PACK:]
    step = pl.program_id(0)
    width = weight.shape[1]

    @pl.when(step == 0)
    def _():
        buffer[...] = jnp.zeros_like(buffer)
        columns[...] = jnp.zeros_like(columns)

    @pl.when(step * PACK < count[0])
    def _():
        for e in range(PACK):
            buffer[tall : 2 * tall, :] = (jnp.where(step * PACK + e < count[0], acts[e][0].astype(F32), 0.0))
            for m in range(blocks):
                columns[e * pitch : e * pitch + tall, m * width : (m + 1) * width] = shifted(buffer, tall - shift[m], tall)
        total = dot(columns[...], weight[...])
        for e in range(PACK):
            ready[step % 2, e] = total[e * pitch : e * pitch + tall].astype(BF)

    scatter_out(order, count, ready, sem, out, tall, step, steps)


def iso_back_body(tall, pitch, blocks, steps, order, count, shift, *refs):
    acts, grads = refs[:PACK], refs[PACK : 2 * PACK]
    weight, out, kernel_grad, buffer, columns, gathered, ahead, ready, sem = refs[2 * PACK :]
    step = pl.program_id(0)
    width = weight.shape[1]

    @pl.when(step == 0)
    def _():
        buffer[...] = jnp.zeros_like(buffer)
        columns[...] = jnp.zeros_like(columns)
        gathered[...] = jnp.zeros_like(gathered)
        ahead[...] = jnp.zeros_like(ahead)
        kernel_grad[...] = jnp.zeros_like(kernel_grad)

    @pl.when(step * PACK < count[0])
    def _():
        for e in range(PACK):
            alive = step * PACK + e < count[0]
            buffer[tall : 2 * tall, :] = (jnp.where(alive, acts[e][0].astype(F32), 0.0))
            for m in range(blocks):
                columns[e * pitch : e * pitch + tall, m * width : (m + 1) * width] = shifted(buffer, tall - shift[m], tall)
            gathered[e * pitch : e * pitch + tall, :] = jnp.where(alive, grads[e][0].astype(F32), 0.0).astype(BF)
        for m in range(blocks):
            kernel_grad[m * width : (m + 1) * width, :] += dot_at(columns[:, m * width : (m + 1) * width], gathered[...])
        for e in range(PACK):
            alive = step * PACK + e < count[0]
            ahead[:tall, :] = (jnp.where(alive, grads[e][0].astype(F32), 0.0))
            for m in range(blocks):
                columns[e * pitch : e * pitch + tall, m * width : (m + 1) * width] = shifted(ahead, shift[m], tall)
        total = dot_bt(columns[:, :width], weight[:width, :])
        for m in range(1, blocks):
            total += dot_bt(columns[:, m * width : (m + 1) * width], weight[m * width : (m + 1) * width, :])
        for e in range(PACK):
            ready[step % 2, e] = total[e * pitch : e * pitch + tall].astype(BF)

    scatter_out(order, count, ready, sem, out, tall, step, steps)


def iso_call(back, order, count, shift, weight, *windows):
    many, tall, width = windows[0].shape
    blocks = weight.shape[0] // width
    pitch = up_to(tall, 16)
    steps = many // PACK
    held = pl.BlockSpec(weight.shape, lambda step, *_: (0, 0))
    out_shape = [jax.ShapeDtypeStruct((many, tall, width), BF)]
    out_specs = [ANY]
    copies = pltpu.VMEM((2 * tall + SUBLANES, width), F32)
    scratch = [copies, pltpu.VMEM((PACK * pitch, blocks * width), BF)]
    if back:
        out_shape.append(jax.ShapeDtypeStruct(weight.shape, F32))
        out_specs.append(held)
        scratch += [pltpu.VMEM((PACK * pitch, width), BF), copies]
    scratch += [pltpu.VMEM((2, PACK, tall, width), BF), pltpu.SemaphoreType.DMA((2, PACK))]
    body = iso_back_body if back else iso_forward_body
    flops = 2 * many * tall * weight.size * (2 if back else 1) // 3
    return pl.pallas_call(
        functools.partial(body, tall, pitch, blocks, steps),
        out_shape=out_shape,
        grid_spec=pltpu.PrefetchScalarGridSpec(
            num_scalar_prefetch=3,
            grid=(steps,),
            in_specs=[s for _ in windows for s in iso_specs(tall, width, steps)] + [held],
            out_specs=out_specs,
            scratch_shapes=scratch,
        ),
        compiler_params=pltpu.CompilerParams(vmem_limit_bytes=56 * MIB),
        cost_estimate=pl.CostEstimate(flops=flops, bytes_accessed=4 * MIB, transcendentals=0),
    )(order, count, shift, *[v for v in windows for _ in range(PACK)], weight)


def feed_body(per_window, tile, live, own, bo_send, d_out, merge_weight, ff_in, ff_in_bias, ff_out, biases, gains,
              layer_out, grad_own, arrived, merge_grad, in_grad, out_grad, bias_grad, sums,
              slope, hidden_kept, other_slots, grad_slots, merge_sum, in_sum, out_sum, bo_sent, bo_come, back_sent, back_come):
    step, steps = pl.program_id(0), pl.num_programs(0)
    branch, me = lax.axis_index("branch"), lax.axis_index("dp")
    partner = (1 - branch, me)
    block, width = own.shape

    def forth(at):
        return pltpu.make_async_remote_copy(
            bo_send.at[pl.ds(pl.multiple_of(at * block, 8), block), :], other_slots.at[at], bo_sent.at[at], bo_come.at[at],
            device_id=partner, device_id_type=MESH,
        )

    def back_copy(at):
        return pltpu.make_async_remote_copy(
            grad_slots.at[at], arrived.at[pl.ds(pl.multiple_of(at * block, 8), block), :], back_sent.at[at], back_come.at[at],
            device_id=partner, device_id_type=MESH,
        )

    @pl.when(step == 0)
    def _():
        barrier = pltpu.get_barrier_semaphore()
        pl.semaphore_signal(barrier, 1, device_id=partner, device_id_type=MESH)
        pl.semaphore_wait(barrier, 1)
        forth(0).start()
        forth(1).start()
        bias_grad[...] = jnp.zeros_like(bias_grad)
        sums[...] = jnp.zeros_like(sums)
        merge_sum[...] = jnp.zeros_like(merge_sum)
        in_sum[...] = jnp.zeros_like(in_sum)
        out_sum[...] = jnp.zeros_like(out_sum)

    forth(step).wait_recv()

    @pl.when(step + 2 < steps)
    def _():
        forth(step + 2).start()

    alive = jnp.where(2 * (step // per_window) + branch < live[0], 1.0, 0.0)
    own_rows, other_rows = own[...], other_slots[step]
    own_at = pl.ds(pl.multiple_of(branch * width, width), width)
    other_at = pl.ds(pl.multiple_of((1 - branch) * width, width), width)
    merged = dot(own_rows, merge_weight[own_at, :]) + dot(other_rows, merge_weight[other_at, :]) + biases[0:1, :]
    xhat_one, rho_one = normalise(merged)
    normed = (xhat_one * gains[0:1, :] + biases[1:2, :]).astype(BF)
    units = ff_in.shape[1]
    total = merged + biases[2:3, :]
    for u in range(0, units, tile):
        inner = dot(normed, ff_in[:, u : u + tile]) + ff_in_bias[:, u : u + tile]
        phi_total = 0.5 * (1.0 + lax.erf(inner * 0.7071067811865476))
        hidden = (inner * phi_total).astype(BF)
        slope[:, u : u + tile] = phi_total + inner * (jnp.exp(-0.5 * inner * inner) * 0.3989422804014327)
        hidden_kept[:, u : u + tile] = hidden
        total += dot(hidden, ff_out[u : u + tile, :])
    xhat_two, rho_two = normalise(total)
    layer_out[...] = ((xhat_two * gains[1:2, :] + biases[3:4, :]) * alive).astype(BF)
    q = d_out[...].astype(F32) * alive
    grad_sum = norm_back(q * gains[1:2, :], xhat_two, rho_two)
    grad_outer = grad_sum.astype(BF)
    back = jnp.zeros_like(merged)
    for u in range(0, units, tile):
        grad_inner = (dot_bt(grad_outer, ff_out[u : u + tile, :]) * slope[:, u : u + tile]).astype(BF)
        bias_grad[:, u : u + tile] += column_sum(grad_inner.astype(F32))
        back += dot_bt(grad_inner, ff_in[:, u : u + tile])
        in_sum[:, u : u + tile] += dot_at(normed, grad_inner)
        out_sum[u : u + tile, :] += dot_at(hidden_kept[:, u : u + tile], grad_outer)
    grad_merged = (grad_sum + norm_back(back * gains[0:1, :], xhat_one, rho_one)).astype(BF)
    grad_slots[step] = dot_bt(grad_merged, merge_weight[other_at, :]).astype(BF)
    back_copy(step).start()
    grad_own[...] = dot_bt(grad_merged, merge_weight[own_at, :]).astype(BF)
    merge_sum[own_at, :] += dot_at(own_rows, grad_merged)
    merge_sum[other_at, :] += dot_at(other_rows, grad_merged)
    sums[0:1, :] += column_sum(grad_merged.astype(F32))
    sums[1:2, :] += column_sum(back)
    sums[2:3, :] += column_sum(grad_outer.astype(F32))
    sums[3:4, :] += column_sum(q)
    sums[4:5, :] += column_sum(back * xhat_one)
    sums[5:6, :] += column_sum(q * xhat_two)

    @pl.when(step == steps - 1)
    def _():
        merge_grad[...] = merge_sum[...].astype(BF)
        in_grad[...] = in_sum[...].astype(BF)
        out_grad[...] = out_sum[...].astype(BF)

        def finish(at, carry):
            forth(at).wait_send()
            back_copy(at).wait_send()
            back_copy(at).wait_recv()
            return carry

        lax.fori_loop(0, steps, finish, 0)


def feed_call(live, own, bo_send, d_out, merge_weight, ff_in, ff_in_bias, ff_out, biases, gains, per_window, collective_id):
    rows, width = own.shape
    units = ff_in.shape[1]
    steps = MICRO * per_window
    block = rows // steps

    def rowed(columns):
        return pl.BlockSpec((block, columns), lambda step, *_: (step, 0))

    def held(shape):
        return pl.BlockSpec(shape, lambda step, *_: (0, 0), pipeline_mode=pl.Buffered(1))

    def shaped(*shape):
        return jax.ShapeDtypeStruct(shape, BF)

    weights = (merge_weight, ff_in, ff_in_bias, ff_out, biases, gains)
    outs = [(rows, width), (rows, width), (rows, width), merge_weight.shape, ff_in.shape, ff_out.shape]
    return pl.pallas_call(
        functools.partial(feed_body, per_window, 512),
        out_shape=[shaped(*s) for s in outs] + [jax.ShapeDtypeStruct((1, units), F32), jax.ShapeDtypeStruct((8, width), F32)],
        grid_spec=pltpu.PrefetchScalarGridSpec(
            num_scalar_prefetch=1,
            grid=(steps,),
            in_specs=[rowed(width), ANY, rowed(width)] + [held(v.shape) for v in weights],
            out_specs=[rowed(width), rowed(width), ANY] + [held(s) for s in outs[3:]] + [held((1, units)), held((8, width))],
            scratch_shapes=[
                pltpu.VMEM((block, units), F32), pltpu.VMEM((block, units), BF), pltpu.VMEM((steps, block, width), BF),
                pltpu.VMEM((steps, block, width), BF), pltpu.VMEM(merge_weight.shape, F32), pltpu.VMEM(ff_in.shape, F32),
                pltpu.VMEM(ff_out.shape, F32), pltpu.SemaphoreType.DMA((steps,)), pltpu.SemaphoreType.DMA((steps,)),
                pltpu.SemaphoreType.DMA((steps,)), pltpu.SemaphoreType.DMA((steps,)),
            ],
        ),
        compiler_params=pltpu.CompilerParams(vmem_limit_bytes=58 * MIB, collective_id=collective_id, has_side_effects=True),
        cost_estimate=pl.CostEstimate(flops=rows * width * units * 2 * 8, bytes_accessed=40 * MIB, transcendentals=rows * units),
    )(live, own, bo_send, d_out, *weights)


def total_body(depth, values, out, pair, come, far, sent_sem, come_sem, far_sent, far_come):
    b, me, z, y, c = place()
    peers = ((b, me + 1 - 2 * c), (1 - b, me), (b, me + 2 - 4 * y))
    barrier = pltpu.get_barrier_semaphore()
    for peer in peers:
        pl.semaphore_signal(barrier, 1, device_id=peer, device_id_type=MESH)

    def along(what):
        def each(other, carry):
            @pl.when(other != z)
            def _():
                what(other)

            return carry

        lax.fori_loop(0, depth, each, 0)

    def at_row(other):
        return b, me + 4 * (other - z)

    along(lambda other: pl.semaphore_signal(barrier, 1, device_id=at_row(other), device_id_type=MESH))
    pl.semaphore_wait(barrier, len(peers) + depth - 1)
    pair[0] = values[...]
    for step, peer in enumerate(peers):
        copy = pltpu.make_async_remote_copy(
            pair.at[step], come.at[step], sent_sem.at[step], come_sem.at[step], device_id=peer, device_id_type=MESH
        )
        copy.start()
        copy.wait()
        pair[step + 1] = pair[step] + come[step]

    def outward(other):
        return pltpu.make_async_remote_copy(
            pair.at[len(peers)], far.at[z], far_sent.at[other], far_come.at[z], device_id=at_row(other), device_id_type=MESH
        )

    def inward(other):
        return pltpu.make_async_remote_copy(
            pair.at[len(peers)], far.at[other], far_sent.at[other], far_come.at[other], device_id=at_row(other), device_id_type=MESH
        )

    along(lambda other: outward(other).start())
    far[z] = pair[len(peers)]
    along(lambda other: outward(other).wait_send())
    along(lambda other: inward(other).wait_recv())
    out[...] = far[0]

    def add(other, carry):
        out[...] += far[other]
        return carry

    lax.fori_loop(1, depth, add, 0)


def total_over(mesh, values, collective_id):
    depth = mesh.shape["dp"] // 4
    return pl.pallas_call(
        functools.partial(total_body, depth),
        out_shape=jax.ShapeDtypeStruct(values.shape, F32),
        in_specs=[VMEM],
        out_specs=VMEM,
        scratch_shapes=[
            pltpu.VMEM((4, *values.shape), F32), pltpu.VMEM((3, *values.shape), F32), pltpu.VMEM((depth, *values.shape), F32),
            pltpu.SemaphoreType.DMA((3,)), pltpu.SemaphoreType.DMA((3,)), pltpu.SemaphoreType.DMA((depth,)),
            pltpu.SemaphoreType.DMA((depth,)),
        ],
        compiler_params=pltpu.CompilerParams(collective_id=collective_id, has_side_effects=True),
    )(values)


def branch_index_pair(branch, first, second, *operands):
    return lax.cond(branch == 0, first, second, *operands)


def solution(mesh):
    def per_device(inputs, window_count, branch_blocks, branch_gains, branch_biases, merge_weight, ff_in, ff_in_bias, ff_out,
                   shared_biases, shared_gains, d_out):
        members = mesh.shape["dp"]
        branch, me = lax.axis_index("branch"), lax.axis_index("dp")
        slots, length, width = inputs.shape
        group_rows = branch_blocks.shape[2] * members
        share = branch_blocks.shape[2]
        taps_of = [length // k for k in SCALES]
        tall = up_to(max(taps_of) + 1, 8)
        pitches = [up_to(n, 16) for n in taps_of]
        reach = max(SCALES)
        most = slots * max(pitches)
        live = window_count.astype(jnp.int32)
        half = branch.astype(jnp.int32)[None]
        gain, bias = branch_gains, branch_biases[0]

        npd = 8 if share % 64 == 0 else 1
        chunk = share // npd
        down_ranges = tuple((0, -(-k * width // chunk)) for k in SCALES)
        up_starts = [(k + n) * width - group_rows for k, n in zip(SCALES, taps_of)]
        up_ranges = tuple((s // chunk, -(-(s + k * width) // chunk)) for s, k in zip(up_starts, SCALES))
        up_offs = [s - r[0] * chunk for s, r in zip(up_starts, up_ranges)]
        swaps = (-1, 1) if members == 16 else (-1, -1)
        none = ((), ())
        own_rows = branch_blocks.reshape(GROUPS * share, width)
        down_weight, up_weight = gather_rows(
            mesh, own_rows, ((npd, chunk, 0, down_ranges, swaps, none), (npd, chunk, share, up_ranges, (-1, -1), none)), 1
        )

        blocks = (share + width - 1) // width + 1
        k_of = jnp.where(branch == 0, SCALES[0], SCALES[1])
        n_of = jnp.where(branch == 0, taps_of[0], taps_of[1])
        rows_at = jnp.arange(share)
        padded, shifts, insides, lead = [], [], [], []
        for g in range(GROUPS):
            first = g * group_rows + me * share - k_of * width
            inside = jnp.logical_and(first + rows_at >= 0, first + rows_at < n_of * width)
            start = first // width
            shifts.append(jnp.clip(n_of - 1 - start - jnp.arange(blocks), 0, tall))
            lead.append(first - start * width)
            insides.append(inside)
            kept = jnp.where(inside[:, None], own_rows[g * share : (g + 1) * share], 0)
            padded.append(lax.dynamic_update_slice(jnp.zeros((blocks * width, width), BF), kept, (lead[g], 0)))
        iso_weight = jnp.concatenate(padded, axis=0)
        shift = jnp.concatenate(shifts).astype(jnp.int32)

        def windows_shape(kind):
            return jax.ShapeDtypeStruct((slots, tall, width), kind)

        full = jax.ShapeDtypeStruct((slots // 2, length, width), BF)
        taps_shape = jax.ShapeDtypeStruct((most, reach * width), BF)
        part_shape = jax.ShapeDtypeStruct((max(r[1] - r[0] for r in down_ranges) * chunk, width), BF)
        up_part_shape = jax.ShapeDtypeStruct((max(r[1] - r[0] for r in up_ranges) * chunk, width), BF)
        sm = pl.BlockSpec(memory_space=pltpu.SMEM)

        def call(body, index, off, outs, scratch, scalars, *operands):
            k, n, pitch = SCALES[index], taps_of[index], pitches[index]
            return pl.pallas_call(
                functools.partial(body, k, n, pitch, off),
                out_shape=outs,
                in_specs=[sm] * scalars + [VMEM] * (len(operands) - scalars),
                out_specs=jax.tree.map(lambda _: VMEM, outs),
                scratch_shapes=scratch,
                compiler_params=pltpu.CompilerParams(vmem_limit_bytes=60 * MIB),
            )(*operands)

        def rows_scratch(index):
            return pltpu.VMEM((slots * pitches[index], width), BF)

        def spread_scratch(index, count_of=slots):
            return pltpu.VMEM((count_of, width // LANES, pitches[index] * SCALES[index], LANES), F32)

        def down_of(index):
            def run(*operands):
                return call(down_body, index, 0, (windows_shape(F32), windows_shape(BF), taps_shape),
                            [pltpu.VMEM((width // LANES, pitches[index] * SCALES[index], LANES), F32)], 1, *operands)
            return run

        pre, act, taps = branch_index_pair(branch, down_of(0), down_of(1), live, inputs, down_weight, bias)

        passes = 1 if members <= 32 else slots
        per = slots // passes
        pieces = 2 if per % 2 == 0 else 1

        def spread_windows(values, collective_id):
            flat = values.reshape(slots * tall, width)
            [every] = gather_rows(mesh, flat, ((2, slots * tall // 2, 0, ((0, 2 * members),) * 2, (-1, -1), none),), collective_id)
            return every.reshape(members * slots, tall, width)

        def sum_windows(values, collective_id):
            parts = values.reshape(members, passes, per, tall, width)
            results = [
                reduce_rows(mesh, [parts[:, p].reshape(-1, width)],
                            ((pieces, per * tall // pieces, ((0, pieces * members),) * 2, (-1, -1), none),), collective_id + p, F32)[0]
                for p in range(passes)
            ]
            return jnp.concatenate([r.reshape(per, tall, width) for r in results], axis=0)

        acts = spread_windows(act, 3)
        alive = acts[:, tall - 1, 0] > 0.5
        places = jnp.arange(members * slots)
        rank = jnp.sum(jnp.logical_and(alive[None, :], places[None, :] < places[:, None]).astype(jnp.int32), axis=1)
        order = jnp.sum(
            jnp.where(jnp.logical_and(alive[:, None], rank[:, None] == places[None, :]), places[:, None], 0), axis=0
        ).astype(jnp.int32)
        count = jnp.sum(alive.astype(jnp.int32))[None]
        [terms] = iso_call(False, order, count, shift, iso_weight, acts)
        pre_iso = sum_windows(terms, 16)

        def up_of(index):
            def run(*operands):
                return call(up_body, index, up_offs[index], (full, full), [rows_scratch(index), spread_scratch(index)], 2, *operands)
            return run

        bo_own, bo_send = branch_index_pair(branch, up_of(0), up_of(1), live, half, pre_iso, up_weight, inputs, gain, bias)
        (layer_out, grad_own, arrived, merge_grad, ff_in_grad, ff_out_grad, bias_grad, sums) = feed_call(
            live, bo_own.reshape(-1, width), bo_send.reshape(-1, width), d_out.reshape(-1, width), merge_weight, ff_in,
            ff_in_bias[None], ff_out, shared_biases, shared_gains, 3, 7,
        )
        wide = lax.psum((merge_grad, ff_in_grad, ff_out_grad), ("branch", "dp"))

        def up_back_of(index):
            def run(*operands):
                return call(up_back_body, index, up_offs[index],
                            (windows_shape(BF), jax.ShapeDtypeStruct((8, width), F32), taps_shape, up_part_shape),
                            [rows_scratch(index), spread_scratch(index)], 2, *operands)
            return run

        grad_iso, vectors, grad_taps, up_part = branch_index_pair(
            branch, up_back_of(0), up_back_of(1), live, half, grad_own.reshape(full.shape), arrived.reshape(full.shape), pre_iso, up_weight, inputs, gain, bias
        )
        grads = spread_windows(grad_iso, 4)
        back_terms, kernel_grad = iso_call(True, order, count, shift, iso_weight, acts, grads)
        grad_act = sum_windows(back_terms, 32)
        grad_act, wide = lax.optimization_barrier((grad_act, wide))

        def down_back_of(index):
            def run(*operands):
                return call(down_back_body, index, 0, (full, full, jax.ShapeDtypeStruct((1, width), F32), part_shape),
                            [rows_scratch(index), spread_scratch(index)], 2, *operands)
            return run

        values_keep, values_send, down_vector, down_part = branch_index_pair(
            branch, down_back_of(0), down_back_of(1), live, half, grad_act, pre, grad_taps, taps, down_weight
        )
        vectors = jnp.concatenate([vectors[:1], down_vector, vectors[2:5]], axis=0)
        both = jnp.where((jnp.arange(2) == branch)[:, None, None], vectors[None], 0.0).reshape(10, width)
        pieces_of = bias_grad.shape[1] // width
        small = total_over(mesh, jnp.concatenate([sums, bias_grad.reshape(pieces_of, width), both, jnp.zeros((2, width), F32)]), 8)
        values_send, small = lax.optimization_barrier((values_send, small))
        arrived_values = lax.ppermute(values_send, "branch", [(0, 1), (1, 0)])
        grad_inputs = (values_keep.astype(F32) + arrived_values.astype(F32)).astype(BF)
        own_vectors = lax.dynamic_slice_in_dim(small[8 + pieces_of :], 5 * branch, 5, 0)[None]
        bias_total = small[8 : 8 + pieces_of].reshape(-1)

        up_sum, down_sum = [
            total.reshape(share, width)
            for total in reduce_rows(
                mesh, [up_part, down_part], ((npd, chunk, up_ranges, (-1, -1), none), (npd, chunk, down_ranges, swaps, none)), 5,
                BF, 6,
            )
        ]
        group_grads = []
        for g, side in enumerate((down_sum, up_sum)):
            at = g * group_rows + me * share + rows_at
            low, high = (0, k_of * width) if g == 0 else ((k_of + n_of) * width, (2 * k_of + n_of) * width)
            iso_rows = lax.dynamic_slice(kernel_grad, (g * blocks * width + lead[g], 0), (share, width))
            outside = jnp.where(jnp.logical_and(at >= low, at < high)[:, None], side.astype(F32), 0.0)
            group_grads.append(jnp.where(insides[g][:, None], iso_rows, outside))
        grad_blocks = jnp.stack(group_grads)[None]
        return (
            layer_out.reshape(MICRO, 1, 1, length, width), grad_inputs[:, None, None], grad_blocks,
            own_vectors[:, 0], own_vectors[:, 1:], wide[0].astype(F32), wide[1].astype(F32), bias_total,
            wide[2].astype(F32), small[:4], small[4:6],
        )

    from jax.sharding import PartitionSpec as P

    placed = (P("dp", None, None), P("dp"), P("branch", None, "dp", None), P("branch", None), P("branch", None, None), P(), P(), P(),
              P(), P(), P(), P("dp", "branch", None, None, None))
    return jax.shard_map(
        per_device, mesh=mesh, in_specs=placed,
        out_specs=(P("dp", "branch", None, None, None), P("dp", "branch", None, None, None), P("branch", None, "dp", None),
                   P("branch", None), P("branch", None, None), P(), P(), P(), P(), P(), P()),
        check_vma=False,
    )
```

```python
import functools
import jax, jax.numpy as jnp
from jax import lax
from jax.experimental import pallas as pl
from jax.experimental.pallas import tpu as pltpu

MESH = pl.DeviceIdType.MESH
ANY = pl.BlockSpec(memory_space=pl.ANY)


def place():
    me = lax.axis_index("dp")
    return lax.axis_index("branch"), me, me // 4, (me // 2) % 2, me % 2


def listed(j, b, lists):
    found = jnp.bool_(False)
    for which, owners in enumerate(lists):
        for owner in owners:
            found = jnp.logical_or(found, jnp.logical_and(b == which, j == owner))
    return found


def meet(depth, b, me, z):
    barrier = pltpu.get_barrier_semaphore()
    y, c = (me // 2) % 2, me % 2
    pl.semaphore_signal(barrier, 1, device_id=(b, me + 1 - 2 * c), device_id_type=MESH)
    pl.semaphore_signal(barrier, 1, device_id=(b, me + 2 - 4 * y), device_id_type=MESH)

    @pl.when(z > 0)
    def _():
        pl.semaphore_signal(barrier, 1, device_id=(b, me - 4), device_id_type=MESH)

    @pl.when(z < depth - 1)
    def _():
        pl.semaphore_signal(barrier, 1, device_id=(b, me + 4), device_id_type=MESH)

    count = 2 + jnp.where(z > 0, 1, 0) + jnp.where(z < depth - 1, 1, 0)
    pl.semaphore_wait(barrier, count)


def gather_region(depth, npd, rows, base, ranges, swaps, duals, src, dst, hold, local_sem, recv_sem, send_sem):
    b, me, z, y, c = place()
    (a0, a1), (b0, b1) = ranges
    q0 = jnp.where(b == 0, a0, b0)
    q1 = jnp.where(b == 0, a1, b1)
    swap = jnp.where(b == 0, swaps[0], swaps[1])
    core_peer, y_peer = (b, me + 1 - 2 * c), (b, me + 2 - 4 * y)

    def chunk(ref, index):
        return ref.at[pl.ds(pl.multiple_of(index * rows, 8), rows), :]

    def own(i):
        return src.at[pl.ds(pl.multiple_of(base + i * rows, 8), rows), :]

    def remote(kind, q, device, from_own=False):
        k = q - q0
        return pltpu.make_async_remote_copy(
            own(q - me * npd) if from_own else chunk(dst, k), chunk(dst, k), send_sem.at[kind, k], recv_sem.at[k],
            device_id=device, device_id_type=MESH,
        )

    def each_own(what):
        for i in range(npd):
            q = me * npd + i

            @pl.when(jnp.logical_and(q >= q0, q < q1))
            def _():
                what(q, i)

    def take(q, i):
        return pltpu.make_async_copy(own(i), hold.at[i], local_sem.at[0, i])

    def put(q, i):
        return pltpu.make_async_copy(hold.at[i], chunk(dst, q - q0), local_sem.at[1, i])

    def column(j):
        ys = (j // 2) % 2
        return jnp.where(j == swap, 1 - ys, ys)

    def each(core, what):
        def over(zs, t, s):
            for ys in (y, 1 - y):
                j = (zs * 2 + ys) * 2 + core
                col = column(j)
                i = s - t - jnp.where(ys != col, 1, 0) - jnp.where(y != col, 1, 0)
                i = jnp.where(jnp.logical_and(t == 0, ys == y), s, i)
                q = j * npd + i

                @pl.when(jnp.logical_and(jnp.logical_and(i >= 0, i < npd), jnp.logical_and(q >= q0, q < q1)))
                def _():
                    what(q, j)

        def over_step(s):
            def over_far(t, inner):
                @pl.when(z >= t)
                def _():
                    over(z - t, t, s)

                @pl.when(jnp.logical_and(z + t < depth, t > 0))
                def _():
                    over(z + t, t, s)

                return inner

            lax.fori_loop(0, depth, over_far, 0)

        return over_step

    def sends(q, j, act, from_own=False):
        zs, ys = j // 4, (j // 2) % 2
        col, dual = column(j), listed(j, b, duals)
        chain = y == col
        along = jnp.logical_or(chain, dual)

        @pl.when(jnp.logical_and(along, jnp.logical_and(z >= zs, z < depth - 1)))
        def _():
            act(remote(0, q, (b, me + 4), from_own))

        @pl.when(jnp.logical_and(along, jnp.logical_and(z <= zs, z > 0)))
        def _():
            act(remote(1, q, (b, me - 4), from_own))

        start_here = jnp.logical_and(z == zs, ys != col)

        @pl.when(jnp.logical_and(chain != start_here, jnp.logical_or(jnp.logical_not(dual), me == j)))
        def _():
            act(remote(2, q, y_peer, from_own))

        act(remote(3, q, core_peer, from_own))

    def forward(q, j):
        @pl.when(me == j)
        def _():
            sends(q, j, lambda copy: copy.start(), True)

        @pl.when(me != j)
        def _():
            remote(3, q, core_peer).wait_recv()
            sends(q, j, lambda copy: copy.start())

    def begin():
        each_own(lambda q, i: take(q, i).start())

    def swap_own(q, i):
        take(q, i).wait()
        put(q, i).start()

    work = each(c, forward)

    def finish(q, carry):
        j = q // npd

        @pl.when(c == j % 2)
        def _():
            sends(q, j, lambda copy: copy.wait_send())

        @pl.when(c != j % 2)
        def _():
            remote(3, q, core_peer).wait_recv()

        return carry

    def end():
        each_own(swap_own)
        lax.fori_loop(q0, q1, finish, 0)
        each_own(lambda q, i: put(q, i).wait())

    return begin, work, end, npd + depth + 1


def gather_body(depth, regions, *refs):
    count = len(regions)
    src, dsts, scratch = refs[0], refs[1 : 1 + count], refs[1 + count :]
    b, me, z, y, c = place()
    meet(depth, b, me, z)
    phases = [
        gather_region(depth, *region, src, dsts[r], *scratch[4 * r : 4 * r + 4]) for r, region in enumerate(regions)
    ]
    for begin, *_ in phases:
        begin()

    def step(s, carry):
        for phase in phases:
            phase[1](s)
        return carry

    lax.fori_loop(0, max(phase[3] for phase in phases), step, 0)
    for phase in phases:
        phase[2]()


def gather_rows(mesh, src, regions, collective_id):
    depth, width = mesh.shape["dp"] // 4, src.shape[1]
    shapes, scratch = [], []
    for npd, rows, _, ranges, *_ in regions:
        count = max(r[1] - r[0] for r in ranges)
        shapes.append(jax.ShapeDtypeStruct((count * rows, width), src.dtype))
        scratch += [
            pltpu.VMEM((npd, rows, width), src.dtype),
            pltpu.SemaphoreType.DMA((2, npd)),
            pltpu.SemaphoreType.DMA((count,)),
            pltpu.SemaphoreType.DMA((4, count)),
        ]
    return pl.pallas_call(
        functools.partial(gather_body, depth, regions),
        out_shape=shapes,
        in_specs=[ANY],
        out_specs=[ANY] * len(shapes),
        scratch_shapes=scratch,
        compiler_params=pltpu.CompilerParams(collective_id=collective_id, has_side_effects=True),
        cost_estimate=pl.CostEstimate(flops=5 * 10**10, bytes_accessed=2**24, transcendentals=0),
    )(src)


def reduce_region(depth, npd, rows, ranges, swaps, duals, lag, src, out, own, rc, ry, rz, acc, own_sem, rc_sem, ry_sem, rz_sem, send_sem):
    b, me, z, y, c = place()
    (a0, a1), (b0, b1) = ranges
    q0 = jnp.where(b == 0, a0, b0)
    q1 = jnp.where(b == 0, a1, b1)
    swap = jnp.where(b == 0, swaps[0], swaps[1])
    pair0 = q0 // npd // 2
    core_peer, y_peer = (b, me + 1 - 2 * c), (b, me + 2 - 4 * y)
    up, down = (b, jnp.minimum(me + 4, 4 * depth - 1)), (b, jnp.maximum(me - 4, 0))

    def column(j):
        ys = (j // 2) % 2
        return jnp.where(j == swap, 1 - ys, ys)

    def slot(j, i):
        return (j // 2 - pair0) * npd + i

    def part(j, i):
        return src.at[pl.ds(pl.multiple_of((j * npd + i - q0) * rows, 8), rows), :]

    def keep(j, i):
        return pltpu.make_async_copy(part(j, i), own.at[slot(j, i)], own_sem.at[slot(j, i)])

    def remote(kind, frm, to, sem, k, device):
        return pltpu.make_async_remote_copy(
            frm, to, send_sem.at[kind, k], sem, device_id=device, device_id_type=MESH
        )

    def to_core(j, i):
        k = slot(j, i)
        return remote(0, part(j, i), rc.at[k], rc_sem.at[k], k, core_peer)

    def to_y(j, i):
        k = slot(j, i)
        return remote(1, own.at[k], ry.at[k], ry_sem.at[k], k, y_peer)

    def to_z(j, i, way):
        k = slot(j, i)
        return remote(2, own.at[k], rz.at[way, k], rz_sem.at[way, k], k, (up, down)[way])

    def to_owner(j, i):
        k = slot(j, i)
        return remote(2, own.at[k], ry.at[k], ry_sem.at[k], k, y_peer)

    def owners(n, core, what):
        pos, i = n // npd, n % npd
        rising = pos + jnp.where(pos >= z, 1, 0)
        falling = depth - 1 - pos
        falling = falling - jnp.where(falling <= z, 1, 0)
        zs = jnp.where(pos == depth - 1, z, jnp.where(z >= depth // 2, rising, falling))
        for ys in (0, 1):
            j = (zs * 2 + ys) * 2 + core
            q = j * npd + i

            @pl.when(jnp.logical_and(q >= q0, q < q1))
            def _():
                what(j, i, zs, ys)

    total = depth * npd

    def first(n, carry):
        owners(n, 1 - c, lambda j, i, zs, ys: to_core(j, i).start())
        owners(n, c, lambda j, i, zs, ys: keep(j, i).start())
        return carry

    def cross(j, i, zs, ys):
        @pl.when(jnp.logical_and(column(j) != y, jnp.logical_not(listed(j, b, duals))))
        def _():
            k = slot(j, i)
            keep(j, i).wait()
            to_core(j, i).wait_recv()
            own[k] = (own[k].astype(jnp.float32) + rc[k].astype(jnp.float32)).astype(own.dtype)
            to_y(j, i).start()

    def chain(j, i, zs, ys):
        dual = listed(j, b, duals)

        @pl.when(jnp.logical_or(column(j) == y, dual))
        def _():
            k = slot(j, i)
            keep(j, i).wait()
            to_core(j, i).wait_recv()
            acc[...] = own[k].astype(jnp.float32) + rc[k].astype(jnp.float32)

            @pl.when(jnp.logical_or(jnp.logical_not(dual), jnp.logical_and(z == zs, ys == y)))
            def _():
                to_y(j, i).wait_recv()
                acc[...] += ry[k].astype(jnp.float32)

            @pl.when(jnp.logical_and(z >= zs, z < depth - 1))
            def _():
                to_z(j, i, 1).wait_recv()
                acc[...] += rz[1, k].astype(jnp.float32)

            @pl.when(jnp.logical_and(z <= zs, z > 0))
            def _():
                to_z(j, i, 0).wait_recv()
                acc[...] += rz[0, k].astype(jnp.float32)

            @pl.when(jnp.logical_and(z == zs, ys == y))
            def _():
                out[i] = acc[...].astype(out.dtype)

            @pl.when(jnp.logical_not(jnp.logical_and(z == zs, ys == y)))
            def _():
                own[k] = acc[...].astype(own.dtype)

            @pl.when(z > zs)
            def _():
                to_z(j, i, 1).start()

            @pl.when(z < zs)
            def _():
                to_z(j, i, 0).start()

            @pl.when(jnp.logical_and(z == zs, ys != y))
            def _():
                @pl.when(dual)
                def _():
                    to_y(j, i).start()

                @pl.when(jnp.logical_not(dual))
                def _():
                    to_owner(j, i).start()

    def step(s):
        @pl.when(s < total)
        def _():
            owners(s, c, cross)

        @pl.when(jnp.logical_and(s >= lag, s < total + lag))
        def _():
            owners(s - lag, c, chain)

    def sent(j, i, zs, ys):
        dual = listed(j, b, duals)

        @pl.when(jnp.logical_and(column(j) != y, jnp.logical_not(dual)))
        def _():
            to_y(j, i).wait_send()

            @pl.when(me == j)
            def _():
                to_owner(j, i).wait_recv()
                out[i] = ry[slot(j, i)].astype(out.dtype)

        @pl.when(jnp.logical_or(column(j) == y, dual))
        def _():
            @pl.when(z != zs)
            def _():
                to_z(j, i, 0).wait_send()

            @pl.when(jnp.logical_and(z == zs, ys != y))
            def _():
                @pl.when(dual)
                def _():
                    to_y(j, i).wait_send()

                @pl.when(jnp.logical_not(dual))
                def _():
                    to_owner(j, i).wait_send()

    def last(n, carry):
        owners(n, 1 - c, lambda j, i, zs, ys: to_core(j, i).wait_send())
        owners(n, c, sent)
        return carry

    return (
        lambda: lax.fori_loop(0, total, first, 0),
        step,
        lambda: lax.fori_loop(0, total, last, 0),
        total + lag,
    )


def reduce_body(depth, regions, *refs):
    count = len(regions)
    srcs, outs, scratch = refs[:count], refs[count : 2 * count], refs[2 * count :]
    b, me, z, y, c = place()
    meet(depth, b, me, z)
    size = len(scratch) // count
    phases = [
        reduce_region(depth, *region, srcs[r], outs[r], *scratch[size * r : size * (r + 1)]) for r, region in enumerate(regions)
    ]
    for begin, *_ in phases:
        begin()

    def step(s, carry):
        for phase in phases:
            phase[1](s)
        return carry

    lax.fori_loop(0, max(phase[3] for phase in phases), step, 0)
    for phase in phases:
        phase[2]()


def reduce_rows(mesh, srcs, regions, collective_id, dtype, lag=2):
    depth, width = mesh.shape["dp"] // 4, srcs[0].shape[1]
    kind = srcs[0].dtype
    shapes, scratch = [], []
    for npd, rows, ranges, *_ in regions:
        pairs = max((r[1] + npd - 1) // npd // 2 + (r[1] + npd - 1) // npd % 2 - r[0] // npd // 2 for r in ranges)
        held = pairs * npd
        block = (held, rows, width)
        shapes.append(jax.ShapeDtypeStruct((npd, rows, width), dtype))
        scratch += [
            pltpu.VMEM(block, kind),
            pltpu.VMEM(block, kind),
            pltpu.VMEM(block, kind),
            pltpu.VMEM((2, *block), kind),
            pltpu.VMEM((rows, width), jnp.float32),
            pltpu.SemaphoreType.DMA((held,)),
            pltpu.SemaphoreType.DMA((held,)),
            pltpu.SemaphoreType.DMA((held,)),
            pltpu.SemaphoreType.DMA((2, held)),
            pltpu.SemaphoreType.DMA((3, held)),
        ]
    return pl.pallas_call(
        functools.partial(reduce_body, depth, tuple((*region, lag) for region in regions)),
        out_shape=shapes,
        in_specs=[ANY] * len(srcs),
        out_specs=[pl.BlockSpec(memory_space=pltpu.VMEM)] * len(shapes),
        scratch_shapes=scratch,
        compiler_params=pltpu.CompilerParams(
            collective_id=collective_id, has_side_effects=True, vmem_limit_bytes=60 * 2**20
        ),
        cost_estimate=pl.CostEstimate(flops=5 * 10**10, bytes_accessed=2**24, transcendentals=0),
    )(*srcs)
SCALES = (12, 16)
MICRO = 3
GROUPS = 2
EPSILON = 1e-05
BF, F32 = jnp.bfloat16, jnp.float32
MIB = 2**20


def up_to(value, step):
    return (value + step - 1) // step * step


def dot(a, b):
    return jnp.dot(a, b, preferred_element_type=F32)


def dot_bt(a, b):
    return lax.dot_general(a, b, (((1,), (1,)), ((), ())), preferred_element_type=F32)


def dot_at(a, b):
    return lax.dot_general(a, b, (((0,), (0,)), ((), ())), preferred_element_type=F32)


def mean(values):
    return jnp.mean(values, axis=-1, keepdims=True)


def normalise(values):
    centre = values - mean(values)
    rho = lax.rsqrt(mean(centre * centre) + EPSILON)
    return centre * rho, rho


def norm_back(q_gain, xhat, rho):
    return rho * (q_gain - mean(q_gain) - xhat * mean(q_gain * xhat))


def column_sum(values):
    return jnp.sum(values, axis=0, keepdims=True)


VMEM = pl.BlockSpec(memory_space=pltpu.VMEM)


LANES = 128


def panels(ref, lead, rows):
    return jnp.concatenate([ref[(*lead, p, rows, slice(None))] for p in range(ref.shape[-3])], axis=1)


def set_panels(ref, lead, rows, values):
    for p in range(ref.shape[-3]):
        ref[(*lead, p, rows, slice(None))] = values[:, p * LANES : (p + 1) * LANES]


def stride_of(k):
    return k if k % 8 else k + 1


def put_rows(ref, lead, k, values):
    stride = stride_of(k)
    if stride == k:
        set_panels(ref, lead, slice(0, values.shape[0]), values)
        return
    for t in range(values.shape[0] // k):
        set_panels(ref, lead, slice(t * stride, t * stride + k), values[t * k : (t + 1) * k])


def get_rows(ref, lead, k, length):
    stride = stride_of(k)
    if stride == k:
        return panels(ref, lead, slice(0, length))
    return jnp.concatenate([panels(ref, lead, slice(t * stride, t * stride + k)) for t in range(length // k)], axis=0)


def tap_rows(k, r, pitch):
    return pl.ds(r, pitch, stride=stride_of(k))


def at_window(w, pitch):
    return pl.ds(pl.multiple_of(w * pitch, 16), pitch)


def block_of(r, width, off=0):
    return pl.ds(pl.multiple_of(off + r * width, 16), width)


def fit(values, tall):
    rows = values.shape[0]
    if rows >= tall:
        return values[:tall]
    return jnp.concatenate([values, jnp.zeros((tall - rows, values.shape[1]), values.dtype)], axis=0)


def iso_of(n, pitch, pre_iso, bias):
    rows = fit(jnp.tanh(pre_iso + bias[1:2, :]), pitch)
    step = lax.broadcasted_iota(jnp.int32, rows.shape, 0)
    return jnp.where(step < n, rows, 0.0)


def set_iso_rows(n, pitch, live, pre_iso, bias, iso_rows):
    for w in range(pre_iso.shape[0]):
        iso = iso_of(n, pitch, pre_iso[w], bias)
        iso_rows[w * pitch : (w + 1) * pitch, :] = jnp.where(w < live[0], iso, 0.0).astype(BF)


def each_of(count, what):
    def step(at, carry):
        what(at)
        return carry

    lax.fori_loop(0, count, step, 0)


def down_body(k, n, pitch, off, live, x, weight, bias, pre, act, taps, x_held, w_held, t_held, total, spread, x_sem, w_sem, t_sem):
    slots, length, width = x.shape

    def window(w):
        return pltpu.make_async_copy(x.at[w], x_held.at[w], x_sem.at[w])

    def block(r):
        return pltpu.make_async_copy(weight.at[block_of(r, width, off), :], w_held.at[r], w_sem.at[r])

    def out(w):
        rows = at_window(w, pitch)
        return pltpu.make_async_copy(t_held.at[:, rows, :], taps.at[pl.ds(0, k), rows, :], t_sem.at[w])

    each_of(slots, lambda w: window(w).start())
    each_of(k, lambda r: block(r).start())
    used = n * stride_of(k)
    spread[:, used:, :] = jnp.zeros((spread.shape[0], spread.shape[1] - used, LANES), F32)

    def lay(w):
        window(w).wait()
        put_rows(spread, (), k, x_held[w].astype(F32))
        for r in range(k):
            t_held[r, at_window(w, pitch), :] = panels(spread, (), tap_rows(k, r, pitch)).astype(BF)
        out(w).start()

    each_of(slots, lay)
    total[...] = jnp.zeros_like(total)

    def tap(r):
        block(r).wait()
        total[...] += dot(t_held[r], w_held[r])

    each_of(k, tap)
    tall = pre.shape[1]
    for w in range(slots):
        rows = fit(total[w * pitch : (w + 1) * pitch, :] + bias[0:1, :], tall)
        pre[w] = rows
        step = lax.broadcasted_iota(jnp.int32, rows.shape, 0)
        flag = jnp.where(step == tall - 1, jnp.where(w < live[0], 1.0, 0.0), 0.0)
        act[w] = jnp.where(step < n, jnp.tanh(rows), flag).astype(BF)
    each_of(slots, lambda w: out(w).wait())


def up_body(k, n, pitch, off, live, half, pre_iso, weight, x, gain, bias, own, send, x_held, w_held, o_held, iso_rows, spread,
            x_sem, w_sem, o_sem):
    slots, length, width = x.shape

    def window(w):
        return pltpu.make_async_copy(x.at[w], x_held.at[w], x_sem.at[w])

    def block(r):
        return pltpu.make_async_copy(weight.at[block_of(r, width, off), :], w_held.at[r], w_sem.at[r])

    def out(which, m):
        return pltpu.make_async_copy(o_held.at[which, m], (send, own)[which].at[m], o_sem.at[which, m])

    each_of(k, lambda r: block(r).start())
    each_of(slots, lambda w: window(w).start())
    set_iso_rows(n, pitch, live, pre_iso, bias, iso_rows)

    def tap(r):
        block(r).wait()
        rows = dot(iso_rows[...], w_held[r])
        for w in range(slots):
            set_panels(spread, (w,), tap_rows(k, r, pitch), rows[w * pitch : (w + 1) * pitch])

    each_of(k, tap)

    def finish(m):
        for which, w in enumerate((2 * m + 1 - half[0], 2 * m + half[0])):
            window(w).wait()
            values = get_rows(spread, (w,), k, length) + bias[2:3, :] + x_held[w].astype(F32)
            xhat, _ = normalise(values)
            o_held[which, m] = (xhat * gain[0:1, :] + bias[3:4, :]).astype(BF)
            out(which, m).start()

    each_of(slots // 2, finish)
    for which in range(2):
        each_of(slots // 2, lambda m, which=which: out(which, m).wait())


def up_back_body(k, n, pitch, off, live, half, grad_own, grad_arrived, pre_iso, weight, taps, gain, bias, grad_iso, vectors,
                 grad_taps, part, g_held, w_held, t_held, q_held, p_held, iso_rows, total, spread, g_sem, w_sem, t_sem, q_sem, p_sem):
    (half_slots, length, width), slots = grad_own.shape, pre_iso.shape[0]
    many = slots * pitch

    def window(which, m):
        return pltpu.make_async_copy((grad_own, grad_arrived)[which].at[m], g_held.at[which, m], g_sem.at[which, m])

    def block(r):
        return pltpu.make_async_copy(weight.at[block_of(r, width, off), :], w_held.at[r], w_sem.at[r])

    def tap_in(r):
        return pltpu.make_async_copy(taps.at[r, pl.ds(0, many), :], t_held.at[r], t_sem.at[r])

    def tap_out(r):
        return pltpu.make_async_copy(q_held.at[r], grad_taps.at[r, pl.ds(0, many), :], q_sem.at[r])

    def part_out(r):
        return pltpu.make_async_copy(p_held.at[r % 2], part.at[block_of(r, width, off), :], p_sem.at[r % 2])

    for which in range(2):
        each_of(half_slots, lambda m, which=which: window(which, m).start())

    def fetch(r):
        block(r).start()
        tap_in(r).start()

    each_of(k, fetch)
    set_iso_rows(n, pitch, live, pre_iso, bias, iso_rows)
    used = n * stride_of(k)
    spread[:, used:, :] = jnp.zeros((spread.shape[0], spread.shape[1] - used, LANES), F32)

    def lay(m):
        for which, w in enumerate((2 * m + half[0], 2 * m + 1 - half[0])):
            window(which, m).wait()
            put_rows(spread, (), k, g_held[which, m].astype(F32))
            for r in range(k):
                q_held[r, at_window(w, pitch), :] = panels(spread, (), tap_rows(k, r, pitch)).astype(BF)

    each_of(half_slots, lay)
    vectors[...] = jnp.zeros_like(vectors)
    total[...] = jnp.zeros_like(total)

    def tap(r):
        block(r).wait()
        tap_in(r).wait()
        values = dot(iso_rows[...], w_held[r]) + bias[2:3, :] + t_held[r].astype(F32)
        xhat, rho = normalise(values)
        q = q_held[r].astype(F32)
        residual = norm_back(q * gain[0:1, :], xhat, rho).astype(BF)
        q_held[r] = residual
        tap_out(r).start()
        vectors[0:1, :] += column_sum(q * xhat)
        vectors[3:4, :] += column_sum(residual.astype(F32))
        vectors[4:5, :] += column_sum(q)
        total[...] += dot_bt(residual, w_held[r])

        @pl.when(r >= 2)
        def _():
            part_out(r - 2).wait()

        p_held[r % 2] = dot_at(iso_rows[...], residual).astype(BF)
        part_out(r).start()

    each_of(k, tap)
    tall = grad_iso.shape[1]
    for w in range(slots):
        iso = iso_of(n, pitch, pre_iso[w], bias)
        slope = jnp.where(lax.broadcasted_iota(jnp.int32, iso.shape, 0) < n, 1.0 - iso * iso, 0.0)
        back = jnp.where(w < live[0], total[w * pitch : (w + 1) * pitch, :] * slope, 0.0).astype(BF)
        vectors[2:3, :] += column_sum(back.astype(F32))
        grad_iso[w] = fit(back.astype(F32), tall).astype(BF)
    part_out(k - 2).wait()
    part_out(k - 1).wait()
    each_of(k, lambda r: tap_out(r).wait())


def down_back_body(k, n, pitch, off, live, half, grad_act, pre, grad_taps, taps, weight, keep, send, vector, part, g_held, w_held,
                   t_held, p_held, o_held, rows, spread, g_sem, w_sem, t_sem, p_sem, o_sem):
    slots, (half_slots, length, width) = pre.shape[0], keep.shape
    many = slots * pitch

    def block(r):
        return pltpu.make_async_copy(weight.at[block_of(r, width, off), :], w_held.at[r], w_sem.at[r])

    def grad_in(r):
        return pltpu.make_async_copy(grad_taps.at[r, pl.ds(0, many), :], g_held.at[r], g_sem.at[r])

    def tap_in(r):
        return pltpu.make_async_copy(taps.at[r, pl.ds(0, many), :], t_held.at[r], t_sem.at[r])

    def part_out(r):
        return pltpu.make_async_copy(p_held.at[r % 2], part.at[block_of(r, width, off), :], p_sem.at[r % 2])

    def out(which, m):
        return pltpu.make_async_copy(o_held.at[which, m], (send, keep)[which].at[m], o_sem.at[which, m])

    def fetch(r):
        block(r).start()
        grad_in(r).start()
        tap_in(r).start()

    each_of(k, fetch)
    vector[...] = jnp.zeros_like(vector)
    for w in range(slots):
        act = jnp.tanh(fit(pre[w], pitch))
        step = lax.broadcasted_iota(jnp.int32, act.shape, 0)
        back = fit(grad_act[w], pitch) * (1.0 - act * act)
        back = jnp.where(jnp.logical_and(step < n, w < live[0]), back, 0.0).astype(BF)
        vector[...] += column_sum(back.astype(F32))
        rows[w * pitch : (w + 1) * pitch, :] = back

    def tap(r):
        block(r).wait()
        grad_in(r).wait()
        tap_in(r).wait()
        back = dot_bt(rows[...], w_held[r]) + g_held[r].astype(F32)
        for w in range(slots):
            set_panels(spread, (w,), tap_rows(k, r, pitch), back[w * pitch : (w + 1) * pitch])

        @pl.when(r >= 2)
        def _():
            part_out(r - 2).wait()

        p_held[r % 2] = dot_at(t_held[r], rows[...]).astype(BF)
        part_out(r).start()

    each_of(k, tap)

    def finish(m):
        for which, w in enumerate((2 * m + 1 - half[0], 2 * m + half[0])):
            o_held[which, m] = get_rows(spread, (w,), k, length).astype(BF)
            out(which, m).start()

    each_of(half_slots, finish)
    part_out(k - 2).wait()
    part_out(k - 1).wait()
    for which in range(2):
        each_of(half_slots, lambda m, which=which: out(which, m).wait())


SUBLANES = 8


def shifted(ref, start, tall):
    width = ref.shape[1]
    first = pl.multiple_of(start // SUBLANES * SUBLANES, SUBLANES)
    ahead = start % SUBLANES
    tiles = ref[pl.ds(first, tall + SUBLANES), :].reshape(tall // SUBLANES + 1, SUBLANES, width)
    turned = pltpu.roll(tiles, (SUBLANES - ahead) % SUBLANES, 1)
    row = lax.broadcasted_iota(jnp.int32, (tall // SUBLANES, SUBLANES, width), 1)
    return jnp.where(row < SUBLANES - ahead, turned[:-1], turned[1:]).reshape(tall, width).astype(BF)


PACK = 8


def iso_specs(tall, width, pieces):
    def spec(e):
        def at(step, order, count, shift):
            last = jnp.maximum(count[0] - 1, 0) // PACK
            return order[jnp.minimum(step, last) * PACK + e], 0, 0

        return pl.BlockSpec((1, tall, width), at)

    return [spec(e) for e in range(PACK)]


def scatter_out(order, count, slots_ref, sem, out, tall, step, steps):
    def copy(at, e):
        where = jnp.minimum(at * PACK + e, order.shape[0] - 1)
        return pltpu.make_async_copy(
            slots_ref.at[at % 2, e], out.at[order[where]], sem.at[at % 2, e]
        )

    live = pl.cdiv(count[0], PACK)

    @pl.when(step < live)
    def _():
        for e in range(PACK):
            @pl.when(step * PACK + e < count[0])
            def _():
                copy(step, e).start()

    @pl.when(jnp.logical_and(step >= 1, step <= live))
    def _():
        for e in range(PACK):
            @pl.when((step - 1) * PACK + e < count[0])
            def _():
                copy(step - 1, e).wait()

    @pl.when(jnp.logical_and(step == steps - 1, live == steps))
    def _():
        for e in range(PACK):
            @pl.when(step * PACK + e < count[0])
            def _():
                copy(step, e).wait()


def iso_forward_body(tall, pitch, blocks, steps, order, count, shift, *refs):
    acts, (weight, out, buffer, columns, ready, sem) = refs[:PACK], refs[PACK:]
    step = pl.program_id(0)
    width = weight.shape[1]

    @pl.when(step == 0)
    def _():
        buffer[...] = jnp.zeros_like(buffer)
        columns[...] = jnp.zeros_like(columns)

    @pl.when(step * PACK < count[0])
    def _():
        for e in range(PACK):
            buffer[tall : 2 * tall, :] = (jnp.where(step * PACK + e < count[0], acts[e][0].astype(F32), 0.0))
            for m in range(blocks):
                columns[e * pitch : e * pitch + tall, m * width : (m + 1) * width] = shifted(buffer, tall - shift[m], tall)
        total = dot(columns[...], weight[...])
        for e in range(PACK):
            ready[step % 2, e] = total[e * pitch : e * pitch + tall].astype(BF)

    scatter_out(order, count, ready, sem, out, tall, step, steps)


def iso_back_body(tall, pitch, blocks, steps, order, count, shift, *refs):
    acts, grads = refs[:PACK], refs[PACK : 2 * PACK]
    weight, out, kernel_grad, buffer, columns, gathered, ahead, ready, sem = refs[2 * PACK :]
    step = pl.program_id(0)
    width = weight.shape[1]

    @pl.when(step == 0)
    def _():
        buffer[...] = jnp.zeros_like(buffer)
        columns[...] = jnp.zeros_like(columns)
        gathered[...] = jnp.zeros_like(gathered)
        ahead[...] = jnp.zeros_like(ahead)
        kernel_grad[...] = jnp.zeros_like(kernel_grad)

    @pl.when(step * PACK < count[0])
    def _():
        for e in range(PACK):
            alive = step * PACK + e < count[0]
            buffer[tall : 2 * tall, :] = (jnp.where(alive, acts[e][0].astype(F32), 0.0))
            for m in range(blocks):
                columns[e * pitch : e * pitch + tall, m * width : (m + 1) * width] = shifted(buffer, tall - shift[m], tall)
            gathered[e * pitch : e * pitch + tall, :] = jnp.where(alive, grads[e][0].astype(F32), 0.0).astype(BF)
        for m in range(blocks):
            kernel_grad[m * width : (m + 1) * width, :] += dot_at(columns[:, m * width : (m + 1) * width], gathered[...])
        for e in range(PACK):
            alive = step * PACK + e < count[0]
            ahead[:tall, :] = (jnp.where(alive, grads[e][0].astype(F32), 0.0))
            for m in range(blocks):
                columns[e * pitch : e * pitch + tall, m * width : (m + 1) * width] = shifted(ahead, shift[m], tall)
        total = dot_bt(columns[:, :width], weight[:width, :])
        for m in range(1, blocks):
            total += dot_bt(columns[:, m * width : (m + 1) * width], weight[m * width : (m + 1) * width, :])
        for e in range(PACK):
            ready[step % 2, e] = total[e * pitch : e * pitch + tall].astype(BF)

    scatter_out(order, count, ready, sem, out, tall, step, steps)


def iso_call(back, order, count, shift, weight, *windows):
    many, tall, width = windows[0].shape
    blocks = weight.shape[0] // width
    pitch = up_to(tall, 16)
    steps = many // PACK
    held = pl.BlockSpec(weight.shape, lambda step, *_: (0, 0))
    out_shape = [jax.ShapeDtypeStruct((many, tall, width), BF)]
    out_specs = [ANY]
    copies = pltpu.VMEM((2 * tall + SUBLANES, width), F32)
    scratch = [copies, pltpu.VMEM((PACK * pitch, blocks * width), BF)]
    if back:
        out_shape.append(jax.ShapeDtypeStruct(weight.shape, F32))
        out_specs.append(held)
        scratch += [pltpu.VMEM((PACK * pitch, width), BF), copies]
    scratch += [pltpu.VMEM((2, PACK, tall, width), BF), pltpu.SemaphoreType.DMA((2, PACK))]
    body = iso_back_body if back else iso_forward_body
    flops = 2 * many * tall * weight.size * (2 if back else 1) // 3
    return pl.pallas_call(
        functools.partial(body, tall, pitch, blocks, steps),
        out_shape=out_shape,
        grid_spec=pltpu.PrefetchScalarGridSpec(
            num_scalar_prefetch=3,
            grid=(steps,),
            in_specs=[s for _ in windows for s in iso_specs(tall, width, steps)] + [held],
            out_specs=out_specs,
            scratch_shapes=scratch,
        ),
        compiler_params=pltpu.CompilerParams(vmem_limit_bytes=56 * MIB),
        cost_estimate=pl.CostEstimate(flops=flops, bytes_accessed=4 * MIB, transcendentals=0),
    )(order, count, shift, *[v for v in windows for _ in range(PACK)], weight)


def feed_body(per_window, tile, live, own, bo_send, d_out, merge_weight, ff_in, ff_in_bias, ff_out, biases, gains,
              layer_out, grad_own, arrived, merge_grad, in_grad, out_grad, bias_grad, sums,
              slope, hidden_kept, other_slots, grad_slots, merge_sum, in_sum, out_sum, bo_sent, bo_come, back_sent, back_come):
    step, steps = pl.program_id(0), pl.num_programs(0)
    branch, me = lax.axis_index("branch"), lax.axis_index("dp")
    partner = (1 - branch, me)
    block, width = own.shape

    def forth(at):
        return pltpu.make_async_remote_copy(
            bo_send.at[pl.ds(pl.multiple_of(at * block, 8), block), :], other_slots.at[at], bo_sent.at[at], bo_come.at[at],
            device_id=partner, device_id_type=MESH,
        )

    def back_copy(at):
        return pltpu.make_async_remote_copy(
            grad_slots.at[at], arrived.at[pl.ds(pl.multiple_of(at * block, 8), block), :], back_sent.at[at], back_come.at[at],
            device_id=partner, device_id_type=MESH,
        )

    @pl.when(step == 0)
    def _():
        barrier = pltpu.get_barrier_semaphore()
        pl.semaphore_signal(barrier, 1, device_id=partner, device_id_type=MESH)
        pl.semaphore_wait(barrier, 1)
        forth(0).start()
        forth(1).start()
        bias_grad[...] = jnp.zeros_like(bias_grad)
        sums[...] = jnp.zeros_like(sums)
        merge_sum[...] = jnp.zeros_like(merge_sum)
        in_sum[...] = jnp.zeros_like(in_sum)
        out_sum[...] = jnp.zeros_like(out_sum)

    forth(step).wait_recv()

    @pl.when(step + 2 < steps)
    def _():
        forth(step + 2).start()

    alive = jnp.where(2 * (step // per_window) + branch < live[0], 1.0, 0.0)
    own_rows, other_rows = own[...], other_slots[step]
    own_at = pl.ds(pl.multiple_of(branch * width, width), width)
    other_at = pl.ds(pl.multiple_of((1 - branch) * width, width), width)
    merged = dot(own_rows, merge_weight[own_at, :]) + dot(other_rows, merge_weight[other_at, :]) + biases[0:1, :]
    xhat_one, rho_one = normalise(merged)
    normed = (xhat_one * gains[0:1, :] + biases[1:2, :]).astype(BF)
    units = ff_in.shape[1]
    total = merged + biases[2:3, :]
    for u in range(0, units, tile):
        inner = dot(normed, ff_in[:, u : u + tile]) + ff_in_bias[:, u : u + tile]
        phi_total = 0.5 * (1.0 + lax.erf(inner * 0.7071067811865476))
        hidden = (inner * phi_total).astype(BF)
        slope[:, u : u + tile] = phi_total + inner * (jnp.exp(-0.5 * inner * inner) * 0.3989422804014327)
        hidden_kept[:, u : u + tile] = hidden
        total += dot(hidden, ff_out[u : u + tile, :])
    xhat_two, rho_two = normalise(total)
    layer_out[...] = ((xhat_two * gains[1:2, :] + biases[3:4, :]) * alive).astype(BF)
    q = d_out[...].astype(F32) * alive
    grad_sum = norm_back(q * gains[1:2, :], xhat_two, rho_two)
    grad_outer = grad_sum.astype(BF)
    back = jnp.zeros_like(merged)
    for u in range(0, units, tile):
        grad_inner = (dot_bt(grad_outer, ff_out[u : u + tile, :]) * slope[:, u : u + tile]).astype(BF)
        bias_grad[:, u : u + tile] += column_sum(grad_inner.astype(F32))
        back += dot_bt(grad_inner, ff_in[:, u : u + tile])
        in_sum[:, u : u + tile] += dot_at(normed, grad_inner)
        out_sum[u : u + tile, :] += dot_at(hidden_kept[:, u : u + tile], grad_outer)
    grad_merged = (grad_sum + norm_back(back * gains[0:1, :], xhat_one, rho_one)).astype(BF)
    grad_slots[step] = dot_bt(grad_merged, merge_weight[other_at, :]).astype(BF)
    back_copy(step).start()
    grad_own[...] = dot_bt(grad_merged, merge_weight[own_at, :]).astype(BF)
    merge_sum[own_at, :] += dot_at(own_rows, grad_merged)
    merge_sum[other_at, :] += dot_at(other_rows, grad_merged)
    sums[0:1, :] += column_sum(grad_merged.astype(F32))
    sums[1:2, :] += column_sum(back)
    sums[2:3, :] += column_sum(grad_outer.astype(F32))
    sums[3:4, :] += column_sum(q)
    sums[4:5, :] += column_sum(back * xhat_one)
    sums[5:6, :] += column_sum(q * xhat_two)

    @pl.when(step == steps - 1)
    def _():
        merge_grad[...] = merge_sum[...].astype(BF)
        in_grad[...] = in_sum[...].astype(BF)
        out_grad[...] = out_sum[...].astype(BF)

        def finish(at, carry):
            forth(at).wait_send()
            back_copy(at).wait_send()
            back_copy(at).wait_recv()
            return carry

        lax.fori_loop(0, steps, finish, 0)


def feed_call(live, own, bo_send, d_out, merge_weight, ff_in, ff_in_bias, ff_out, biases, gains, per_window, collective_id):
    rows, width = own.shape
    units = ff_in.shape[1]
    steps = MICRO * per_window
    block = rows // steps

    def rowed(columns):
        return pl.BlockSpec((block, columns), lambda step, *_: (step, 0))

    def held(shape):
        return pl.BlockSpec(shape, lambda step, *_: (0, 0), pipeline_mode=pl.Buffered(1))

    def shaped(*shape):
        return jax.ShapeDtypeStruct(shape, BF)

    weights = (merge_weight, ff_in, ff_in_bias, ff_out, biases, gains)
    outs = [(rows, width), (rows, width), (rows, width), merge_weight.shape, ff_in.shape, ff_out.shape]
    return pl.pallas_call(
        functools.partial(feed_body, per_window, 512),
        out_shape=[shaped(*s) for s in outs] + [jax.ShapeDtypeStruct((1, units), F32), jax.ShapeDtypeStruct((8, width), F32)],
        grid_spec=pltpu.PrefetchScalarGridSpec(
            num_scalar_prefetch=1,
            grid=(steps,),
            in_specs=[rowed(width), ANY, rowed(width)] + [held(v.shape) for v in weights],
            out_specs=[rowed(width), rowed(width), ANY] + [held(s) for s in outs[3:]] + [held((1, units)), held((8, width))],
            scratch_shapes=[
                pltpu.VMEM((block, units), F32), pltpu.VMEM((block, units), BF), pltpu.VMEM((steps, block, width), BF),
                pltpu.VMEM((steps, block, width), BF), pltpu.VMEM(merge_weight.shape, F32), pltpu.VMEM(ff_in.shape, F32),
                pltpu.VMEM(ff_out.shape, F32), pltpu.SemaphoreType.DMA((steps,)), pltpu.SemaphoreType.DMA((steps,)),
                pltpu.SemaphoreType.DMA((steps,)), pltpu.SemaphoreType.DMA((steps,)),
            ],
        ),
        compiler_params=pltpu.CompilerParams(vmem_limit_bytes=58 * MIB, collective_id=collective_id, has_side_effects=True),
        cost_estimate=pl.CostEstimate(flops=rows * width * units * 2 * 8, bytes_accessed=40 * MIB, transcendentals=rows * units),
    )(live, own, bo_send, d_out, *weights)


def total_body(depth, values, out, pair, come, far, sent_sem, come_sem, far_sent, far_come):
    b, me, z, y, c = place()
    peers = ((b, me + 1 - 2 * c), (1 - b, me), (b, me + 2 - 4 * y))
    barrier = pltpu.get_barrier_semaphore()
    for peer in peers:
        pl.semaphore_signal(barrier, 1, device_id=peer, device_id_type=MESH)

    def along(what):
        def each(other, carry):
            @pl.when(other != z)
            def _():
                what(other)

            return carry

        lax.fori_loop(0, depth, each, 0)

    def at_row(other):
        return b, me + 4 * (other - z)

    along(lambda other: pl.semaphore_signal(barrier, 1, device_id=at_row(other), device_id_type=MESH))
    pl.semaphore_wait(barrier, len(peers) + depth - 1)
    pair[0] = values[...]
    for step, peer in enumerate(peers):
        copy = pltpu.make_async_remote_copy(
            pair.at[step], come.at[step], sent_sem.at[step], come_sem.at[step], device_id=peer, device_id_type=MESH
        )
        copy.start()
        copy.wait()
        pair[step + 1] = pair[step] + come[step]

    def outward(other):
        return pltpu.make_async_remote_copy(
            pair.at[len(peers)], far.at[z], far_sent.at[other], far_come.at[z], device_id=at_row(other), device_id_type=MESH
        )

    def inward(other):
        return pltpu.make_async_remote_copy(
            pair.at[len(peers)], far.at[other], far_sent.at[other], far_come.at[other], device_id=at_row(other), device_id_type=MESH
        )

    along(lambda other: outward(other).start())
    far[z] = pair[len(peers)]
    along(lambda other: outward(other).wait_send())
    along(lambda other: inward(other).wait_recv())
    out[...] = far[0]

    def add(other, carry):
        out[...] += far[other]
        return carry

    lax.fori_loop(1, depth, add, 0)


def total_over(mesh, values, collective_id):
    depth = mesh.shape["dp"] // 4
    return pl.pallas_call(
        functools.partial(total_body, depth),
        out_shape=jax.ShapeDtypeStruct(values.shape, F32),
        in_specs=[VMEM],
        out_specs=VMEM,
        scratch_shapes=[
            pltpu.VMEM((4, *values.shape), F32), pltpu.VMEM((3, *values.shape), F32), pltpu.VMEM((depth, *values.shape), F32),
            pltpu.SemaphoreType.DMA((3,)), pltpu.SemaphoreType.DMA((3,)), pltpu.SemaphoreType.DMA((depth,)),
            pltpu.SemaphoreType.DMA((depth,)),
        ],
        compiler_params=pltpu.CompilerParams(collective_id=collective_id, has_side_effects=True),
    )(values)


def branch_index_pair(branch, first, second, *operands):
    return lax.cond(branch == 0, first, second, *operands)


def solution(mesh):
    def per_device(inputs, window_count, branch_blocks, branch_gains, branch_biases, merge_weight, ff_in, ff_in_bias, ff_out,
                   shared_biases, shared_gains, d_out):
        members = mesh.shape["dp"]
        branch, me = lax.axis_index("branch"), lax.axis_index("dp")
        slots, length, width = inputs.shape
        group_rows = branch_blocks.shape[2] * members
        share = branch_blocks.shape[2]
        taps_of = [length // k for k in SCALES]
        tall = up_to(max(taps_of) + 1, 8)
        pitches = [up_to(n, 16) for n in taps_of]
        reach = max(SCALES)
        most = slots * max(pitches)
        live = window_count.astype(jnp.int32)
        half = branch.astype(jnp.int32)[None]
        gain, bias = branch_gains, branch_biases[0]

        npd = 8 if share % 64 == 0 else 1
        chunk = share // npd
        down_ranges = tuple((0, -(-k * width // chunk)) for k in SCALES)
        up_starts = [(k + n) * width - group_rows for k, n in zip(SCALES, taps_of)]
        up_ranges = tuple((s // chunk, -(-(s + k * width) // chunk)) for s, k in zip(up_starts, SCALES))
        up_offs = [s - r[0] * chunk for s, r in zip(up_starts, up_ranges)]
        swaps = (-1, 1) if members == 16 else (-1, -1)
        none = ((), ())
        own_rows = branch_blocks.reshape(GROUPS * share, width)
        down_weight, up_weight = gather_rows(
            mesh, own_rows, ((npd, chunk, 0, down_ranges, swaps, none), (npd, chunk, share, up_ranges, (-1, -1), none)), 1
        )

        blocks = (share + width - 1) // width + 1
        k_of = jnp.where(branch == 0, SCALES[0], SCALES[1])
        n_of = jnp.where(branch == 0, taps_of[0], taps_of[1])
        rows_at = jnp.arange(share)
        padded, shifts, insides, lead = [], [], [], []
        for g in range(GROUPS):
            first = g * group_rows + me * share - k_of * width
            inside = jnp.logical_and(first + rows_at >= 0, first + rows_at < n_of * width)
            start = first // width
            shifts.append(jnp.clip(n_of - 1 - start - jnp.arange(blocks), 0, tall))
            lead.append(first - start * width)
            insides.append(inside)
            kept = jnp.where(inside[:, None], own_rows[g * share : (g + 1) * share], 0)
            padded.append(lax.dynamic_update_slice(jnp.zeros((blocks * width, width), BF), kept, (lead[g], 0)))
        iso_weight = jnp.concatenate(padded, axis=0)
        shift = jnp.concatenate(shifts).astype(jnp.int32)

        def windows_shape(kind):
            return jax.ShapeDtypeStruct((slots, tall, width), kind)

        full = jax.ShapeDtypeStruct((slots // 2, length, width), BF)
        taps_shape = jax.ShapeDtypeStruct((reach, most, width), BF)
        part_shape = jax.ShapeDtypeStruct((max(r[1] - r[0] for r in down_ranges) * chunk, width), BF)
        up_part_shape = jax.ShapeDtypeStruct((max(r[1] - r[0] for r in up_ranges) * chunk, width), BF)
        sm = pl.BlockSpec(memory_space=pltpu.SMEM)

        def call(body, index, off, outs, held, kinds, *operands):
            k, n, pitch = SCALES[index], taps_of[index], pitches[index]
            spec = {"s": sm, "v": VMEM, "h": ANY}
            scratch = {
                "w": pltpu.VMEM((k, width, width), BF), "t": pltpu.VMEM((k, slots * pitch, width), BF),
                "x": pltpu.VMEM((slots, length, width), BF), "o": pltpu.VMEM((2, slots // 2, length, width), BF),
                "p": pltpu.VMEM((2, width, width), BF), "i": pltpu.VMEM((slots * pitch, width), BF),
                "f": pltpu.VMEM((slots * pitch, width), F32),
                "1": pltpu.VMEM((width // LANES, pitch * stride_of(k), LANES), F32),
                "6": pltpu.VMEM((slots, width // LANES, pitch * stride_of(k), LANES), F32),
                "K": pltpu.SemaphoreType.DMA((k,)), "S": pltpu.SemaphoreType.DMA((slots,)),
                "H": pltpu.SemaphoreType.DMA((2, slots // 2)), "P": pltpu.SemaphoreType.DMA((2,)),
            }
            return pl.pallas_call(
                functools.partial(body, k, n, pitch, off),
                out_shape=outs,
                in_specs=[spec[s] for s in kinds[: len(operands)]],
                out_specs=tuple(spec[s] for s in kinds[len(operands) :]),
                scratch_shapes=[scratch[s] for s in held],
                compiler_params=pltpu.CompilerParams(vmem_limit_bytes=60 * MIB),
                cost_estimate=pl.CostEstimate(flops=2 * 10**10, bytes_accessed=2**24, transcendentals=0),
            )(*operands)

        def down_of(index):
            def run(*operands):
                return call(down_body, index, 0, (windows_shape(F32), windows_shape(BF), taps_shape), "xwtf1SKS", "shhvvvh",
                            *operands)
            return run

        pre, act, taps = branch_index_pair(branch, down_of(0), down_of(1), live, inputs, down_weight, bias)

        passes = 1 if members <= 32 else slots
        per = slots // passes
        pieces = 2 if per % 2 == 0 else 1

        def spread_windows(values, collective_id):
            flat = values.reshape(slots * tall, width)
            [every] = gather_rows(mesh, flat, ((2, slots * tall // 2, 0, ((0, 2 * members),) * 2, (-1, -1), none),), collective_id)
            return every.reshape(members * slots, tall, width)

        def sum_windows(values, collective_id):
            parts = values.reshape(members, passes, per, tall, width)
            results = [
                reduce_rows(mesh, [parts[:, p].reshape(-1, width)],
                            ((pieces, per * tall // pieces, ((0, pieces * members),) * 2, (-1, -1), none),), collective_id + p, F32)[0]
                for p in range(passes)
            ]
            return jnp.concatenate([r.reshape(per, tall, width) for r in results], axis=0)

        acts = spread_windows(act, 3)
        alive = acts[:, tall - 1, 0] > 0.5
        places = jnp.arange(members * slots)
        rank = jnp.sum(jnp.logical_and(alive[None, :], places[None, :] < places[:, None]).astype(jnp.int32), axis=1)
        order = jnp.sum(
            jnp.where(jnp.logical_and(alive[:, None], rank[:, None] == places[None, :]), places[:, None], 0), axis=0
        ).astype(jnp.int32)
        count = jnp.sum(alive.astype(jnp.int32))[None]
        [terms] = iso_call(False, order, count, shift, iso_weight, acts)
        pre_iso = sum_windows(terms, 16)

        def up_of(index):
            def run(*operands):
                return call(up_body, index, up_offs[index], (full, full), "xwoi6SKH", "ssvhhvvhh", *operands)
            return run

        bo_own, bo_send = branch_index_pair(branch, up_of(0), up_of(1), live, half, pre_iso, up_weight, inputs, gain, bias)
        (layer_out, grad_own, arrived, merge_grad, ff_in_grad, ff_out_grad, bias_grad, sums) = feed_call(
            live, bo_own.reshape(-1, width), bo_send.reshape(-1, width), d_out.reshape(-1, width), merge_weight, ff_in,
            ff_in_bias[None], ff_out, shared_biases, shared_gains, 3, 7,
        )
        wide = lax.psum((merge_grad, ff_in_grad, ff_out_grad), ("branch", "dp"))

        def up_back_of(index):
            def run(*operands):
                return call(up_back_body, index, up_offs[index],
                            (windows_shape(BF), jax.ShapeDtypeStruct((8, width), F32), taps_shape, up_part_shape),
                            "owttpif1HKKKP", "sshhvhhvvvvhh", *operands)
            return run

        grad_iso, vectors, grad_taps, up_part = branch_index_pair(
            branch, up_back_of(0), up_back_of(1), live, half, grad_own.reshape(full.shape), arrived.reshape(full.shape), pre_iso, up_weight, taps, gain, bias
        )
        grads = spread_windows(grad_iso, 4)
        back_terms, kernel_grad = iso_call(True, order, count, shift, iso_weight, acts, grads)
        grad_act = sum_windows(back_terms, 32)
        grad_act, wide = lax.optimization_barrier((grad_act, wide))

        def down_back_of(index):
            def run(*operands):
                return call(down_back_body, index, 0, (full, full, jax.ShapeDtypeStruct((1, width), F32), part_shape),
                            "twtpoi6KKKPH", "ssvvhhhhhvh", *operands)
            return run

        values_keep, values_send, down_vector, down_part = branch_index_pair(
            branch, down_back_of(0), down_back_of(1), live, half, grad_act, pre, grad_taps, taps, down_weight
        )
        vectors = jnp.concatenate([vectors[:1], down_vector, vectors[2:5]], axis=0)
        both = jnp.where((jnp.arange(2) == branch)[:, None, None], vectors[None], 0.0).reshape(10, width)
        pieces_of = bias_grad.shape[1] // width
        small = total_over(mesh, jnp.concatenate([sums, bias_grad.reshape(pieces_of, width), both, jnp.zeros((2, width), F32)]), 8)
        values_send, small = lax.optimization_barrier((values_send, small))
        arrived_values = lax.ppermute(values_send, "branch", [(0, 1), (1, 0)])
        grad_inputs = (values_keep.astype(F32) + arrived_values.astype(F32)).astype(BF)
        own_vectors = lax.dynamic_slice_in_dim(small[8 + pieces_of :], 5 * branch, 5, 0)[None]
        bias_total = small[8 : 8 + pieces_of].reshape(-1)

        up_sum, down_sum = [
            total.reshape(share, width)
            for total in reduce_rows(
                mesh, [up_part, down_part], ((npd, chunk, up_ranges, (-1, -1), none), (npd, chunk, down_ranges, swaps, none)), 5,
                BF, 6,
            )
        ]
        group_grads = []
        for g, side in enumerate((down_sum, up_sum)):
            at = g * group_rows + me * share + rows_at
            low, high = (0, k_of * width) if g == 0 else ((k_of + n_of) * width, (2 * k_of + n_of) * width)
            iso_rows = lax.dynamic_slice(kernel_grad, (g * blocks * width + lead[g], 0), (share, width))
            outside = jnp.where(jnp.logical_and(at >= low, at < high)[:, None], side.astype(F32), 0.0)
            group_grads.append(jnp.where(insides[g][:, None], iso_rows, outside))
        grad_blocks = jnp.stack(group_grads)[None]
        return (
            layer_out.reshape(MICRO, 1, 1, length, width), grad_inputs[:, None, None], grad_blocks,
            own_vectors[:, 0], own_vectors[:, 1:], wide[0].astype(F32), wide[1].astype(F32), bias_total,
            wide[2].astype(F32), small[:4], small[4:6],
        )

    from jax.sharding import PartitionSpec as P

    placed = (P("dp", None, None), P("dp"), P("branch", None, "dp", None), P("branch", None), P("branch", None, None), P(), P(), P(),
              P(), P(), P(), P("dp", "branch", None, None, None))
    return jax.shard_map(
        per_device, mesh=mesh, in_specs=placed,
        out_specs=(P("dp", "branch", None, None, None), P("dp", "branch", None, None, None), P("branch", None, "dp", None),
                   P("branch", None), P("branch", None, None), P(), P(), P(), P(), P(), P()),
        check_vma=False,
    )
```

```python
import functools
import jax, jax.numpy as jnp
from jax import lax
from jax.experimental import pallas as pl
from jax.experimental.pallas import tpu as pltpu

MESH = pl.DeviceIdType.MESH
ANY = pl.BlockSpec(memory_space=pl.ANY)


def place():
    me = lax.axis_index("dp")
    return lax.axis_index("branch"), me, me // 4, (me // 2) % 2, me % 2


def listed(j, b, lists):
    found = jnp.bool_(False)
    for which, owners in enumerate(lists):
        for owner in owners:
            found = jnp.logical_or(found, jnp.logical_and(b == which, j == owner))
    return found


def meet(depth, b, me, z):
    barrier = pltpu.get_barrier_semaphore()
    y, c = (me // 2) % 2, me % 2
    pl.semaphore_signal(barrier, 1, device_id=(b, me + 1 - 2 * c), device_id_type=MESH)
    pl.semaphore_signal(barrier, 1, device_id=(b, me + 2 - 4 * y), device_id_type=MESH)

    @pl.when(z > 0)
    def _():
        pl.semaphore_signal(barrier, 1, device_id=(b, me - 4), device_id_type=MESH)

    @pl.when(z < depth - 1)
    def _():
        pl.semaphore_signal(barrier, 1, device_id=(b, me + 4), device_id_type=MESH)

    count = 2 + jnp.where(z > 0, 1, 0) + jnp.where(z < depth - 1, 1, 0)
    pl.semaphore_wait(barrier, count)


def gather_region(depth, npd, rows, base, ranges, swaps, duals, src, dst, hold, local_sem, recv_sem, send_sem):
    b, me, z, y, c = place()
    (a0, a1), (b0, b1) = ranges
    q0 = jnp.where(b == 0, a0, b0)
    q1 = jnp.where(b == 0, a1, b1)
    swap = jnp.where(b == 0, swaps[0], swaps[1])
    core_peer, y_peer = (b, me + 1 - 2 * c), (b, me + 2 - 4 * y)

    def chunk(ref, index):
        return ref.at[pl.ds(pl.multiple_of(index * rows, 8), rows), :]

    def own(i):
        return src.at[pl.ds(pl.multiple_of(base + i * rows, 8), rows), :]

    def remote(kind, q, device, from_own=False):
        k = q - q0
        return pltpu.make_async_remote_copy(
            own(q - me * npd) if from_own else chunk(dst, k), chunk(dst, k), send_sem.at[kind, k], recv_sem.at[k],
            device_id=device, device_id_type=MESH,
        )

    def each_own(what):
        for i in range(npd):
            q = me * npd + i

            @pl.when(jnp.logical_and(q >= q0, q < q1))
            def _():
                what(q, i)

    def kept(i):
        return hold.at[i, pl.ds(0, rows), :]

    def take(q, i):
        return pltpu.make_async_copy(own(i), kept(i), local_sem.at[0, i])

    def put(q, i):
        return pltpu.make_async_copy(kept(i), chunk(dst, q - q0), local_sem.at[1, i])

    def column(j):
        ys = (j // 2) % 2
        return jnp.where(j == swap, 1 - ys, ys)

    def each(core, what):
        def over(zs, t, s):
            for ys in (y, 1 - y):
                j = (zs * 2 + ys) * 2 + core
                col = column(j)
                i = s - t - jnp.where(ys != col, 1, 0) - jnp.where(y != col, 1, 0)
                i = jnp.where(jnp.logical_and(t == 0, ys == y), s, i)
                q = j * npd + i

                @pl.when(jnp.logical_and(jnp.logical_and(i >= 0, i < npd), jnp.logical_and(q >= q0, q < q1)))
                def _():
                    what(q, j)

        def over_step(s):
            def over_far(t, inner):
                @pl.when(z >= t)
                def _():
                    over(z - t, t, s)

                @pl.when(jnp.logical_and(z + t < depth, t > 0))
                def _():
                    over(z + t, t, s)

                return inner

            lax.fori_loop(0, depth, over_far, 0)

        return over_step

    def sends(q, j, act, from_own=False):
        zs, ys = j // 4, (j // 2) % 2
        col, dual = column(j), listed(j, b, duals)
        chain = y == col
        along = jnp.logical_or(chain, dual)

        @pl.when(jnp.logical_and(along, jnp.logical_and(z >= zs, z < depth - 1)))
        def _():
            act(remote(0, q, (b, me + 4), from_own))

        @pl.when(jnp.logical_and(along, jnp.logical_and(z <= zs, z > 0)))
        def _():
            act(remote(1, q, (b, me - 4), from_own))

        start_here = jnp.logical_and(z == zs, ys != col)

        @pl.when(jnp.logical_and(chain != start_here, jnp.logical_or(jnp.logical_not(dual), me == j)))
        def _():
            act(remote(2, q, y_peer, from_own))

        act(remote(3, q, core_peer, from_own))

    def forward(q, j):
        @pl.when(me == j)
        def _():
            sends(q, j, lambda copy: copy.start(), True)

        @pl.when(me != j)
        def _():
            remote(3, q, core_peer).wait_recv()
            sends(q, j, lambda copy: copy.start())

    def begin():
        each_own(lambda q, i: take(q, i).start())

    def swap_own(q, i):
        take(q, i).wait()
        put(q, i).start()

    work = each(c, forward)

    def finish(q, carry):
        j = q // npd

        @pl.when(c == j % 2)
        def _():
            sends(q, j, lambda copy: copy.wait_send())

        @pl.when(c != j % 2)
        def _():
            remote(3, q, core_peer).wait_recv()

        return carry

    def end():
        each_own(swap_own)
        lax.fori_loop(q0, q1, finish, 0)
        each_own(lambda q, i: put(q, i).wait())

    return begin, work, end, npd + depth + 1


def by_branch(b, regions, run):
    if all(rows[0] == rows[1] for _, rows, *_ in regions):
        run(0)
        return
    for which in range(2):
        pl.when(b == which)(lambda which=which: run(which))


def gather_body(depth, regions, *refs):
    count = len(regions)
    src, dsts, scratch = refs[0], refs[1 : 1 + count], refs[1 + count :]
    b, me, z, y, c = place()
    meet(depth, b, me, z)

    def run(which):
        phases = [
            gather_region(depth, npd, rows[which], *rest, src, dsts[r], *scratch[4 * r : 4 * r + 4])
            for r, (npd, rows, *rest) in enumerate(regions)
        ]
        for begin, *_ in phases:
            begin()

        def step(s, carry):
            for phase in phases:
                phase[1](s)
            return carry

        lax.fori_loop(0, max(phase[3] for phase in phases), step, 0)
        for phase in phases:
            phase[2]()

    by_branch(b, regions, run)


def gather_rows(mesh, src, regions, collective_id):
    depth, width = mesh.shape["dp"] // 4, src.shape[1]
    shapes, scratch = [], []
    for npd, rows, _, ranges, *_ in regions:
        count = max(r[1] - r[0] for r in ranges)
        shapes.append(jax.ShapeDtypeStruct((count * max(rows), width), src.dtype))
        scratch += [
            pltpu.VMEM((npd, max(rows), width), src.dtype),
            pltpu.SemaphoreType.DMA((2, npd)),
            pltpu.SemaphoreType.DMA((count,)),
            pltpu.SemaphoreType.DMA((4, count)),
        ]
    return pl.pallas_call(
        functools.partial(gather_body, depth, regions),
        out_shape=shapes,
        in_specs=[ANY],
        out_specs=[ANY] * len(shapes),
        scratch_shapes=scratch,
        compiler_params=pltpu.CompilerParams(collective_id=collective_id, has_side_effects=True),
        cost_estimate=pl.CostEstimate(flops=5 * 10**10, bytes_accessed=2**24, transcendentals=0),
    )(src)


def reduce_region(depth, npd, rows, ranges, swaps, duals, lag, src, out, own, rc, ry, rz, acc, own_sem, rc_sem, ry_sem, rz_sem, send_sem):
    b, me, z, y, c = place()
    (a0, a1), (b0, b1) = ranges
    q0 = jnp.where(b == 0, a0, b0)
    q1 = jnp.where(b == 0, a1, b1)
    swap = jnp.where(b == 0, swaps[0], swaps[1])
    pair0 = q0 // npd // 2
    core_peer, y_peer = (b, me + 1 - 2 * c), (b, me + 2 - 4 * y)
    up, down = (b, jnp.minimum(me + 4, 4 * depth - 1)), (b, jnp.maximum(me - 4, 0))

    def column(j):
        ys = (j // 2) % 2
        return jnp.where(j == swap, 1 - ys, ys)

    def at(ref, *index):
        return ref.at[(*index, pl.ds(0, rows), slice(None))]

    def slot(j, i):
        return (j // 2 - pair0) * npd + i

    def part(j, i):
        return src.at[pl.ds(pl.multiple_of((j * npd + i - q0) * rows, 8), rows), :]

    def keep(j, i):
        return pltpu.make_async_copy(part(j, i), at(own, slot(j, i)), own_sem.at[slot(j, i)])

    def remote(kind, frm, to, sem, k, device):
        return pltpu.make_async_remote_copy(
            frm, to, send_sem.at[kind, k], sem, device_id=device, device_id_type=MESH
        )

    def to_core(j, i):
        k = slot(j, i)
        return remote(0, part(j, i), at(rc, k), rc_sem.at[k], k, core_peer)

    def to_y(j, i):
        k = slot(j, i)
        return remote(1, at(own, k), at(ry, k), ry_sem.at[k], k, y_peer)

    def to_z(j, i, way):
        k = slot(j, i)
        return remote(2, at(own, k), at(rz, way, k), rz_sem.at[way, k], k, (up, down)[way])

    def to_owner(j, i):
        k = slot(j, i)
        return remote(2, at(own, k), at(ry, k), ry_sem.at[k], k, y_peer)

    def owners(n, core, what):
        pos, i = n // npd, n % npd
        rising = pos + jnp.where(pos >= z, 1, 0)
        falling = depth - 1 - pos
        falling = falling - jnp.where(falling <= z, 1, 0)
        zs = jnp.where(pos == depth - 1, z, jnp.where(z >= depth // 2, rising, falling))
        for ys in (0, 1):
            j = (zs * 2 + ys) * 2 + core
            q = j * npd + i

            @pl.when(jnp.logical_and(q >= q0, q < q1))
            def _():
                what(j, i, zs, ys)

    total = depth * npd

    def first(n, carry):
        owners(n, 1 - c, lambda j, i, zs, ys: to_core(j, i).start())
        owners(n, c, lambda j, i, zs, ys: keep(j, i).start())
        return carry

    def cross(j, i, zs, ys):
        @pl.when(jnp.logical_and(column(j) != y, jnp.logical_not(listed(j, b, duals))))
        def _():
            k = slot(j, i)
            keep(j, i).wait()
            to_core(j, i).wait_recv()
            own[k, :rows] = (own[k, :rows].astype(jnp.float32) + rc[k, :rows].astype(jnp.float32)).astype(own.dtype)
            to_y(j, i).start()

    def chain(j, i, zs, ys):
        dual = listed(j, b, duals)

        @pl.when(jnp.logical_or(column(j) == y, dual))
        def _():
            k = slot(j, i)
            keep(j, i).wait()
            to_core(j, i).wait_recv()
            acc[:rows] = own[k, :rows].astype(jnp.float32) + rc[k, :rows].astype(jnp.float32)

            @pl.when(jnp.logical_or(jnp.logical_not(dual), jnp.logical_and(z == zs, ys == y)))
            def _():
                to_y(j, i).wait_recv()
                acc[:rows] += ry[k, :rows].astype(jnp.float32)

            @pl.when(jnp.logical_and(z >= zs, z < depth - 1))
            def _():
                to_z(j, i, 1).wait_recv()
                acc[:rows] += rz[1, k, :rows].astype(jnp.float32)

            @pl.when(jnp.logical_and(z <= zs, z > 0))
            def _():
                to_z(j, i, 0).wait_recv()
                acc[:rows] += rz[0, k, :rows].astype(jnp.float32)

            @pl.when(jnp.logical_and(z == zs, ys == y))
            def _():
                out[i, :rows] = acc[:rows].astype(out.dtype)

            @pl.when(jnp.logical_not(jnp.logical_and(z == zs, ys == y)))
            def _():
                own[k, :rows] = acc[:rows].astype(own.dtype)

            @pl.when(z > zs)
            def _():
                to_z(j, i, 1).start()

            @pl.when(z < zs)
            def _():
                to_z(j, i, 0).start()

            @pl.when(jnp.logical_and(z == zs, ys != y))
            def _():
                @pl.when(dual)
                def _():
                    to_y(j, i).start()

                @pl.when(jnp.logical_not(dual))
                def _():
                    to_owner(j, i).start()

    def step(s):
        @pl.when(s < total)
        def _():
            owners(s, c, cross)

        @pl.when(jnp.logical_and(s >= lag, s < total + lag))
        def _():
            owners(s - lag, c, chain)

    def sent(j, i, zs, ys):
        dual = listed(j, b, duals)

        @pl.when(jnp.logical_and(column(j) != y, jnp.logical_not(dual)))
        def _():
            to_y(j, i).wait_send()

            @pl.when(me == j)
            def _():
                to_owner(j, i).wait_recv()
                out[i, :rows] = ry[slot(j, i), :rows].astype(out.dtype)

        @pl.when(jnp.logical_or(column(j) == y, dual))
        def _():
            @pl.when(z != zs)
            def _():
                to_z(j, i, 0).wait_send()

            @pl.when(jnp.logical_and(z == zs, ys != y))
            def _():
                @pl.when(dual)
                def _():
                    to_y(j, i).wait_send()

                @pl.when(jnp.logical_not(dual))
                def _():
                    to_owner(j, i).wait_send()

    def last(n, carry):
        owners(n, 1 - c, lambda j, i, zs, ys: to_core(j, i).wait_send())
        owners(n, c, sent)
        return carry

    return (
        lambda: lax.fori_loop(0, total, first, 0),
        step,
        lambda: lax.fori_loop(0, total, last, 0),
        total + lag,
    )


def reduce_body(depth, regions, *refs):
    count = len(regions)
    srcs, outs, scratch = refs[:count], refs[count : 2 * count], refs[2 * count :]
    b, me, z, y, c = place()
    meet(depth, b, me, z)
    size = len(scratch) // count

    def run(which):
        phases = [
            reduce_region(depth, npd, rows[which], *rest, srcs[r], outs[r], *scratch[size * r : size * (r + 1)])
            for r, (npd, rows, *rest) in enumerate(regions)
        ]
        for begin, *_ in phases:
            begin()

        def step(s, carry):
            for phase in phases:
                phase[1](s)
            return carry

        lax.fori_loop(0, max(phase[3] for phase in phases), step, 0)
        for phase in phases:
            phase[2]()

    by_branch(b, regions, run)


def reduce_rows(mesh, srcs, regions, collective_id, dtype, lag=2):
    depth, width = mesh.shape["dp"] // 4, srcs[0].shape[1]
    kind = srcs[0].dtype
    shapes, scratch = [], []
    for npd, rows, ranges, *_ in regions:
        pairs = max((r[1] + npd - 1) // npd // 2 + (r[1] + npd - 1) // npd % 2 - r[0] // npd // 2 for r in ranges)
        held = pairs * npd
        block = (held, max(rows), width)
        shapes.append(jax.ShapeDtypeStruct((npd, max(rows), width), dtype))
        scratch += [
            pltpu.VMEM(block, kind),
            pltpu.VMEM(block, kind),
            pltpu.VMEM(block, kind),
            pltpu.VMEM((2, *block), kind),
            pltpu.VMEM((max(rows), width), jnp.float32),
            pltpu.SemaphoreType.DMA((held,)),
            pltpu.SemaphoreType.DMA((held,)),
            pltpu.SemaphoreType.DMA((held,)),
            pltpu.SemaphoreType.DMA((2, held)),
            pltpu.SemaphoreType.DMA((3, held)),
        ]
    return pl.pallas_call(
        functools.partial(reduce_body, depth, tuple((*region, lag) for region in regions)),
        out_shape=shapes,
        in_specs=[ANY] * len(srcs),
        out_specs=[pl.BlockSpec(memory_space=pltpu.VMEM)] * len(shapes),
        scratch_shapes=scratch,
        compiler_params=pltpu.CompilerParams(
            collective_id=collective_id, has_side_effects=True, vmem_limit_bytes=60 * 2**20
        ),
        cost_estimate=pl.CostEstimate(flops=5 * 10**10, bytes_accessed=2**24, transcendentals=0),
    )(*srcs)
SCALES = (12, 16)
MICRO = 3
GROUPS = 2
EPSILON = 1e-05
BF, F32 = jnp.bfloat16, jnp.float32
MIB = 2**20


def up_to(value, step):
    return (value + step - 1) // step * step


def dot(a, b):
    return jnp.dot(a, b, preferred_element_type=F32)


def dot_bt(a, b):
    return lax.dot_general(a, b, (((1,), (1,)), ((), ())), preferred_element_type=F32)


def dot_at(a, b):
    return lax.dot_general(a, b, (((0,), (0,)), ((), ())), preferred_element_type=F32)


def mean(values):
    return jnp.mean(values, axis=-1, keepdims=True)


def normalise(values):
    centre = values - mean(values)
    rho = lax.rsqrt(mean(centre * centre) + EPSILON)
    return centre * rho, rho


def norm_back(q_gain, xhat, rho):
    return rho * (q_gain - mean(q_gain) - xhat * mean(q_gain * xhat))


def column_sum(values):
    return jnp.sum(values, axis=0, keepdims=True)


VMEM = pl.BlockSpec(memory_space=pltpu.VMEM)


LANES = 128


def panels(ref, lead, rows):
    return jnp.concatenate([ref[(*lead, p, rows, slice(None))] for p in range(ref.shape[-3])], axis=1)


def set_panels(ref, lead, rows, values):
    for p in range(ref.shape[-3]):
        ref[(*lead, p, rows, slice(None))] = values[:, p * LANES : (p + 1) * LANES]


def stride_of(k):
    return k if k % 8 else k + 1


def put_rows(ref, lead, k, values):
    stride = stride_of(k)
    if stride == k:
        set_panels(ref, lead, slice(0, values.shape[0]), values)
        return
    for t in range(values.shape[0] // k):
        set_panels(ref, lead, slice(t * stride, t * stride + k), values[t * k : (t + 1) * k])


def get_rows(ref, lead, k, length):
    stride = stride_of(k)
    if stride == k:
        return panels(ref, lead, slice(0, length))
    return jnp.concatenate([panels(ref, lead, slice(t * stride, t * stride + k)) for t in range(length // k)], axis=0)


def tap_rows(k, r, pitch):
    return pl.ds(r, pitch, stride=stride_of(k))


def at_window(w, pitch):
    return pl.ds(pl.multiple_of(w * pitch, 16), pitch)


def block_of(r, width, off=0):
    return pl.ds(pl.multiple_of(off + r * width, 16), width)


def fit(values, tall):
    rows = values.shape[0]
    if rows >= tall:
        return values[:tall]
    return jnp.concatenate([values, jnp.zeros((tall - rows, values.shape[1]), values.dtype)], axis=0)


def iso_of(n, pitch, pre_iso, bias):
    rows = fit(jnp.tanh(pre_iso + bias[1:2, :]), pitch)
    step = lax.broadcasted_iota(jnp.int32, rows.shape, 0)
    return jnp.where(step < n, rows, 0.0)


def window_of(ref, tall, slots, w):
    per = slots // ref.shape[0]
    return ref[w // per, w % per * tall : (w % per + 1) * tall, :]


def set_iso_rows(n, pitch, tall, slots, live, pre_iso, bias, iso_rows):
    for w in range(slots):
        iso = iso_of(n, pitch, window_of(pre_iso, tall, slots, w), bias)
        iso_rows[w * pitch : (w + 1) * pitch, :] = jnp.where(w < live[0], iso, 0.0).astype(BF)


def each_of(count, what):
    def step(at, carry):
        what(at)
        return carry

    lax.fori_loop(0, count, step, 0)


def down_body(k, n, pitch, tall, off, live, x, weight, bias, pre, act, taps, x_held, w_held, t_held, total, spread, x_sem, w_sem, t_sem):
    slots, length, width = x.shape

    def window(w):
        return pltpu.make_async_copy(x.at[w], x_held.at[w], x_sem.at[w])

    def block(r):
        return pltpu.make_async_copy(weight.at[block_of(r, width, off), :], w_held.at[r], w_sem.at[r])

    def out(w):
        rows = at_window(w, pitch)
        return pltpu.make_async_copy(t_held.at[:, rows, :], taps.at[pl.ds(0, k), rows, :], t_sem.at[w])

    each_of(slots, lambda w: window(w).start())
    each_of(k, lambda r: block(r).start())
    used = n * stride_of(k)
    spread[:, used:, :] = jnp.zeros((spread.shape[0], spread.shape[1] - used, LANES), F32)

    def lay(w):
        window(w).wait()
        put_rows(spread, (), k, x_held[w].astype(F32))
        for r in range(k):
            t_held[r, at_window(w, pitch), :] = panels(spread, (), tap_rows(k, r, pitch)).astype(BF)
        out(w).start()

    each_of(slots, lay)
    total[...] = jnp.zeros_like(total)

    def tap(r):
        block(r).wait()
        total[...] += dot(t_held[r], w_held[r])

    each_of(k, tap)
    for w in range(slots):
        rows = fit(total[w * pitch : (w + 1) * pitch, :] + bias[0:1, :], tall)
        pre[w, :tall] = rows
        step = lax.broadcasted_iota(jnp.int32, rows.shape, 0)
        flag = jnp.where(step == tall - 1, jnp.where(w < live[0], 1.0, 0.0), 0.0)
        act[w * tall : (w + 1) * tall, :] = jnp.where(step < n, jnp.tanh(rows), flag).astype(BF)
    each_of(slots, lambda w: out(w).wait())


def up_body(k, n, pitch, tall, off, live, half, pre_iso, weight, x, gain, bias, own, send, x_held, w_held, o_held, iso_rows, spread,
            x_sem, w_sem, o_sem):
    slots, length, width = x.shape

    def window(w):
        return pltpu.make_async_copy(x.at[w], x_held.at[w], x_sem.at[w])

    def block(r):
        return pltpu.make_async_copy(weight.at[block_of(r, width, off), :], w_held.at[r], w_sem.at[r])

    def out(which, m):
        return pltpu.make_async_copy(o_held.at[which, m], (send, own)[which].at[m], o_sem.at[which, m])

    each_of(k, lambda r: block(r).start())
    each_of(slots, lambda w: window(w).start())
    set_iso_rows(n, pitch, tall, slots, live, pre_iso, bias, iso_rows)

    def tap(r):
        block(r).wait()
        rows = dot(iso_rows[...], w_held[r])
        for w in range(slots):
            set_panels(spread, (w,), tap_rows(k, r, pitch), rows[w * pitch : (w + 1) * pitch])

    each_of(k, tap)

    def finish(m):
        for which, w in enumerate((2 * m + 1 - half[0], 2 * m + half[0])):
            window(w).wait()
            values = get_rows(spread, (w,), k, length) + bias[2:3, :] + x_held[w].astype(F32)
            xhat, _ = normalise(values)
            o_held[which, m] = (xhat * gain[0:1, :] + bias[3:4, :]).astype(BF)
            out(which, m).start()

    each_of(slots // 2, finish)
    for which in range(2):
        each_of(slots // 2, lambda m, which=which: out(which, m).wait())


def up_back_body(k, n, pitch, tall, off, live, half, grad_own, grad_arrived, pre_iso, weight, taps, gain, bias, grad_iso, vectors,
                 grad_taps, part, g_held, w_held, t_held, q_held, p_held, iso_rows, total, spread, g_sem, w_sem, t_sem, q_sem, p_sem):
    (half_slots, length, width), slots = grad_own.shape, 2 * grad_own.shape[0]
    many = slots * pitch

    def window(which, m):
        return pltpu.make_async_copy((grad_own, grad_arrived)[which].at[m], g_held.at[which, m], g_sem.at[which, m])

    def block(r):
        return pltpu.make_async_copy(weight.at[block_of(r, width, off), :], w_held.at[r], w_sem.at[r])

    def tap_in(r):
        return pltpu.make_async_copy(taps.at[r, pl.ds(0, many), :], t_held.at[r], t_sem.at[r])

    def tap_out(r):
        return pltpu.make_async_copy(q_held.at[r], grad_taps.at[r, pl.ds(0, many), :], q_sem.at[r])

    def part_out(r):
        return pltpu.make_async_copy(p_held.at[r % 2], part.at[block_of(r, width, off), :], p_sem.at[r % 2])

    for which in range(2):
        each_of(half_slots, lambda m, which=which: window(which, m).start())

    def fetch(r):
        block(r).start()
        tap_in(r).start()

    each_of(k, fetch)
    set_iso_rows(n, pitch, tall, slots, live, pre_iso, bias, iso_rows)
    used = n * stride_of(k)
    spread[:, used:, :] = jnp.zeros((spread.shape[0], spread.shape[1] - used, LANES), F32)

    def lay(m):
        for which, w in enumerate((2 * m + half[0], 2 * m + 1 - half[0])):
            window(which, m).wait()
            put_rows(spread, (), k, g_held[which, m].astype(F32))
            for r in range(k):
                q_held[r, at_window(w, pitch), :] = panels(spread, (), tap_rows(k, r, pitch)).astype(BF)

    each_of(half_slots, lay)
    vectors[...] = jnp.zeros_like(vectors)
    total[...] = jnp.zeros_like(total)

    def tap(r):
        block(r).wait()
        tap_in(r).wait()
        values = dot(iso_rows[...], w_held[r]) + bias[2:3, :] + t_held[r].astype(F32)
        xhat, rho = normalise(values)
        q = q_held[r].astype(F32)
        residual = norm_back(q * gain[0:1, :], xhat, rho).astype(BF)
        q_held[r] = residual
        tap_out(r).start()
        vectors[0:1, :] += column_sum(q * xhat)
        vectors[3:4, :] += column_sum(residual.astype(F32))
        vectors[4:5, :] += column_sum(q)
        total[...] += dot_bt(residual, w_held[r])

        @pl.when(r >= 2)
        def _():
            part_out(r - 2).wait()

        p_held[r % 2] = dot_at(iso_rows[...], residual).astype(BF)
        part_out(r).start()

    each_of(k, tap)
    for w in range(slots):
        iso = iso_of(n, pitch, window_of(pre_iso, tall, slots, w), bias)
        slope = jnp.where(lax.broadcasted_iota(jnp.int32, iso.shape, 0) < n, 1.0 - iso * iso, 0.0)
        back = jnp.where(w < live[0], total[w * pitch : (w + 1) * pitch, :] * slope, 0.0).astype(BF)
        vectors[2:3, :] += column_sum(back.astype(F32))
        grad_iso[w * tall : (w + 1) * tall, :] = fit(back.astype(F32), tall).astype(BF)
    part_out(k - 2).wait()
    part_out(k - 1).wait()
    each_of(k, lambda r: tap_out(r).wait())


def down_back_body(k, n, pitch, tall, off, live, half, grad_act, pre, grad_taps, taps, weight, keep, send, vector, part, g_held, w_held,
                   t_held, p_held, o_held, rows, spread, g_sem, w_sem, t_sem, p_sem, o_sem):
    slots, (half_slots, length, width) = pre.shape[0], keep.shape
    many = slots * pitch

    def block(r):
        return pltpu.make_async_copy(weight.at[block_of(r, width, off), :], w_held.at[r], w_sem.at[r])

    def grad_in(r):
        return pltpu.make_async_copy(grad_taps.at[r, pl.ds(0, many), :], g_held.at[r], g_sem.at[r])

    def tap_in(r):
        return pltpu.make_async_copy(taps.at[r, pl.ds(0, many), :], t_held.at[r], t_sem.at[r])

    def part_out(r):
        return pltpu.make_async_copy(p_held.at[r % 2], part.at[block_of(r, width, off), :], p_sem.at[r % 2])

    def out(which, m):
        return pltpu.make_async_copy(o_held.at[which, m], (send, keep)[which].at[m], o_sem.at[which, m])

    def fetch(r):
        block(r).start()
        grad_in(r).start()
        tap_in(r).start()

    each_of(k, fetch)
    vector[...] = jnp.zeros_like(vector)
    for w in range(slots):
        act = jnp.tanh(fit(pre[w, :tall], pitch))
        step = lax.broadcasted_iota(jnp.int32, act.shape, 0)
        back = fit(window_of(grad_act, tall, slots, w), pitch) * (1.0 - act * act)
        back = jnp.where(jnp.logical_and(step < n, w < live[0]), back, 0.0).astype(BF)
        vector[...] += column_sum(back.astype(F32))
        rows[w * pitch : (w + 1) * pitch, :] = back

    def tap(r):
        block(r).wait()
        grad_in(r).wait()
        tap_in(r).wait()
        back = dot_bt(rows[...], w_held[r]) + g_held[r].astype(F32)
        for w in range(slots):
            set_panels(spread, (w,), tap_rows(k, r, pitch), back[w * pitch : (w + 1) * pitch])

        @pl.when(r >= 2)
        def _():
            part_out(r - 2).wait()

        p_held[r % 2] = dot_at(t_held[r], rows[...]).astype(BF)
        part_out(r).start()

    each_of(k, tap)

    def finish(m):
        for which, w in enumerate((2 * m + 1 - half[0], 2 * m + half[0])):
            o_held[which, m] = get_rows(spread, (w,), k, length).astype(BF)
            out(which, m).start()

    each_of(half_slots, finish)
    part_out(k - 2).wait()
    part_out(k - 1).wait()
    for which in range(2):
        each_of(half_slots, lambda m, which=which: out(which, m).wait())


SUBLANES = 8


def shifted(ref, start, tall):
    width = ref.shape[1]
    first = pl.multiple_of(start // SUBLANES * SUBLANES, SUBLANES)
    ahead = start % SUBLANES
    tiles = ref[pl.ds(first, tall + SUBLANES), :].reshape(tall // SUBLANES + 1, SUBLANES, width)
    turned = pltpu.roll(tiles, (SUBLANES - ahead) % SUBLANES, 1)
    row = lax.broadcasted_iota(jnp.int32, (tall // SUBLANES, SUBLANES, width), 1)
    return jnp.where(row < SUBLANES - ahead, turned[:-1], turned[1:]).reshape(tall, width).astype(BF)


PACK = 8


def iso_specs(tall, width, pieces):
    def spec(e):
        def at(step, order, count, shift):
            last = jnp.maximum(count[0] - 1, 0) // PACK
            return order[jnp.minimum(step, last) * PACK + e], 0

        return pl.BlockSpec((tall, width), at)

    return [spec(e) for e in range(PACK)]


def scatter_out(order, count, slots_ref, sem, out, tall, step, steps):
    def copy(at, e):
        where = jnp.minimum(at * PACK + e, order.shape[0] - 1)
        return pltpu.make_async_copy(
            slots_ref.at[at % 2, e], out.at[pl.ds(pl.multiple_of(order[where] * tall, SUBLANES), tall), :], sem.at[at % 2, e]
        )

    live = pl.cdiv(count[0], PACK)

    @pl.when(step < live)
    def _():
        for e in range(PACK):
            @pl.when(step * PACK + e < count[0])
            def _():
                copy(step, e).start()

    @pl.when(jnp.logical_and(step >= 1, step <= live))
    def _():
        for e in range(PACK):
            @pl.when((step - 1) * PACK + e < count[0])
            def _():
                copy(step - 1, e).wait()

    @pl.when(jnp.logical_and(step == steps - 1, live == steps))
    def _():
        for e in range(PACK):
            @pl.when(step * PACK + e < count[0])
            def _():
                copy(step, e).wait()


PARTS = 2


def iso_forward_body(tall, pitch, blocks, steps, order, count, shift, *refs):
    acts, (weight, out), rest = refs[:PACK], refs[PACK : PACK + 2], refs[PACK + 2 :]
    buffers, columns, (ready, sem) = rest[:PACK], rest[PACK : PACK + PARTS], rest[PACK + PARTS :]
    step = pl.program_id(0)
    width = weight.shape[1]
    group = PACK // PARTS

    @pl.when(step == 0)
    def _():
        for ref in (*buffers, *columns):
            ref[...] = jnp.zeros_like(ref)

    @pl.when(step * PACK < count[0])
    def _():
        for p in range(PARTS):
            for at in range(group):
                e = p * group + at
                buffers[e][tall : 2 * tall, :] = jnp.where(step * PACK + e < count[0], acts[e][...].astype(F32), 0.0)
                for m in range(blocks):
                    columns[p][at * pitch : at * pitch + tall, m * width : (m + 1) * width] = shifted(
                        buffers[e], tall - shift[m], tall
                    )
            total = dot(columns[p][...], weight[...])
            for at in range(group):
                ready[step % 2, p * group + at] = total[at * pitch : at * pitch + tall].astype(BF)

    scatter_out(order, count, ready, sem, out, tall, step, steps)


def iso_back_body(tall, pitch, blocks, steps, order, count, shift, *refs):
    acts, grads = refs[:PACK], refs[PACK : 2 * PACK]
    (weight, out, kernel_grad), rest = refs[2 * PACK : 2 * PACK + 3], refs[2 * PACK + 3 :]
    buffers, ahead, rest = rest[:PACK], rest[PACK : 2 * PACK], rest[2 * PACK :]
    columns, later, (gathered, ready, sem) = rest[0], rest[1 : 1 + PARTS], rest[1 + PARTS :]
    step = pl.program_id(0)
    width = weight.shape[1]
    group = PACK // PARTS

    @pl.when(step == 0)
    def _():
        for ref in (*buffers, *ahead, columns, *later, gathered, kernel_grad):
            ref[...] = jnp.zeros_like(ref)

    @pl.when(step * PACK < count[0])
    def _():
        for e in range(PACK):
            alive = step * PACK + e < count[0]
            grad = jnp.where(alive, grads[e][...].astype(F32), 0.0)
            ahead[e][:tall, :] = grad
            gathered[e * pitch : e * pitch + tall, :] = grad.astype(BF)
        for p in range(PARTS):
            for at in range(group):
                e = p * group + at
                for m in range(blocks):
                    later[p][at * pitch : at * pitch + tall, m * width : (m + 1) * width] = shifted(ahead[e], shift[m], tall)
            total = dot_bt(later[p][:, :width], weight[:width, :])
            for m in range(1, blocks):
                total += dot_bt(later[p][:, m * width : (m + 1) * width], weight[m * width : (m + 1) * width, :])
            for at in range(group):
                ready[step % 2, p * group + at] = total[at * pitch : at * pitch + tall].astype(BF)
        for e in range(PACK):
            alive = step * PACK + e < count[0]
            buffers[e][tall : 2 * tall, :] = jnp.where(alive, acts[e][...].astype(F32), 0.0)
        for m in range(blocks):
            for e in range(PACK):
                columns[e * pitch : e * pitch + tall, m * width : (m + 1) * width] = shifted(buffers[e], tall - shift[m], tall)
            kernel_grad[m * width : (m + 1) * width, :] += dot_at(columns[:, m * width : (m + 1) * width], gathered[...])

    scatter_out(order, count, ready, sem, out, tall, step, steps)


def iso_call(back, tall, order, count, shift, weight, *windows):
    many, (rows, width) = order.shape[0], windows[0].shape
    blocks = weight.shape[0] // width
    pitch = up_to(tall, 16)
    steps = many // PACK
    held = pl.BlockSpec(weight.shape, lambda step, *_: (0, 0))
    out_shape = [jax.ShapeDtypeStruct((rows, width), BF)]
    out_specs = [ANY]
    copies = [pltpu.VMEM((2 * tall + SUBLANES, width), F32)] * PACK
    halves = [pltpu.VMEM((PACK // PARTS * pitch, blocks * width), BF)] * PARTS
    if back:
        out_shape.append(jax.ShapeDtypeStruct(weight.shape, F32))
        out_specs.append(held)
        scratch = [*copies, *copies, pltpu.VMEM((PACK * pitch, blocks * width), BF), *halves, pltpu.VMEM((PACK * pitch, width), BF)]
    else:
        scratch = [*copies, *halves]
    scratch += [pltpu.VMEM((2, PACK, tall, width), BF), pltpu.SemaphoreType.DMA((2, PACK))]
    body = iso_back_body if back else iso_forward_body
    flops = 2 * many * tall * weight.size * (2 if back else 1) // 3
    return pl.pallas_call(
        functools.partial(body, tall, pitch, blocks, steps),
        out_shape=out_shape,
        grid_spec=pltpu.PrefetchScalarGridSpec(
            num_scalar_prefetch=3,
            grid=(steps,),
            in_specs=[s for _ in windows for s in iso_specs(tall, width, steps)] + [held],
            out_specs=out_specs,
            scratch_shapes=scratch,
        ),
        compiler_params=pltpu.CompilerParams(vmem_limit_bytes=56 * MIB),
        cost_estimate=pl.CostEstimate(flops=flops, bytes_accessed=4 * MIB, transcendentals=0),
    )(order, count, shift, *[v for v in windows for _ in range(PACK)], weight)


def feed_body(per_window, tile, live, own, bo_send, d_out, merge_weight, ff_in, ff_in_bias, ff_out, biases, gains,
              layer_out, grad_own, arrived, merge_grad, in_grad, out_grad, bias_grad, sums,
              slope, hidden_kept, other_slots, grad_slots, merge_sum, in_sum, out_sum, bo_sent, bo_come, back_sent, back_come):
    step, steps = pl.program_id(0), pl.num_programs(0)
    branch, me = lax.axis_index("branch"), lax.axis_index("dp")
    partner = (1 - branch, me)
    block, width = own.shape

    def forth(at):
        return pltpu.make_async_remote_copy(
            bo_send.at[pl.ds(pl.multiple_of(at * block, 8), block), :], other_slots.at[at], bo_sent.at[at], bo_come.at[at],
            device_id=partner, device_id_type=MESH,
        )

    def back_copy(at):
        return pltpu.make_async_remote_copy(
            grad_slots.at[at], arrived.at[pl.ds(pl.multiple_of(at * block, 8), block), :], back_sent.at[at], back_come.at[at],
            device_id=partner, device_id_type=MESH,
        )

    @pl.when(step == 0)
    def _():
        barrier = pltpu.get_barrier_semaphore()
        pl.semaphore_signal(barrier, 1, device_id=partner, device_id_type=MESH)
        pl.semaphore_wait(barrier, 1)
        forth(0).start()
        forth(1).start()
        bias_grad[...] = jnp.zeros_like(bias_grad)
        sums[...] = jnp.zeros_like(sums)
        merge_sum[...] = jnp.zeros_like(merge_sum)
        in_sum[...] = jnp.zeros_like(in_sum)
        out_sum[...] = jnp.zeros_like(out_sum)

    forth(step).wait_recv()

    @pl.when(step + 2 < steps)
    def _():
        forth(step + 2).start()

    alive = jnp.where(2 * (step // per_window) + branch < live[0], 1.0, 0.0)
    own_rows, other_rows = own[...], other_slots[step]
    own_at = pl.ds(pl.multiple_of(branch * width, width), width)
    other_at = pl.ds(pl.multiple_of((1 - branch) * width, width), width)
    merged = dot(own_rows, merge_weight[own_at, :]) + dot(other_rows, merge_weight[other_at, :]) + biases[0:1, :]
    xhat_one, rho_one = normalise(merged)
    normed = (xhat_one * gains[0:1, :] + biases[1:2, :]).astype(BF)
    units = ff_in.shape[1]
    total = merged + biases[2:3, :]
    for u in range(0, units, tile):
        inner = dot(normed, ff_in[:, u : u + tile]) + ff_in_bias[:, u : u + tile]
        phi_total = 0.5 * (1.0 + lax.erf(inner * 0.7071067811865476))
        hidden = (inner * phi_total).astype(BF)
        slope[:, u : u + tile] = phi_total + inner * (jnp.exp(-0.5 * inner * inner) * 0.3989422804014327)
        hidden_kept[:, u : u + tile] = hidden
        total += dot(hidden, ff_out[u : u + tile, :])
    xhat_two, rho_two = normalise(total)
    layer_out[...] = ((xhat_two * gains[1:2, :] + biases[3:4, :]) * alive).astype(BF)
    q = d_out[...].astype(F32) * alive
    grad_sum = norm_back(q * gains[1:2, :], xhat_two, rho_two)
    grad_outer = grad_sum.astype(BF)
    back = jnp.zeros_like(merged)
    for u in range(0, units, tile):
        grad_inner = (dot_bt(grad_outer, ff_out[u : u + tile, :]) * slope[:, u : u + tile]).astype(BF)
        bias_grad[:, u : u + tile] += column_sum(grad_inner.astype(F32))
        back += dot_bt(grad_inner, ff_in[:, u : u + tile])
        in_sum[:, u : u + tile] += dot_at(normed, grad_inner)
        out_sum[u : u + tile, :] += dot_at(hidden_kept[:, u : u + tile], grad_outer)
    grad_merged = (grad_sum + norm_back(back * gains[0:1, :], xhat_one, rho_one)).astype(BF)
    grad_slots[step] = dot_bt(grad_merged, merge_weight[other_at, :]).astype(BF)
    back_copy(step).start()
    grad_own[...] = dot_bt(grad_merged, merge_weight[own_at, :]).astype(BF)
    merge_sum[own_at, :] += dot_at(own_rows, grad_merged)
    merge_sum[other_at, :] += dot_at(other_rows, grad_merged)
    sums[0:1, :] += column_sum(grad_merged.astype(F32))
    sums[1:2, :] += column_sum(back)
    sums[2:3, :] += column_sum(grad_outer.astype(F32))
    sums[3:4, :] += column_sum(q)
    sums[4:5, :] += column_sum(back * xhat_one)
    sums[5:6, :] += column_sum(q * xhat_two)

    @pl.when(step == steps - 1)
    def _():
        merge_grad[...] = merge_sum[...].astype(BF)
        in_grad[...] = in_sum[...].astype(BF)
        out_grad[...] = out_sum[...].astype(BF)

        def finish(at, carry):
            forth(at).wait_send()
            back_copy(at).wait_send()
            back_copy(at).wait_recv()
            return carry

        lax.fori_loop(0, steps, finish, 0)


def feed_call(live, own, bo_send, d_out, merge_weight, ff_in, ff_in_bias, ff_out, biases, gains, per_window, collective_id):
    rows, width = own.shape
    units = ff_in.shape[1]
    steps = MICRO * per_window
    block = rows // steps

    def rowed(columns):
        return pl.BlockSpec((block, columns), lambda step, *_: (step, 0))

    def held(shape):
        return pl.BlockSpec(shape, lambda step, *_: (0, 0), pipeline_mode=pl.Buffered(1))

    def shaped(*shape):
        return jax.ShapeDtypeStruct(shape, BF)

    weights = (merge_weight, ff_in, ff_in_bias, ff_out, biases, gains)
    outs = [(rows, width), (rows, width), (rows, width), merge_weight.shape, ff_in.shape, ff_out.shape]
    return pl.pallas_call(
        functools.partial(feed_body, per_window, 512),
        out_shape=[shaped(*s) for s in outs] + [jax.ShapeDtypeStruct((1, units), F32), jax.ShapeDtypeStruct((8, width), F32)],
        grid_spec=pltpu.PrefetchScalarGridSpec(
            num_scalar_prefetch=1,
            grid=(steps,),
            in_specs=[rowed(width), ANY, rowed(width)] + [held(v.shape) for v in weights],
            out_specs=[rowed(width), rowed(width), ANY] + [held(s) for s in outs[3:]] + [held((1, units)), held((8, width))],
            scratch_shapes=[
                pltpu.VMEM((block, units), F32), pltpu.VMEM((block, units), BF), pltpu.VMEM((steps, block, width), BF),
                pltpu.VMEM((steps, block, width), BF), pltpu.VMEM(merge_weight.shape, F32), pltpu.VMEM(ff_in.shape, F32),
                pltpu.VMEM(ff_out.shape, F32), pltpu.SemaphoreType.DMA((steps,)), pltpu.SemaphoreType.DMA((steps,)),
                pltpu.SemaphoreType.DMA((steps,)), pltpu.SemaphoreType.DMA((steps,)),
            ],
        ),
        compiler_params=pltpu.CompilerParams(vmem_limit_bytes=58 * MIB, collective_id=collective_id, has_side_effects=True),
        cost_estimate=pl.CostEstimate(flops=rows * width * units * 2 * 8, bytes_accessed=40 * MIB, transcendentals=rows * units),
    )(live, own, bo_send, d_out, *weights)


def total_body(depth, values, out, pair, come, far, sent_sem, come_sem, far_sent, far_come):
    b, me, z, y, c = place()
    peers = ((b, me + 1 - 2 * c), (1 - b, me), (b, me + 2 - 4 * y))
    barrier = pltpu.get_barrier_semaphore()
    for peer in peers:
        pl.semaphore_signal(barrier, 1, device_id=peer, device_id_type=MESH)

    def along(what):
        def each(other, carry):
            @pl.when(other != z)
            def _():
                what(other)

            return carry

        lax.fori_loop(0, depth, each, 0)

    def at_row(other):
        return b, me + 4 * (other - z)

    along(lambda other: pl.semaphore_signal(barrier, 1, device_id=at_row(other), device_id_type=MESH))
    pl.semaphore_wait(barrier, len(peers) + depth - 1)
    pair[0] = values[...]
    for step, peer in enumerate(peers):
        copy = pltpu.make_async_remote_copy(
            pair.at[step], come.at[step], sent_sem.at[step], come_sem.at[step], device_id=peer, device_id_type=MESH
        )
        copy.start()
        copy.wait()
        pair[step + 1] = pair[step] + come[step]

    def outward(other):
        return pltpu.make_async_remote_copy(
            pair.at[len(peers)], far.at[z], far_sent.at[other], far_come.at[z], device_id=at_row(other), device_id_type=MESH
        )

    def inward(other):
        return pltpu.make_async_remote_copy(
            pair.at[len(peers)], far.at[other], far_sent.at[other], far_come.at[other], device_id=at_row(other), device_id_type=MESH
        )

    along(lambda other: outward(other).start())
    far[z] = pair[len(peers)]
    along(lambda other: outward(other).wait_send())
    along(lambda other: inward(other).wait_recv())
    out[...] = far[0]

    def add(other, carry):
        out[...] += far[other]
        return carry

    lax.fori_loop(1, depth, add, 0)


def total_over(mesh, values, collective_id):
    depth = mesh.shape["dp"] // 4
    return pl.pallas_call(
        functools.partial(total_body, depth),
        out_shape=jax.ShapeDtypeStruct(values.shape, F32),
        in_specs=[VMEM],
        out_specs=VMEM,
        scratch_shapes=[
            pltpu.VMEM((4, *values.shape), F32), pltpu.VMEM((3, *values.shape), F32), pltpu.VMEM((depth, *values.shape), F32),
            pltpu.SemaphoreType.DMA((3,)), pltpu.SemaphoreType.DMA((3,)), pltpu.SemaphoreType.DMA((depth,)),
            pltpu.SemaphoreType.DMA((depth,)),
        ],
        compiler_params=pltpu.CompilerParams(collective_id=collective_id, has_side_effects=True),
    )(values)


def branch_index_pair(branch, first, second, *operands):
    return lax.cond(branch == 0, first, second, *operands)


def solution(mesh):
    def per_device(inputs, window_count, branch_blocks, branch_gains, branch_biases, merge_weight, ff_in, ff_in_bias, ff_out,
                   shared_biases, shared_gains, d_out):
        members = mesh.shape["dp"]
        branch, me = lax.axis_index("branch"), lax.axis_index("dp")
        slots, length, width = inputs.shape
        group_rows = branch_blocks.shape[2] * members
        share = branch_blocks.shape[2]
        taps_of = [length // k for k in SCALES]
        members = mesh.shape["dp"]
        tall = up_to(max(taps_of) + 1, 8)
        talls = [up_to(n + 1, 8) if members <= 32 else tall for n in taps_of]
        pitches = [up_to(n, 16) for n in taps_of]
        reach = max(SCALES)
        most = slots * max(pitches)
        live = window_count.astype(jnp.int32)
        half = branch.astype(jnp.int32)[None]
        gain, bias = branch_gains, branch_biases[0]

        npd = 8 if share % 64 == 0 else 1
        chunk = share // npd
        down_ranges = tuple((0, -(-k * width // chunk)) for k in SCALES)
        up_starts = [(k + n) * width - group_rows for k, n in zip(SCALES, taps_of)]
        up_ranges = tuple((s // chunk, -(-(s + k * width) // chunk)) for s, k in zip(up_starts, SCALES))
        up_offs = [s - r[0] * chunk for s, r in zip(up_starts, up_ranges)]
        swaps = (-1, 1) if members == 16 else (-1, -1)
        none = ((), ())
        own_rows = branch_blocks.reshape(GROUPS * share, width)
        down_weight, up_weight = gather_rows(
            mesh, own_rows, ((npd, (chunk, chunk), 0, down_ranges, swaps, none), (npd, (chunk, chunk), share, up_ranges, (-1, -1), none)), 1
        )

        blocks = (share + width - 1) // width + 1
        k_of = jnp.where(branch == 0, SCALES[0], SCALES[1])
        n_of = jnp.where(branch == 0, taps_of[0], taps_of[1])
        rows_at = jnp.arange(share)
        padded, shifts, insides, lead = [], [], [], []
        for g in range(GROUPS):
            first = g * group_rows + me * share - k_of * width
            inside = jnp.logical_and(first + rows_at >= 0, first + rows_at < n_of * width)
            start = first // width
            shifts.append(jnp.clip(n_of - 1 - start - jnp.arange(blocks), 0, jnp.where(branch == 0, talls[0], talls[1])))
            lead.append(first - start * width)
            insides.append(inside)
            kept = jnp.where(inside[:, None], own_rows[g * share : (g + 1) * share], 0)
            padded.append(lax.dynamic_update_slice(jnp.zeros((blocks * width, width), BF), kept, (lead[g], 0)))
        iso_weight = jnp.concatenate(padded, axis=0)
        shift = jnp.concatenate(shifts).astype(jnp.int32)

        def windows_shape(kind):
            return jax.ShapeDtypeStruct((slots, tall, width), kind)

        flat_shape = jax.ShapeDtypeStruct((slots * tall, width), BF)
        full = jax.ShapeDtypeStruct((slots // 2, length, width), BF)
        taps_shape = jax.ShapeDtypeStruct((reach, most, width), BF)
        part_shape = jax.ShapeDtypeStruct((max(r[1] - r[0] for r in down_ranges) * chunk, width), BF)
        up_part_shape = jax.ShapeDtypeStruct((max(r[1] - r[0] for r in up_ranges) * chunk, width), BF)
        sm = pl.BlockSpec(memory_space=pltpu.SMEM)

        def call(body, index, off, outs, held, kinds, *operands):
            k, n, pitch = SCALES[index], taps_of[index], pitches[index]
            spec = {"s": sm, "v": VMEM, "h": ANY}
            scratch = {
                "w": pltpu.VMEM((k, width, width), BF), "t": pltpu.VMEM((k, slots * pitch, width), BF),
                "x": pltpu.VMEM((slots, length, width), BF), "o": pltpu.VMEM((2, slots // 2, length, width), BF),
                "p": pltpu.VMEM((2, width, width), BF), "i": pltpu.VMEM((slots * pitch, width), BF),
                "f": pltpu.VMEM((slots * pitch, width), F32),
                "1": pltpu.VMEM((width // LANES, pitch * stride_of(k), LANES), F32),
                "6": pltpu.VMEM((slots, width // LANES, pitch * stride_of(k), LANES), F32),
                "K": pltpu.SemaphoreType.DMA((k,)), "S": pltpu.SemaphoreType.DMA((slots,)),
                "H": pltpu.SemaphoreType.DMA((2, slots // 2)), "P": pltpu.SemaphoreType.DMA((2,)),
            }
            return pl.pallas_call(
                functools.partial(body, k, n, pitch, talls[index], off),
                out_shape=outs,
                in_specs=[spec[s] for s in kinds[: len(operands)]],
                out_specs=tuple(spec[s] for s in kinds[len(operands) :]),
                scratch_shapes=[scratch[s] for s in held],
                compiler_params=pltpu.CompilerParams(vmem_limit_bytes=60 * MIB),
                cost_estimate=pl.CostEstimate(flops=2 * 10**10, bytes_accessed=2**24, transcendentals=0),
            )(*operands)

        def down_of(index):
            def run(*operands):
                return call(down_body, index, 0, (windows_shape(F32), flat_shape, taps_shape), "xwtf1SKS", "shhvvvh",
                            *operands)
            return run

        pre, act, taps = branch_index_pair(branch, down_of(0), down_of(1), live, inputs, down_weight, bias)

        passes = 1 if members <= 32 else slots
        per = slots // passes
        pieces = 2 if per % 2 == 0 else 1

        def spread_windows(values, collective_id):
            rows = tuple(slots * t // 2 for t in talls)
            [every] = gather_rows(mesh, values, ((2, rows, 0, ((0, 2 * members),) * 2, (-1, -1), none),), collective_id)
            return every

        def sum_windows(values, collective_id):
            rows = tuple(per * t // pieces for t in talls)
            parts = values.reshape(members, passes, per * tall, width)
            results = [
                reduce_rows(mesh, [parts[:, p].reshape(-1, width)],
                            ((pieces, rows, ((0, pieces * members),) * 2, (-1, -1), none),), collective_id + p, F32)[0]
                for p in range(passes)
            ]
            return jnp.concatenate(results, axis=0)

        def iso_of_branch(back):
            return [lambda *operands, t=t: iso_call(back, t, *operands) for t in talls]

        acts = spread_windows(act, 3)
        flags = [acts[t - 1 : members * slots * t : t, 0] for t in talls]
        alive = jnp.where(branch == 0, flags[0], flags[1]) > 0.5
        places = jnp.arange(members * slots)
        rank = jnp.sum(jnp.logical_and(alive[None, :], places[None, :] < places[:, None]).astype(jnp.int32), axis=1)
        order = jnp.sum(
            jnp.where(jnp.logical_and(alive[:, None], rank[:, None] == places[None, :]), places[:, None], 0), axis=0
        ).astype(jnp.int32)
        count = jnp.sum(alive.astype(jnp.int32))[None]
        [terms] = branch_index_pair(branch, *iso_of_branch(False), order, count, shift, iso_weight, acts)
        pre_iso = sum_windows(terms, 16)

        def up_of(index):
            def run(*operands):
                return call(up_body, index, up_offs[index], (full, full), "xwoi6SKH", "ssvhhvvhh", *operands)
            return run

        bo_own, bo_send = branch_index_pair(branch, up_of(0), up_of(1), live, half, pre_iso, up_weight, inputs, gain, bias)
        (layer_out, grad_own, arrived, merge_grad, ff_in_grad, ff_out_grad, bias_grad, sums) = feed_call(
            live, bo_own.reshape(-1, width), bo_send.reshape(-1, width), d_out.reshape(-1, width), merge_weight, ff_in,
            ff_in_bias[None], ff_out, shared_biases, shared_gains, 3, 7,
        )
        wide = lax.psum((merge_grad, ff_in_grad, ff_out_grad), ("branch", "dp"))

        def up_back_of(index):
            def run(*operands):
                return call(up_back_body, index, up_offs[index],
                            (flat_shape, jax.ShapeDtypeStruct((8, width), F32), taps_shape, up_part_shape),
                            "owttpif1HKKKP", "sshhvhhvvvvhh", *operands)
            return run

        grad_iso, vectors, grad_taps, up_part = branch_index_pair(
            branch, up_back_of(0), up_back_of(1), live, half, grad_own.reshape(full.shape), arrived.reshape(full.shape), pre_iso, up_weight, taps, gain, bias
        )
        grads = spread_windows(grad_iso, 4)
        back_terms, kernel_grad = branch_index_pair(branch, *iso_of_branch(True), order, count, shift, iso_weight, acts, grads)
        grad_act = sum_windows(back_terms, 32)
        grad_act, wide = lax.optimization_barrier((grad_act, wide))

        def down_back_of(index):
            def run(*operands):
                return call(down_back_body, index, 0, (full, full, jax.ShapeDtypeStruct((1, width), F32), part_shape),
                            "twtpoi6KKKPH", "ssvvhhhhhvh", *operands)
            return run

        values_keep, values_send, down_vector, down_part = branch_index_pair(
            branch, down_back_of(0), down_back_of(1), live, half, grad_act, pre, grad_taps, taps, down_weight
        )
        vectors = jnp.concatenate([vectors[:1], down_vector, vectors[2:5]], axis=0)
        both = jnp.where((jnp.arange(2) == branch)[:, None, None], vectors[None], 0.0).reshape(10, width)
        pieces_of = bias_grad.shape[1] // width
        small = total_over(mesh, jnp.concatenate([sums, bias_grad.reshape(pieces_of, width), both, jnp.zeros((2, width), F32)]), 8)
        values_send, small = lax.optimization_barrier((values_send, small))
        arrived_values = lax.ppermute(values_send, "branch", [(0, 1), (1, 0)])
        grad_inputs = (values_keep.astype(F32) + arrived_values.astype(F32)).astype(BF)
        own_vectors = lax.dynamic_slice_in_dim(small[8 + pieces_of :], 5 * branch, 5, 0)[None]
        bias_total = small[8 : 8 + pieces_of].reshape(-1)

        up_sum, down_sum = [
            total.reshape(share, width)
            for total in reduce_rows(
                mesh, [up_part, down_part], ((npd, (chunk, chunk), up_ranges, (-1, -1), none), (npd, (chunk, chunk), down_ranges, swaps, none)), 5,
                BF, 6,
            )
        ]
        group_grads = []
        for g, side in enumerate((down_sum, up_sum)):
            at = g * group_rows + me * share + rows_at
            low, high = (0, k_of * width) if g == 0 else ((k_of + n_of) * width, (2 * k_of + n_of) * width)
            iso_rows = lax.dynamic_slice(kernel_grad, (g * blocks * width + lead[g], 0), (share, width))
            outside = jnp.where(jnp.logical_and(at >= low, at < high)[:, None], side.astype(F32), 0.0)
            group_grads.append(jnp.where(insides[g][:, None], iso_rows, outside))
        grad_blocks = jnp.stack(group_grads)[None]
        return (
            layer_out.reshape(MICRO, 1, 1, length, width), grad_inputs[:, None, None], grad_blocks,
            own_vectors[:, 0], own_vectors[:, 1:], wide[0].astype(F32), wide[1].astype(F32), bias_total,
            wide[2].astype(F32), small[:4], small[4:6],
        )

    from jax.sharding import PartitionSpec as P

    placed = (P("dp", None, None), P("dp"), P("branch", None, "dp", None), P("branch", None), P("branch", None, None), P(), P(), P(),
              P(), P(), P(), P("dp", "branch", None, None, None))
    return jax.shard_map(
        per_device, mesh=mesh, in_specs=placed,
        out_specs=(P("dp", "branch", None, None, None), P("dp", "branch", None, None, None), P("branch", None, "dp", None),
                   P("branch", None), P("branch", None, None), P(), P(), P(), P(), P(), P()),
        check_vma=False,
    )
```

```python
import functools
import jax, jax.numpy as jnp
from jax import lax
from jax.experimental import pallas as pl
from jax.experimental.pallas import tpu as pltpu

MESH = pl.DeviceIdType.MESH
ANY = pl.BlockSpec(memory_space=pl.ANY)


def place():
    me = lax.axis_index("dp")
    return lax.axis_index("branch"), me, me // 4, (me // 2) % 2, me % 2


def listed(j, b, lists):
    found = jnp.bool_(False)
    for which, owners in enumerate(lists):
        for owner in owners:
            found = jnp.logical_or(found, jnp.logical_and(b == which, j == owner))
    return found


def each_other_row(depth, z, what):
    def each(other, carry):
        @pl.when(other != z)
        def _():
            what(other)

        return carry

    lax.fori_loop(0, depth, each, 0)


def meet(depth, b, me, z, wide=False):
    barrier = pltpu.get_barrier_semaphore()
    y, c = (me // 2) % 2, me % 2
    pl.semaphore_signal(barrier, 1, device_id=(b, me + 1 - 2 * c), device_id_type=MESH)
    pl.semaphore_signal(barrier, 1, device_id=(b, me + 2 - 4 * y), device_id_type=MESH)
    if wide:
        pl.semaphore_signal(barrier, 1, device_id=(1 - b, me), device_id_type=MESH)
        each_other_row(
            depth, z, lambda other: pl.semaphore_signal(barrier, 1, device_id=(b, me + 4 * (other - z)), device_id_type=MESH)
        )
        pl.semaphore_wait(barrier, 2 + depth)
        return

    @pl.when(z > 0)
    def _():
        pl.semaphore_signal(barrier, 1, device_id=(b, me - 4), device_id_type=MESH)

    @pl.when(z < depth - 1)
    def _():
        pl.semaphore_signal(barrier, 1, device_id=(b, me + 4), device_id_type=MESH)

    count = 2 + jnp.where(z > 0, 1, 0) + jnp.where(z < depth - 1, 1, 0)
    pl.semaphore_wait(barrier, count)


def gather_region(depth, npd, rows, base, ranges, swaps, duals, src, dst, hold, local_sem, recv_sem, send_sem):
    b, me, z, y, c = place()
    (a0, a1), (b0, b1) = ranges
    q0 = jnp.where(b == 0, a0, b0)
    q1 = jnp.where(b == 0, a1, b1)
    swap = jnp.where(b == 0, swaps[0], swaps[1])
    core_peer, y_peer = (b, me + 1 - 2 * c), (b, me + 2 - 4 * y)

    def chunk(ref, index):
        return ref.at[pl.ds(pl.multiple_of(index * rows, 8), rows), :]

    def own(i):
        return src.at[pl.ds(pl.multiple_of(base + i * rows, 8), rows), :]

    def remote(kind, q, device, from_own=False):
        k = q - q0
        return pltpu.make_async_remote_copy(
            own(q - me * npd) if from_own else chunk(dst, k), chunk(dst, k), send_sem.at[kind, k], recv_sem.at[k],
            device_id=device, device_id_type=MESH,
        )

    def each_own(what):
        for i in range(npd):
            q = me * npd + i

            @pl.when(jnp.logical_and(q >= q0, q < q1))
            def _():
                what(q, i)

    def kept(i):
        return hold.at[i, pl.ds(0, rows), :]

    def take(q, i):
        return pltpu.make_async_copy(own(i), kept(i), local_sem.at[0, i])

    def put(q, i):
        return pltpu.make_async_copy(kept(i), chunk(dst, q - q0), local_sem.at[1, i])

    def column(j):
        ys = (j // 2) % 2
        return jnp.where(j == swap, 1 - ys, ys)

    def each(core, what):
        def over(zs, t, s):
            for ys in (y, 1 - y):
                j = (zs * 2 + ys) * 2 + core
                col = column(j)
                i = s - t - jnp.where(ys != col, 1, 0) - jnp.where(y != col, 1, 0)
                i = jnp.where(jnp.logical_and(t == 0, ys == y), s, i)
                q = j * npd + i

                @pl.when(jnp.logical_and(jnp.logical_and(i >= 0, i < npd), jnp.logical_and(q >= q0, q < q1)))
                def _():
                    what(q, j)

        def over_step(s):
            def over_far(t, inner):
                @pl.when(z >= t)
                def _():
                    over(z - t, t, s)

                @pl.when(jnp.logical_and(z + t < depth, t > 0))
                def _():
                    over(z + t, t, s)

                return inner

            lax.fori_loop(0, depth, over_far, 0)

        return over_step

    def sends(q, j, act, from_own=False):
        zs, ys = j // 4, (j // 2) % 2
        col, dual = column(j), listed(j, b, duals)
        chain = y == col
        along = jnp.logical_or(chain, dual)

        @pl.when(jnp.logical_and(along, jnp.logical_and(z >= zs, z < depth - 1)))
        def _():
            act(remote(0, q, (b, me + 4), from_own))

        @pl.when(jnp.logical_and(along, jnp.logical_and(z <= zs, z > 0)))
        def _():
            act(remote(1, q, (b, me - 4), from_own))

        start_here = jnp.logical_and(z == zs, ys != col)

        @pl.when(jnp.logical_and(chain != start_here, jnp.logical_or(jnp.logical_not(dual), me == j)))
        def _():
            act(remote(2, q, y_peer, from_own))

        act(remote(3, q, core_peer, from_own))

    def forward(q, j):
        @pl.when(me == j)
        def _():
            sends(q, j, lambda copy: copy.start(), True)

        @pl.when(me != j)
        def _():
            remote(3, q, core_peer).wait_recv()
            sends(q, j, lambda copy: copy.start())

    def begin():
        each_own(lambda q, i: take(q, i).start())

    def swap_own(q, i):
        take(q, i).wait()
        put(q, i).start()

    work = each(c, forward)

    def finish(q, carry):
        j = q // npd

        @pl.when(c == j % 2)
        def _():
            sends(q, j, lambda copy: copy.wait_send())

        @pl.when(c != j % 2)
        def _():
            remote(3, q, core_peer).wait_recv()

        return carry

    def end():
        each_own(swap_own)
        lax.fori_loop(q0, q1, finish, 0)
        each_own(lambda q, i: put(q, i).wait())

    return begin, work, end, npd + depth + 1


def by_branch(b, regions, run):
    if all(rows[0] == rows[1] for _, rows, *_ in regions):
        run(0)
        return
    for which in range(2):
        pl.when(b == which)(lambda which=which: run(which))


def gather_body(depth, regions, *refs):
    count = len(regions)
    src, dsts, scratch = refs[0], refs[1 : 1 + count], refs[1 + count :]
    b, me, z, y, c = place()
    meet(depth, b, me, z)

    def run(which):
        phases = [
            gather_region(depth, npd, rows[which], *rest, src, dsts[r], *scratch[4 * r : 4 * r + 4])
            for r, (npd, rows, *rest) in enumerate(regions)
        ]
        for begin, *_ in phases:
            begin()

        def step(s, carry):
            for phase in phases:
                phase[1](s)
            return carry

        lax.fori_loop(0, max(phase[3] for phase in phases), step, 0)
        for phase in phases:
            phase[2]()

    by_branch(b, regions, run)


def gather_rows(mesh, src, regions, collective_id):
    depth, width = mesh.shape["dp"] // 4, src.shape[1]
    shapes, scratch = [], []
    for npd, rows, _, ranges, *_ in regions:
        count = max(r[1] - r[0] for r in ranges)
        shapes.append(jax.ShapeDtypeStruct((count * max(rows), width), src.dtype))
        scratch += [
            pltpu.VMEM((npd, max(rows), width), src.dtype),
            pltpu.SemaphoreType.DMA((2, npd)),
            pltpu.SemaphoreType.DMA((count,)),
            pltpu.SemaphoreType.DMA((4, count)),
        ]
    return pl.pallas_call(
        functools.partial(gather_body, depth, regions),
        out_shape=shapes,
        in_specs=[ANY],
        out_specs=[ANY] * len(shapes),
        scratch_shapes=scratch,
        compiler_params=pltpu.CompilerParams(collective_id=collective_id, has_side_effects=True),
        cost_estimate=pl.CostEstimate(flops=5 * 10**10, bytes_accessed=2**24, transcendentals=0),
    )(src)


def reduce_region(depth, npd, rows, ranges, swaps, duals, lag, src, out, own, rc, ry, rz, acc, own_sem, rc_sem, ry_sem, rz_sem, send_sem):
    b, me, z, y, c = place()
    (a0, a1), (b0, b1) = ranges
    q0 = jnp.where(b == 0, a0, b0)
    q1 = jnp.where(b == 0, a1, b1)
    swap = jnp.where(b == 0, swaps[0], swaps[1])
    pair0 = q0 // npd // 2
    core_peer, y_peer = (b, me + 1 - 2 * c), (b, me + 2 - 4 * y)
    up, down = (b, jnp.minimum(me + 4, 4 * depth - 1)), (b, jnp.maximum(me - 4, 0))

    def column(j):
        ys = (j // 2) % 2
        return jnp.where(j == swap, 1 - ys, ys)

    def at(ref, *index):
        return ref.at[(*index, pl.ds(0, rows), slice(None))]

    def slot(j, i):
        return (j // 2 - pair0) * npd + i

    def part(j, i):
        return src.at[pl.ds(pl.multiple_of((j * npd + i - q0) * rows, 8), rows), :]

    def keep(j, i):
        return pltpu.make_async_copy(part(j, i), at(own, slot(j, i)), own_sem.at[slot(j, i)])

    def remote(kind, frm, to, sem, k, device):
        return pltpu.make_async_remote_copy(
            frm, to, send_sem.at[kind, k], sem, device_id=device, device_id_type=MESH
        )

    def to_core(j, i):
        k = slot(j, i)
        return remote(0, part(j, i), at(rc, k), rc_sem.at[k], k, core_peer)

    def to_y(j, i):
        k = slot(j, i)
        return remote(1, at(own, k), at(ry, k), ry_sem.at[k], k, y_peer)

    def to_z(j, i, way):
        k = slot(j, i)
        return remote(2, at(own, k), at(rz, way, k), rz_sem.at[way, k], k, (up, down)[way])

    def to_owner(j, i):
        k = slot(j, i)
        return remote(2, at(own, k), at(ry, k), ry_sem.at[k], k, y_peer)

    def owners(n, core, what):
        pos, i = n // npd, n % npd
        rising = pos + jnp.where(pos >= z, 1, 0)
        falling = depth - 1 - pos
        falling = falling - jnp.where(falling <= z, 1, 0)
        zs = jnp.where(pos == depth - 1, z, jnp.where(z >= depth // 2, rising, falling))
        for ys in (0, 1):
            j = (zs * 2 + ys) * 2 + core
            q = j * npd + i

            @pl.when(jnp.logical_and(q >= q0, q < q1))
            def _():
                what(j, i, zs, ys)

    total = depth * npd

    def first(n, carry):
        owners(n, 1 - c, lambda j, i, zs, ys: to_core(j, i).start())
        owners(n, c, lambda j, i, zs, ys: keep(j, i).start())
        return carry

    def cross(j, i, zs, ys):
        @pl.when(jnp.logical_and(column(j) != y, jnp.logical_not(listed(j, b, duals))))
        def _():
            k = slot(j, i)
            keep(j, i).wait()
            to_core(j, i).wait_recv()
            own[k, :rows] = (own[k, :rows].astype(jnp.float32) + rc[k, :rows].astype(jnp.float32)).astype(own.dtype)
            to_y(j, i).start()

    def chain(j, i, zs, ys):
        dual = listed(j, b, duals)

        @pl.when(jnp.logical_or(column(j) == y, dual))
        def _():
            k = slot(j, i)
            keep(j, i).wait()
            to_core(j, i).wait_recv()
            acc[:rows] = own[k, :rows].astype(jnp.float32) + rc[k, :rows].astype(jnp.float32)

            @pl.when(jnp.logical_or(jnp.logical_not(dual), jnp.logical_and(z == zs, ys == y)))
            def _():
                to_y(j, i).wait_recv()
                acc[:rows] += ry[k, :rows].astype(jnp.float32)

            @pl.when(jnp.logical_and(z >= zs, z < depth - 1))
            def _():
                to_z(j, i, 1).wait_recv()
                acc[:rows] += rz[1, k, :rows].astype(jnp.float32)

            @pl.when(jnp.logical_and(z <= zs, z > 0))
            def _():
                to_z(j, i, 0).wait_recv()
                acc[:rows] += rz[0, k, :rows].astype(jnp.float32)

            @pl.when(jnp.logical_and(z == zs, ys == y))
            def _():
                out[i, :rows] = acc[:rows].astype(out.dtype)

            @pl.when(jnp.logical_not(jnp.logical_and(z == zs, ys == y)))
            def _():
                own[k, :rows] = acc[:rows].astype(own.dtype)

            @pl.when(z > zs)
            def _():
                to_z(j, i, 1).start()

            @pl.when(z < zs)
            def _():
                to_z(j, i, 0).start()

            @pl.when(jnp.logical_and(z == zs, ys != y))
            def _():
                @pl.when(dual)
                def _():
                    to_y(j, i).start()

                @pl.when(jnp.logical_not(dual))
                def _():
                    to_owner(j, i).start()

    def step(s):
        @pl.when(s < total)
        def _():
            owners(s, c, cross)

        @pl.when(jnp.logical_and(s >= lag, s < total + lag))
        def _():
            owners(s - lag, c, chain)

    def sent(j, i, zs, ys):
        dual = listed(j, b, duals)

        @pl.when(jnp.logical_and(column(j) != y, jnp.logical_not(dual)))
        def _():
            to_y(j, i).wait_send()

            @pl.when(me == j)
            def _():
                to_owner(j, i).wait_recv()
                out[i, :rows] = ry[slot(j, i), :rows].astype(out.dtype)

        @pl.when(jnp.logical_or(column(j) == y, dual))
        def _():
            @pl.when(z != zs)
            def _():
                to_z(j, i, 0).wait_send()

            @pl.when(jnp.logical_and(z == zs, ys != y))
            def _():
                @pl.when(dual)
                def _():
                    to_y(j, i).wait_send()

                @pl.when(jnp.logical_not(dual))
                def _():
                    to_owner(j, i).wait_send()

    def last(n, carry):
        owners(n, 1 - c, lambda j, i, zs, ys: to_core(j, i).wait_send())
        owners(n, c, sent)
        return carry

    return (
        lambda: lax.fori_loop(0, total, first, 0),
        step,
        lambda: lax.fori_loop(0, total, last, 0),
        total + lag,
    )


def total_steps(depth, values, out, pair, come, far, sent_sem, come_sem, far_sent, far_come):
    b, me, z, y, c = place()
    peers = ((b, me + 1 - 2 * c), (b, me + 2 - 4 * y), (1 - b, me))

    def swap(at, frm):
        return pltpu.make_async_remote_copy(
            pair.at[frm], come.at[at], sent_sem.at[at], come_sem.at[at], device_id=peers[at], device_id_type=MESH
        )

    def to_row(other, landing):
        return pltpu.make_async_remote_copy(
            pair.at[2], far.at[landing], far_sent.at[other], far_come.at[landing],
            device_id=(b, me + 4 * (other - z)), device_id_type=MESH,
        )

    def start():
        pair[0] = values[...]
        swap(0, 0).start()

    def step(s):
        @pl.when(s == 4)
        def _():
            swap(0, 0).wait()
            pair[1] = pair[0] + come[0]
            swap(1, 1).start()

        @pl.when(s == 12)
        def _():
            swap(1, 1).wait()
            pair[2] = pair[1] + come[1]
            each_other_row(depth, z, lambda other: to_row(other, z).start())
            far[z] = pair[2]

        @pl.when(s == 22)
        def _():
            each_other_row(depth, z, lambda other: to_row(other, z).wait_send())
            each_other_row(depth, z, lambda other: to_row(other, other).wait_recv())
            pair[3] = far[0]

            def add(other, carry):
                pair[3] += far[other]
                return carry

            lax.fori_loop(1, depth, add, 0)
            swap(2, 3).start()

    def end():
        swap(2, 3).wait()
        out[...] = pair[3] + come[2]

    return start, step, end


def reduce_body(depth, regions, extra, *refs):
    count, size = len(regions), 10
    many = count + extra
    srcs, outs, scratch = refs[:many], refs[many : 2 * many], refs[2 * many :]
    b, me, z, y, c = place()
    meet(depth, b, me, z, extra)
    side = [total_steps(depth, srcs[count], outs[count], *scratch[size * count :])] if extra else []

    def run(which):
        phases = [
            reduce_region(depth, npd, rows[which], *rest, srcs[r], outs[r], *scratch[size * r : size * (r + 1)])
            for r, (npd, rows, *rest) in enumerate(regions)
        ]
        for begin, *_ in (*phases, *side):
            begin()

        def step(s, carry):
            for phase in (*phases, *side):
                phase[1](s)
            return carry

        lax.fori_loop(0, max(phase[3] for phase in phases), step, 0)
        for phase in (*phases, *side):
            phase[2]()

    by_branch(b, regions, run)


def reduce_rows(mesh, srcs, regions, collective_id, dtype, lag=2, small=None):
    depth, width = mesh.shape["dp"] // 4, srcs[0].shape[1]
    kind = srcs[0].dtype
    shapes, scratch = [], []
    for npd, rows, ranges, *_ in regions:
        pairs = max((r[1] + npd - 1) // npd // 2 + (r[1] + npd - 1) // npd % 2 - r[0] // npd // 2 for r in ranges)
        held = pairs * npd
        block = (held, max(rows), width)
        shapes.append(jax.ShapeDtypeStruct((npd, max(rows), width), dtype))
        scratch += [
            pltpu.VMEM(block, kind),
            pltpu.VMEM(block, kind),
            pltpu.VMEM(block, kind),
            pltpu.VMEM((2, *block), kind),
            pltpu.VMEM((max(rows), width), jnp.float32),
            pltpu.SemaphoreType.DMA((held,)),
            pltpu.SemaphoreType.DMA((held,)),
            pltpu.SemaphoreType.DMA((held,)),
            pltpu.SemaphoreType.DMA((2, held)),
            pltpu.SemaphoreType.DMA((3, held)),
        ]
    vmem = pl.BlockSpec(memory_space=pltpu.VMEM)
    in_specs, out_specs = [ANY] * len(srcs), [vmem] * len(shapes)
    if small is not None:
        shapes.append(jax.ShapeDtypeStruct(small.shape, jnp.float32))
        in_specs.append(vmem)
        out_specs.append(vmem)
        scratch += [pltpu.VMEM((lead, *small.shape), jnp.float32) for lead in (4, 3, depth)]
        scratch += [pltpu.SemaphoreType.DMA((lead,)) for lead in (3, 3, depth, depth)]
        srcs = [*srcs, small]
    return pl.pallas_call(
        functools.partial(reduce_body, depth, tuple((*region, lag) for region in regions), small is not None),
        out_shape=shapes,
        in_specs=in_specs,
        out_specs=out_specs,
        scratch_shapes=scratch,
        compiler_params=pltpu.CompilerParams(
            collective_id=collective_id, has_side_effects=True, vmem_limit_bytes=60 * 2**20
        ),
        cost_estimate=pl.CostEstimate(flops=5 * 10**10, bytes_accessed=2**24, transcendentals=0),
    )(*srcs)
SCALES = (12, 16)
MICRO = 3
GROUPS = 2
EPSILON = 1e-05
BF, F32 = jnp.bfloat16, jnp.float32
MIB = 2**20


def up_to(value, step):
    return (value + step - 1) // step * step


def dot(a, b):
    return jnp.dot(a, b, preferred_element_type=F32)


def dot_bt(a, b):
    return lax.dot_general(a, b, (((1,), (1,)), ((), ())), preferred_element_type=F32)


def dot_at(a, b):
    return lax.dot_general(a, b, (((0,), (0,)), ((), ())), preferred_element_type=F32)


def mean(values):
    return jnp.mean(values, axis=-1, keepdims=True)


def normalise(values):
    centre = values - mean(values)
    rho = lax.rsqrt(mean(centre * centre) + EPSILON)
    return centre * rho, rho


def norm_back(q_gain, xhat, rho):
    return rho * (q_gain - mean(q_gain) - xhat * mean(q_gain * xhat))


def column_sum(values):
    return jnp.sum(values, axis=0, keepdims=True)


VMEM = pl.BlockSpec(memory_space=pltpu.VMEM)


LANES = 128


def panels(ref, lead, rows):
    return jnp.concatenate([ref[(*lead, p, rows, slice(None))] for p in range(ref.shape[-3])], axis=1)


def set_panels(ref, lead, rows, values):
    for p in range(ref.shape[-3]):
        ref[(*lead, p, rows, slice(None))] = values[:, p * LANES : (p + 1) * LANES]


def stride_of(k):
    return k if k % 8 else k + 1


def put_rows(ref, lead, k, values):
    stride = stride_of(k)
    if stride == k:
        set_panels(ref, lead, slice(0, values.shape[0]), values)
        return
    for t in range(values.shape[0] // k):
        set_panels(ref, lead, slice(t * stride, t * stride + k), values[t * k : (t + 1) * k])


def get_rows(ref, lead, k, length):
    stride = stride_of(k)
    if stride == k:
        return panels(ref, lead, slice(0, length))
    return jnp.concatenate([panels(ref, lead, slice(t * stride, t * stride + k)) for t in range(length // k)], axis=0)


def tap_rows(k, r, pitch):
    return pl.ds(r, pitch, stride=stride_of(k))


def at_window(w, pitch):
    return pl.ds(pl.multiple_of(w * pitch, 16), pitch)


def block_of(r, width, off=0):
    return pl.ds(pl.multiple_of(off + r * width, 16), width)


def fit(values, tall):
    rows = values.shape[0]
    if rows >= tall:
        return values[:tall]
    return jnp.concatenate([values, jnp.zeros((tall - rows, values.shape[1]), values.dtype)], axis=0)


def iso_of(n, pitch, pre_iso, bias):
    rows = fit(jnp.tanh(pre_iso + bias[1:2, :]), pitch)
    step = lax.broadcasted_iota(jnp.int32, rows.shape, 0)
    return jnp.where(step < n, rows, 0.0)


def window_of(ref, tall, slots, w):
    per = slots // ref.shape[0]
    return ref[w // per, w % per * tall : (w % per + 1) * tall, :]


def set_iso_rows(n, pitch, tall, slots, live, pre_iso, bias, iso_rows):
    for w in range(slots):
        iso = iso_of(n, pitch, window_of(pre_iso, tall, slots, w), bias)
        iso_rows[w * pitch : (w + 1) * pitch, :] = jnp.where(w < live[0], iso, 0.0).astype(BF)


def each_of(count, what):
    def step(at, carry):
        what(at)
        return carry

    lax.fori_loop(0, count, step, 0)


def down_body(k, n, pitch, tall, off, live, x, weight, bias, pre, act, taps, x_held, w_held, t_held, total, spread, x_sem, w_sem, t_sem):
    slots, length, width = x.shape

    def window(w):
        return pltpu.make_async_copy(x.at[w], x_held.at[w], x_sem.at[w])

    def block(r):
        return pltpu.make_async_copy(weight.at[block_of(r, width, off), :], w_held.at[r], w_sem.at[r])

    def out(w):
        rows = at_window(w, pitch)
        return pltpu.make_async_copy(t_held.at[:, rows, :], taps.at[pl.ds(0, k), rows, :], t_sem.at[w])

    each_of(slots, lambda w: window(w).start())
    each_of(k, lambda r: block(r).start())
    used = n * stride_of(k)
    spread[:, used:, :] = jnp.zeros((spread.shape[0], spread.shape[1] - used, LANES), F32)

    def lay(w):
        window(w).wait()
        put_rows(spread, (), k, x_held[w].astype(F32))
        for r in range(k):
            t_held[r, at_window(w, pitch), :] = panels(spread, (), tap_rows(k, r, pitch)).astype(BF)
        out(w).start()

    each_of(slots, lay)
    total[...] = jnp.zeros_like(total)

    def tap(r):
        block(r).wait()
        total[...] += dot(t_held[r], w_held[r])

    each_of(k, tap)
    for w in range(slots):
        rows = fit(total[w * pitch : (w + 1) * pitch, :] + bias[0:1, :], tall)
        pre[w, :tall] = rows
        step = lax.broadcasted_iota(jnp.int32, rows.shape, 0)
        flag = jnp.where(step == tall - 1, jnp.where(w < live[0], 1.0, 0.0), 0.0)
        act[w * tall : (w + 1) * tall, :] = jnp.where(step < n, jnp.tanh(rows), flag).astype(BF)
    each_of(slots, lambda w: out(w).wait())


def up_body(k, n, pitch, tall, off, live, half, pre_iso, weight, x, gain, bias, own, send, x_held, w_held, o_held, iso_rows, spread,
            x_sem, w_sem, o_sem):
    slots, length, width = x.shape

    def window(w):
        return pltpu.make_async_copy(x.at[w], x_held.at[w], x_sem.at[w])

    def block(r):
        return pltpu.make_async_copy(weight.at[block_of(r, width, off), :], w_held.at[r], w_sem.at[r])

    def out(which, m):
        return pltpu.make_async_copy(o_held.at[which, m], (send, own)[which].at[m], o_sem.at[which, m])

    each_of(k, lambda r: block(r).start())
    each_of(slots, lambda w: window(w).start())
    set_iso_rows(n, pitch, tall, slots, live, pre_iso, bias, iso_rows)

    def tap(r):
        block(r).wait()
        rows = dot(iso_rows[...], w_held[r])
        for w in range(slots):
            set_panels(spread, (w,), tap_rows(k, r, pitch), rows[w * pitch : (w + 1) * pitch])

    each_of(k, tap)

    def finish(m):
        for which, w in enumerate((2 * m + 1 - half[0], 2 * m + half[0])):
            window(w).wait()
            values = get_rows(spread, (w,), k, length) + bias[2:3, :] + x_held[w].astype(F32)
            xhat, _ = normalise(values)
            o_held[which, m] = (xhat * gain[0:1, :] + bias[3:4, :]).astype(BF)
            out(which, m).start()

    each_of(slots // 2, finish)
    for which in range(2):
        each_of(slots // 2, lambda m, which=which: out(which, m).wait())


def up_back_body(k, n, pitch, tall, off, live, half, grad_own, grad_arrived, pre_iso, weight, taps, gain, bias, grad_iso, vectors,
                 grad_taps, part, g_held, w_held, t_held, q_held, p_held, iso_rows, total, spread, g_sem, w_sem, t_sem, q_sem, p_sem):
    (half_slots, length, width), slots = grad_own.shape, 2 * grad_own.shape[0]
    many = slots * pitch

    def window(which, m):
        return pltpu.make_async_copy((grad_own, grad_arrived)[which].at[m], g_held.at[which, m], g_sem.at[which, m])

    def block(r):
        return pltpu.make_async_copy(weight.at[block_of(r, width, off), :], w_held.at[r], w_sem.at[r])

    def tap_in(r):
        return pltpu.make_async_copy(taps.at[r, pl.ds(0, many), :], t_held.at[r], t_sem.at[r])

    def tap_out(r):
        return pltpu.make_async_copy(q_held.at[r], grad_taps.at[r, pl.ds(0, many), :], q_sem.at[r])

    def part_out(r):
        return pltpu.make_async_copy(p_held.at[r % 2], part.at[block_of(r, width, off), :], p_sem.at[r % 2])

    for which in range(2):
        each_of(half_slots, lambda m, which=which: window(which, m).start())

    def fetch(r):
        block(r).start()
        tap_in(r).start()

    each_of(k, fetch)
    set_iso_rows(n, pitch, tall, slots, live, pre_iso, bias, iso_rows)
    used = n * stride_of(k)
    spread[:, used:, :] = jnp.zeros((spread.shape[0], spread.shape[1] - used, LANES), F32)

    def lay(m):
        for which, w in enumerate((2 * m + half[0], 2 * m + 1 - half[0])):
            window(which, m).wait()
            put_rows(spread, (), k, g_held[which, m].astype(F32))
            for r in range(k):
                q_held[r, at_window(w, pitch), :] = panels(spread, (), tap_rows(k, r, pitch)).astype(BF)

    each_of(half_slots, lay)
    vectors[...] = jnp.zeros_like(vectors)
    total[...] = jnp.zeros_like(total)

    def tap(r):
        block(r).wait()
        tap_in(r).wait()
        values = dot(iso_rows[...], w_held[r]) + bias[2:3, :] + t_held[r].astype(F32)
        xhat, rho = normalise(values)
        q = q_held[r].astype(F32)
        residual = norm_back(q * gain[0:1, :], xhat, rho).astype(BF)
        q_held[r] = residual
        tap_out(r).start()
        vectors[0:1, :] += column_sum(q * xhat)
        vectors[3:4, :] += column_sum(residual.astype(F32))
        vectors[4:5, :] += column_sum(q)
        total[...] += dot_bt(residual, w_held[r])

        @pl.when(r >= 2)
        def _():
            part_out(r - 2).wait()

        p_held[r % 2] = dot_at(iso_rows[...], residual).astype(BF)
        part_out(r).start()

    each_of(k, tap)
    for w in range(slots):
        iso = iso_of(n, pitch, window_of(pre_iso, tall, slots, w), bias)
        slope = jnp.where(lax.broadcasted_iota(jnp.int32, iso.shape, 0) < n, 1.0 - iso * iso, 0.0)
        back = jnp.where(w < live[0], total[w * pitch : (w + 1) * pitch, :] * slope, 0.0).astype(BF)
        vectors[2:3, :] += column_sum(back.astype(F32))
        grad_iso[w * tall : (w + 1) * tall, :] = fit(back.astype(F32), tall).astype(BF)
    part_out(k - 2).wait()
    part_out(k - 1).wait()
    each_of(k, lambda r: tap_out(r).wait())


def down_back_body(k, n, pitch, tall, off, live, half, grad_act, pre, grad_taps, taps, weight, keep, send, vector, part, g_held, w_held,
                   t_held, p_held, o_held, rows, spread, g_sem, w_sem, t_sem, p_sem, o_sem):
    slots, (half_slots, length, width) = pre.shape[0], keep.shape
    many = slots * pitch

    def block(r):
        return pltpu.make_async_copy(weight.at[block_of(r, width, off), :], w_held.at[r], w_sem.at[r])

    def grad_in(r):
        return pltpu.make_async_copy(grad_taps.at[r, pl.ds(0, many), :], g_held.at[r], g_sem.at[r])

    def tap_in(r):
        return pltpu.make_async_copy(taps.at[r, pl.ds(0, many), :], t_held.at[r], t_sem.at[r])

    def part_out(r):
        return pltpu.make_async_copy(p_held.at[r % 2], part.at[block_of(r, width, off), :], p_sem.at[r % 2])

    def out(which, m):
        return pltpu.make_async_copy(o_held.at[which, m], (send, keep)[which].at[m], o_sem.at[which, m])

    def fetch(r):
        block(r).start()
        grad_in(r).start()
        tap_in(r).start()

    each_of(k, fetch)
    vector[...] = jnp.zeros_like(vector)
    for w in range(slots):
        act = jnp.tanh(fit(pre[w, :tall], pitch))
        step = lax.broadcasted_iota(jnp.int32, act.shape, 0)
        back = fit(window_of(grad_act, tall, slots, w), pitch) * (1.0 - act * act)
        back = jnp.where(jnp.logical_and(step < n, w < live[0]), back, 0.0).astype(BF)
        vector[...] += column_sum(back.astype(F32))
        rows[w * pitch : (w + 1) * pitch, :] = back

    def tap(r):
        block(r).wait()
        grad_in(r).wait()
        tap_in(r).wait()
        back = dot_bt(rows[...], w_held[r]) + g_held[r].astype(F32)
        for w in range(slots):
            set_panels(spread, (w,), tap_rows(k, r, pitch), back[w * pitch : (w + 1) * pitch])

        @pl.when(r >= 2)
        def _():
            part_out(r - 2).wait()

        p_held[r % 2] = dot_at(t_held[r], rows[...]).astype(BF)
        part_out(r).start()

    each_of(k, tap)

    def finish(m):
        for which, w in enumerate((2 * m + 1 - half[0], 2 * m + half[0])):
            o_held[which, m] = get_rows(spread, (w,), k, length).astype(BF)
            out(which, m).start()

    each_of(half_slots, finish)
    part_out(k - 2).wait()
    part_out(k - 1).wait()
    for which in range(2):
        each_of(half_slots, lambda m, which=which: out(which, m).wait())


SUBLANES = 8


def shifted(ref, start, tall):
    width = ref.shape[1]
    first = pl.multiple_of(start // SUBLANES * SUBLANES, SUBLANES)
    ahead = start % SUBLANES
    tiles = ref[pl.ds(first, tall + SUBLANES), :].reshape(tall // SUBLANES + 1, SUBLANES, width)
    turned = pltpu.roll(tiles, (SUBLANES - ahead) % SUBLANES, 1)
    row = lax.broadcasted_iota(jnp.int32, (tall // SUBLANES, SUBLANES, width), 1)
    return jnp.where(row < SUBLANES - ahead, turned[:-1], turned[1:]).reshape(tall, width).astype(BF)


PACK = 8


def iso_specs(tall, width, pieces):
    def spec(e):
        def at(step, order, count, shift):
            last = jnp.maximum(count[0] - 1, 0) // PACK
            return order[jnp.minimum(step, last) * PACK + e], 0

        return pl.BlockSpec((tall, width), at)

    return [spec(e) for e in range(PACK)]


def scatter_out(order, count, slots_ref, sem, out, tall, step, steps):
    def copy(at, e):
        where = jnp.minimum(at * PACK + e, order.shape[0] - 1)
        return pltpu.make_async_copy(
            slots_ref.at[at % 2, e], out.at[pl.ds(pl.multiple_of(order[where] * tall, SUBLANES), tall), :], sem.at[at % 2, e]
        )

    live = pl.cdiv(count[0], PACK)

    @pl.when(step < live)
    def _():
        for e in range(PACK):
            @pl.when(step * PACK + e < count[0])
            def _():
                copy(step, e).start()

    @pl.when(jnp.logical_and(step >= 1, step <= live))
    def _():
        for e in range(PACK):
            @pl.when((step - 1) * PACK + e < count[0])
            def _():
                copy(step - 1, e).wait()

    @pl.when(jnp.logical_and(step == steps - 1, live == steps))
    def _():
        for e in range(PACK):
            @pl.when(step * PACK + e < count[0])
            def _():
                copy(step, e).wait()


PARTS = 2


def iso_forward_body(tall, pitch, blocks, steps, order, count, shift, *refs):
    acts, (weight, out), rest = refs[:PACK], refs[PACK : PACK + 2], refs[PACK + 2 :]
    buffers, columns, (ready, sem) = rest[:PACK], rest[PACK : PACK + PARTS], rest[PACK + PARTS :]
    step = pl.program_id(0)
    width = weight.shape[1]
    group = PACK // PARTS

    @pl.when(step == 0)
    def _():
        for ref in (*buffers, *columns):
            ref[...] = jnp.zeros_like(ref)

    @pl.when(step * PACK < count[0])
    def _():
        for p in range(PARTS):
            for at in range(group):
                e = p * group + at
                buffers[e][tall : 2 * tall, :] = jnp.where(step * PACK + e < count[0], acts[e][...].astype(F32), 0.0)
                for m in range(blocks):
                    columns[p][at * pitch : at * pitch + tall, m * width : (m + 1) * width] = shifted(
                        buffers[e], tall - shift[m], tall
                    )
            total = dot(columns[p][...], weight[...])
            for at in range(group):
                ready[step % 2, p * group + at] = total[at * pitch : at * pitch + tall].astype(BF)

    scatter_out(order, count, ready, sem, out, tall, step, steps)


def iso_back_body(tall, pitch, blocks, steps, order, count, shift, *refs):
    acts, grads = refs[:PACK], refs[PACK : 2 * PACK]
    (weight, out, kernel_grad), rest = refs[2 * PACK : 2 * PACK + 3], refs[2 * PACK + 3 :]
    buffers, ahead, rest = rest[:PACK], rest[PACK : 2 * PACK], rest[2 * PACK :]
    columns, later, (gathered, ready, sem) = rest[0], rest[1 : 1 + PARTS], rest[1 + PARTS :]
    step = pl.program_id(0)
    width = weight.shape[1]
    group = PACK // PARTS

    @pl.when(step == 0)
    def _():
        for ref in (*buffers, *ahead, columns, *later, gathered, kernel_grad):
            ref[...] = jnp.zeros_like(ref)

    @pl.when(step * PACK < count[0])
    def _():
        for e in range(PACK):
            alive = step * PACK + e < count[0]
            grad = jnp.where(alive, grads[e][...].astype(F32), 0.0)
            ahead[e][:tall, :] = grad
            gathered[e * pitch : e * pitch + tall, :] = grad.astype(BF)
        for p in range(PARTS):
            for at in range(group):
                e = p * group + at
                for m in range(blocks):
                    later[p][at * pitch : at * pitch + tall, m * width : (m + 1) * width] = shifted(ahead[e], shift[m], tall)
            total = dot_bt(later[p][:, :width], weight[:width, :])
            for m in range(1, blocks):
                total += dot_bt(later[p][:, m * width : (m + 1) * width], weight[m * width : (m + 1) * width, :])
            for at in range(group):
                ready[step % 2, p * group + at] = total[at * pitch : at * pitch + tall].astype(BF)
        for e in range(PACK):
            alive = step * PACK + e < count[0]
            buffers[e][tall : 2 * tall, :] = jnp.where(alive, acts[e][...].astype(F32), 0.0)
        for m in range(blocks):
            for e in range(PACK):
                columns[e * pitch : e * pitch + tall, m * width : (m + 1) * width] = shifted(buffers[e], tall - shift[m], tall)
            kernel_grad[m * width : (m + 1) * width, :] += dot_at(columns[:, m * width : (m + 1) * width], gathered[...])

    scatter_out(order, count, ready, sem, out, tall, step, steps)


def iso_call(back, tall, order, count, shift, weight, *windows):
    many, (rows, width) = order.shape[0], windows[0].shape
    blocks = weight.shape[0] // width
    pitch = up_to(tall, 16)
    steps = many // PACK
    held = pl.BlockSpec(weight.shape, lambda step, *_: (0, 0))
    out_shape = [jax.ShapeDtypeStruct((rows, width), BF)]
    out_specs = [ANY]
    copies = [pltpu.VMEM((2 * tall + SUBLANES, width), F32)] * PACK
    halves = [pltpu.VMEM((PACK // PARTS * pitch, blocks * width), BF)] * PARTS
    if back:
        out_shape.append(jax.ShapeDtypeStruct(weight.shape, F32))
        out_specs.append(held)
        scratch = [*copies, *copies, pltpu.VMEM((PACK * pitch, blocks * width), BF), *halves, pltpu.VMEM((PACK * pitch, width), BF)]
    else:
        scratch = [*copies, *halves]
    scratch += [pltpu.VMEM((2, PACK, tall, width), BF), pltpu.SemaphoreType.DMA((2, PACK))]
    body = iso_back_body if back else iso_forward_body
    flops = 2 * many * tall * weight.size * (2 if back else 1) // 3
    return pl.pallas_call(
        functools.partial(body, tall, pitch, blocks, steps),
        out_shape=out_shape,
        grid_spec=pltpu.PrefetchScalarGridSpec(
            num_scalar_prefetch=3,
            grid=(steps,),
            in_specs=[s for _ in windows for s in iso_specs(tall, width, steps)] + [held],
            out_specs=out_specs,
            scratch_shapes=scratch,
        ),
        compiler_params=pltpu.CompilerParams(vmem_limit_bytes=56 * MIB),
        cost_estimate=pl.CostEstimate(flops=flops, bytes_accessed=4 * MIB, transcendentals=0),
    )(order, count, shift, *[v for v in windows for _ in range(PACK)], weight)


def feed_body(per_window, tile, live, own, bo_send, d_out, merge_weight, ff_in, ff_in_bias, ff_out, biases, gains,
              layer_out, grad_own, arrived, merge_grad, in_grad, out_grad, bias_grad, sums,
              slope, hidden_kept, other_slots, grad_slots, merge_sum, in_sum, out_sum, bo_sent, bo_come, back_sent, back_come):
    step, steps = pl.program_id(0), pl.num_programs(0)
    branch, me = lax.axis_index("branch"), lax.axis_index("dp")
    partner = (1 - branch, me)
    block, width = own.shape

    def forth(at):
        return pltpu.make_async_remote_copy(
            bo_send.at[pl.ds(pl.multiple_of(at * block, 8), block), :], other_slots.at[at], bo_sent.at[at], bo_come.at[at],
            device_id=partner, device_id_type=MESH,
        )

    def back_copy(at):
        return pltpu.make_async_remote_copy(
            grad_slots.at[at], arrived.at[pl.ds(pl.multiple_of(at * block, 8), block), :], back_sent.at[at], back_come.at[at],
            device_id=partner, device_id_type=MESH,
        )

    @pl.when(step == 0)
    def _():
        barrier = pltpu.get_barrier_semaphore()
        pl.semaphore_signal(barrier, 1, device_id=partner, device_id_type=MESH)
        pl.semaphore_wait(barrier, 1)
        forth(0).start()
        forth(1).start()
        bias_grad[...] = jnp.zeros_like(bias_grad)
        sums[...] = jnp.zeros_like(sums)
        merge_sum[...] = jnp.zeros_like(merge_sum)
        in_sum[...] = jnp.zeros_like(in_sum)
        out_sum[...] = jnp.zeros_like(out_sum)

    forth(step).wait_recv()

    @pl.when(step + 2 < steps)
    def _():
        forth(step + 2).start()

    alive = jnp.where(2 * (step // per_window) + branch < live[0], 1.0, 0.0)
    own_rows, other_rows = own[...], other_slots[step]
    own_at = pl.ds(pl.multiple_of(branch * width, width), width)
    other_at = pl.ds(pl.multiple_of((1 - branch) * width, width), width)
    merged = dot(own_rows, merge_weight[own_at, :]) + dot(other_rows, merge_weight[other_at, :]) + biases[0:1, :]
    xhat_one, rho_one = normalise(merged)
    normed = (xhat_one * gains[0:1, :] + biases[1:2, :]).astype(BF)
    units = ff_in.shape[1]
    total = merged + biases[2:3, :]
    for u in range(0, units, tile):
        inner = dot(normed, ff_in[:, u : u + tile]) + ff_in_bias[:, u : u + tile]
        phi_total = 0.5 * (1.0 + lax.erf(inner * 0.7071067811865476))
        hidden = (inner * phi_total).astype(BF)
        slope[:, u : u + tile] = phi_total + inner * (jnp.exp(-0.5 * inner * inner) * 0.3989422804014327)
        hidden_kept[:, u : u + tile] = hidden
        total += dot(hidden, ff_out[u : u + tile, :])
    xhat_two, rho_two = normalise(total)
    layer_out[...] = ((xhat_two * gains[1:2, :] + biases[3:4, :]) * alive).astype(BF)
    q = d_out[...].astype(F32) * alive
    grad_sum = norm_back(q * gains[1:2, :], xhat_two, rho_two)
    grad_outer = grad_sum.astype(BF)
    back = jnp.zeros_like(merged)
    for u in range(0, units, tile):
        grad_inner = (dot_bt(grad_outer, ff_out[u : u + tile, :]) * slope[:, u : u + tile]).astype(BF)
        bias_grad[:, u : u + tile] += column_sum(grad_inner.astype(F32))
        back += dot_bt(grad_inner, ff_in[:, u : u + tile])
        in_sum[:, u : u + tile] += dot_at(normed, grad_inner)
        out_sum[u : u + tile, :] += dot_at(hidden_kept[:, u : u + tile], grad_outer)
    grad_merged = (grad_sum + norm_back(back * gains[0:1, :], xhat_one, rho_one)).astype(BF)
    grad_slots[step] = dot_bt(grad_merged, merge_weight[other_at, :]).astype(BF)
    back_copy(step).start()
    grad_own[...] = dot_bt(grad_merged, merge_weight[own_at, :]).astype(BF)
    merge_sum[own_at, :] += dot_at(own_rows, grad_merged)
    merge_sum[other_at, :] += dot_at(other_rows, grad_merged)
    sums[0:1, :] += column_sum(grad_merged.astype(F32))
    sums[1:2, :] += column_sum(back)
    sums[2:3, :] += column_sum(grad_outer.astype(F32))
    sums[3:4, :] += column_sum(q)
    sums[4:5, :] += column_sum(back * xhat_one)
    sums[5:6, :] += column_sum(q * xhat_two)

    @pl.when(step == steps - 1)
    def _():
        merge_grad[...] = merge_sum[...].astype(BF)
        in_grad[...] = in_sum[...].astype(BF)
        out_grad[...] = out_sum[...].astype(BF)

        def finish(at, carry):
            forth(at).wait_send()
            back_copy(at).wait_send()
            back_copy(at).wait_recv()
            return carry

        lax.fori_loop(0, steps, finish, 0)


def feed_call(live, own, bo_send, d_out, merge_weight, ff_in, ff_in_bias, ff_out, biases, gains, per_window, collective_id):
    rows, width = own.shape
    units = ff_in.shape[1]
    steps = MICRO * per_window
    block = rows // steps

    def rowed(columns):
        return pl.BlockSpec((block, columns), lambda step, *_: (step, 0))

    def held(shape):
        return pl.BlockSpec(shape, lambda step, *_: (0, 0), pipeline_mode=pl.Buffered(1))

    def shaped(*shape):
        return jax.ShapeDtypeStruct(shape, BF)

    weights = (merge_weight, ff_in, ff_in_bias, ff_out, biases, gains)
    outs = [(rows, width), (rows, width), (rows, width), merge_weight.shape, ff_in.shape, ff_out.shape]
    return pl.pallas_call(
        functools.partial(feed_body, per_window, 512),
        out_shape=[shaped(*s) for s in outs] + [jax.ShapeDtypeStruct((1, units), F32), jax.ShapeDtypeStruct((8, width), F32)],
        grid_spec=pltpu.PrefetchScalarGridSpec(
            num_scalar_prefetch=1,
            grid=(steps,),
            in_specs=[rowed(width), ANY, rowed(width)] + [held(v.shape) for v in weights],
            out_specs=[rowed(width), rowed(width), ANY] + [held(s) for s in outs[3:]] + [held((1, units)), held((8, width))],
            scratch_shapes=[
                pltpu.VMEM((block, units), F32), pltpu.VMEM((block, units), BF), pltpu.VMEM((steps, block, width), BF),
                pltpu.VMEM((steps, block, width), BF), pltpu.VMEM(merge_weight.shape, F32), pltpu.VMEM(ff_in.shape, F32),
                pltpu.VMEM(ff_out.shape, F32), pltpu.SemaphoreType.DMA((steps,)), pltpu.SemaphoreType.DMA((steps,)),
                pltpu.SemaphoreType.DMA((steps,)), pltpu.SemaphoreType.DMA((steps,)),
            ],
        ),
        compiler_params=pltpu.CompilerParams(vmem_limit_bytes=58 * MIB, collective_id=collective_id, has_side_effects=True),
        cost_estimate=pl.CostEstimate(flops=rows * width * units * 2 * 8, bytes_accessed=40 * MIB, transcendentals=rows * units),
    )(live, own, bo_send, d_out, *weights)


def branch_index_pair(branch, first, second, *operands):
    return lax.cond(branch == 0, first, second, *operands)


def solution(mesh):
    def per_device(inputs, window_count, branch_blocks, branch_gains, branch_biases, merge_weight, ff_in, ff_in_bias, ff_out,
                   shared_biases, shared_gains, d_out):
        members = mesh.shape["dp"]
        branch, me = lax.axis_index("branch"), lax.axis_index("dp")
        slots, length, width = inputs.shape
        group_rows = branch_blocks.shape[2] * members
        share = branch_blocks.shape[2]
        taps_of = [length // k for k in SCALES]
        members = mesh.shape["dp"]
        tall = up_to(max(taps_of) + 1, 8)
        talls = [up_to(n + 1, 8) if members <= 32 else tall for n in taps_of]
        pitches = [up_to(n, 16) for n in taps_of]
        reach = max(SCALES)
        most = slots * max(pitches)
        live = window_count.astype(jnp.int32)
        half = branch.astype(jnp.int32)[None]
        gain, bias = branch_gains, branch_biases[0]

        npd = 8 if share % 64 == 0 else 1
        chunk = share // npd
        down_ranges = tuple((0, -(-k * width // chunk)) for k in SCALES)
        up_starts = [(k + n) * width - group_rows for k, n in zip(SCALES, taps_of)]
        up_ranges = tuple((s // chunk, -(-(s + k * width) // chunk)) for s, k in zip(up_starts, SCALES))
        up_offs = [s - r[0] * chunk for s, r in zip(up_starts, up_ranges)]
        swaps = (-1, 1) if members == 16 else (-1, -1)
        none = ((), ())
        own_rows = branch_blocks.reshape(GROUPS * share, width)
        down_weight, up_weight = gather_rows(
            mesh, own_rows, ((npd, (chunk, chunk), 0, down_ranges, swaps, none), (npd, (chunk, chunk), share, up_ranges, (-1, -1), none)), 1
        )

        blocks = (share + width - 1) // width + 1
        k_of = jnp.where(branch == 0, SCALES[0], SCALES[1])
        n_of = jnp.where(branch == 0, taps_of[0], taps_of[1])
        rows_at = jnp.arange(share)
        padded, shifts, insides, lead = [], [], [], []
        for g in range(GROUPS):
            first = g * group_rows + me * share - k_of * width
            inside = jnp.logical_and(first + rows_at >= 0, first + rows_at < n_of * width)
            start = first // width
            shifts.append(jnp.clip(n_of - 1 - start - jnp.arange(blocks), 0, jnp.where(branch == 0, talls[0], talls[1])))
            lead.append(first - start * width)
            insides.append(inside)
            kept = jnp.where(inside[:, None], own_rows[g * share : (g + 1) * share], 0)
            padded.append(lax.dynamic_update_slice(jnp.zeros((blocks * width, width), BF), kept, (lead[g], 0)))
        iso_weight = jnp.concatenate(padded, axis=0)
        shift = jnp.concatenate(shifts).astype(jnp.int32)

        def windows_shape(kind):
            return jax.ShapeDtypeStruct((slots, tall, width), kind)

        flat_shape = jax.ShapeDtypeStruct((slots * tall, width), BF)
        full = jax.ShapeDtypeStruct((slots // 2, length, width), BF)
        taps_shape = jax.ShapeDtypeStruct((reach, most, width), BF)
        part_shape = jax.ShapeDtypeStruct((max(r[1] - r[0] for r in down_ranges) * chunk, width), BF)
        up_part_shape = jax.ShapeDtypeStruct((max(r[1] - r[0] for r in up_ranges) * chunk, width), BF)
        sm = pl.BlockSpec(memory_space=pltpu.SMEM)

        def call(body, index, off, outs, held, kinds, *operands):
            k, n, pitch = SCALES[index], taps_of[index], pitches[index]
            spec = {"s": sm, "v": VMEM, "h": ANY}
            scratch = {
                "w": pltpu.VMEM((k, width, width), BF), "t": pltpu.VMEM((k, slots * pitch, width), BF),
                "x": pltpu.VMEM((slots, length, width), BF), "o": pltpu.VMEM((2, slots // 2, length, width), BF),
                "p": pltpu.VMEM((2, width, width), BF), "i": pltpu.VMEM((slots * pitch, width), BF),
                "f": pltpu.VMEM((slots * pitch, width), F32),
                "1": pltpu.VMEM((width // LANES, pitch * stride_of(k), LANES), F32),
                "6": pltpu.VMEM((slots, width // LANES, pitch * stride_of(k), LANES), F32),
                "K": pltpu.SemaphoreType.DMA((k,)), "S": pltpu.SemaphoreType.DMA((slots,)),
                "H": pltpu.SemaphoreType.DMA((2, slots // 2)), "P": pltpu.SemaphoreType.DMA((2,)),
            }
            return pl.pallas_call(
                functools.partial(body, k, n, pitch, talls[index], off),
                out_shape=outs,
                in_specs=[spec[s] for s in kinds[: len(operands)]],
                out_specs=tuple(spec[s] for s in kinds[len(operands) :]),
                scratch_shapes=[scratch[s] for s in held],
                compiler_params=pltpu.CompilerParams(vmem_limit_bytes=60 * MIB),
                cost_estimate=pl.CostEstimate(flops=2 * 10**10, bytes_accessed=2**24, transcendentals=0),
            )(*operands)

        def down_of(index):
            def run(*operands):
                return call(down_body, index, 0, (windows_shape(F32), flat_shape, taps_shape), "xwtf1SKS", "shhvvvh",
                            *operands)
            return run

        pre, act, taps = branch_index_pair(branch, down_of(0), down_of(1), live, inputs, down_weight, bias)

        passes = 1 if members <= 32 else slots
        per = slots // passes
        pieces = 2 if per % 2 == 0 else 1

        def spread_windows(values, collective_id):
            rows = tuple(slots * t // 2 for t in talls)
            [every] = gather_rows(mesh, values, ((2, rows, 0, ((0, 2 * members),) * 2, (-1, -1), none),), collective_id)
            return every

        def sum_windows(values, collective_id):
            rows = tuple(per * t // pieces for t in talls)
            parts = values.reshape(members, passes, per * tall, width)
            results = [
                reduce_rows(mesh, [parts[:, p].reshape(-1, width)],
                            ((pieces, rows, ((0, pieces * members),) * 2, (-1, -1), none),), collective_id + p, F32)[0]
                for p in range(passes)
            ]
            return jnp.concatenate(results, axis=0)

        def iso_of_branch(back):
            return [lambda *operands, t=t: iso_call(back, t, *operands) for t in talls]

        acts = spread_windows(act, 3)
        flags = [acts[t - 1 : members * slots * t : t, 0] for t in talls]
        alive = jnp.where(branch == 0, flags[0], flags[1]) > 0.5
        places = jnp.arange(members * slots)
        rank = jnp.sum(jnp.logical_and(alive[None, :], places[None, :] < places[:, None]).astype(jnp.int32), axis=1)
        order = jnp.sum(
            jnp.where(jnp.logical_and(alive[:, None], rank[:, None] == places[None, :]), places[:, None], 0), axis=0
        ).astype(jnp.int32)
        count = jnp.sum(alive.astype(jnp.int32))[None]
        [terms] = branch_index_pair(branch, *iso_of_branch(False), order, count, shift, iso_weight, acts)
        pre_iso = sum_windows(terms, 16)

        def up_of(index):
            def run(*operands):
                return call(up_body, index, up_offs[index], (full, full), "xwoi6SKH", "ssvhhvvhh", *operands)
            return run

        bo_own, bo_send = branch_index_pair(branch, up_of(0), up_of(1), live, half, pre_iso, up_weight, inputs, gain, bias)
        (layer_out, grad_own, arrived, merge_grad, ff_in_grad, ff_out_grad, bias_grad, sums) = feed_call(
            live, bo_own.reshape(-1, width), bo_send.reshape(-1, width), d_out.reshape(-1, width), merge_weight, ff_in,
            ff_in_bias[None], ff_out, shared_biases, shared_gains, 3, 7,
        )
        wide = lax.psum((merge_grad, ff_in_grad, ff_out_grad), ("branch", "dp"))

        def up_back_of(index):
            def run(*operands):
                return call(up_back_body, index, up_offs[index],
                            (flat_shape, jax.ShapeDtypeStruct((8, width), F32), taps_shape, up_part_shape),
                            "owttpif1HKKKP", "sshhvhhvvvvhh", *operands)
            return run

        grad_iso, vectors, grad_taps, up_part = branch_index_pair(
            branch, up_back_of(0), up_back_of(1), live, half, grad_own.reshape(full.shape), arrived.reshape(full.shape), pre_iso, up_weight, taps, gain, bias
        )
        grads = spread_windows(grad_iso, 4)
        back_terms, kernel_grad = branch_index_pair(branch, *iso_of_branch(True), order, count, shift, iso_weight, acts, grads)
        grad_act = sum_windows(back_terms, 32)
        grad_act, wide = lax.optimization_barrier((grad_act, wide))

        def down_back_of(index):
            def run(*operands):
                return call(down_back_body, index, 0, (full, full, jax.ShapeDtypeStruct((1, width), F32), part_shape),
                            "twtpoi6KKKPH", "ssvvhhhhhvh", *operands)
            return run

        values_keep, values_send, down_vector, down_part = branch_index_pair(
            branch, down_back_of(0), down_back_of(1), live, half, grad_act, pre, grad_taps, taps, down_weight
        )
        vectors = jnp.concatenate([vectors[:1], down_vector, vectors[2:5]], axis=0)
        both = jnp.where((jnp.arange(2) == branch)[:, None, None], vectors[None], 0.0).reshape(10, width)
        pieces_of = bias_grad.shape[1] // width
        small = jnp.concatenate([sums, bias_grad.reshape(pieces_of, width), both, jnp.zeros((2, width), F32)])
        arrived_values = lax.ppermute(values_send, "branch", [(0, 1), (1, 0)])
        grad_inputs = (values_keep.astype(F32) + arrived_values.astype(F32)).astype(BF)
        up_sum, down_sum, small = reduce_rows(
            mesh, [up_part, down_part],
            ((npd, (chunk, chunk), up_ranges, (-1, -1), none), (npd, (chunk, chunk), down_ranges, swaps, none)), 5, BF, 6, small,
        )
        up_sum, down_sum = up_sum.reshape(share, width), down_sum.reshape(share, width)
        own_vectors = lax.dynamic_slice_in_dim(small[8 + pieces_of :], 5 * branch, 5, 0)[None]
        bias_total = small[8 : 8 + pieces_of].reshape(-1)

        group_grads = []
        for g, side in enumerate((down_sum, up_sum)):
            at = g * group_rows + me * share + rows_at
            low, high = (0, k_of * width) if g == 0 else ((k_of + n_of) * width, (2 * k_of + n_of) * width)
            iso_rows = lax.dynamic_slice(kernel_grad, (g * blocks * width + lead[g], 0), (share, width))
            outside = jnp.where(jnp.logical_and(at >= low, at < high)[:, None], side.astype(F32), 0.0)
            group_grads.append(jnp.where(insides[g][:, None], iso_rows, outside))
        grad_blocks = jnp.stack(group_grads)[None]
        return (
            layer_out.reshape(MICRO, 1, 1, length, width), grad_inputs[:, None, None], grad_blocks,
            own_vectors[:, 0], own_vectors[:, 1:], wide[0].astype(F32), wide[1].astype(F32), bias_total,
            wide[2].astype(F32), small[:4], small[4:6],
        )

    from jax.sharding import PartitionSpec as P

    placed = (P("dp", None, None), P("dp"), P("branch", None, "dp", None), P("branch", None), P("branch", None, None), P(), P(), P(),
              P(), P(), P(), P("dp", "branch", None, None, None))
    return jax.shard_map(
        per_device, mesh=mesh, in_specs=placed,
        out_specs=(P("dp", "branch", None, None, None), P("dp", "branch", None, None, None), P("branch", None, "dp", None),
                   P("branch", None), P("branch", None, None), P(), P(), P(), P(), P(), P()),
        check_vma=False,
    )
```

```python
import functools
import jax, jax.numpy as jnp
from jax import lax
from jax.experimental import pallas as pl
from jax.experimental.pallas import tpu as pltpu

MESH = pl.DeviceIdType.MESH
ANY = pl.BlockSpec(memory_space=pl.ANY)


def place():
    me = lax.axis_index("dp")
    return lax.axis_index("branch"), me, me // 4, (me // 2) % 2, me % 2


def listed(j, b, lists):
    found = jnp.bool_(False)
    for which, owners in enumerate(lists):
        for owner in owners:
            found = jnp.logical_or(found, jnp.logical_and(b == which, j == owner))
    return found


def each_other_row(depth, z, what):
    def each(other, carry):
        @pl.when(other != z)
        def _():
            what(other)

        return carry

    lax.fori_loop(0, depth, each, 0)


def meet(depth, b, me, z, wide=False):
    barrier = pltpu.get_barrier_semaphore()
    y, c = (me // 2) % 2, me % 2
    pl.semaphore_signal(barrier, 1, device_id=(b, me + 1 - 2 * c), device_id_type=MESH)
    pl.semaphore_signal(barrier, 1, device_id=(b, me + 2 - 4 * y), device_id_type=MESH)
    if wide:
        pl.semaphore_signal(barrier, 1, device_id=(1 - b, me), device_id_type=MESH)
        each_other_row(
            depth, z, lambda other: pl.semaphore_signal(barrier, 1, device_id=(b, me + 4 * (other - z)), device_id_type=MESH)
        )
        pl.semaphore_wait(barrier, 2 + depth)
        return

    @pl.when(z > 0)
    def _():
        pl.semaphore_signal(barrier, 1, device_id=(b, me - 4), device_id_type=MESH)

    @pl.when(z < depth - 1)
    def _():
        pl.semaphore_signal(barrier, 1, device_id=(b, me + 4), device_id_type=MESH)

    count = 2 + jnp.where(z > 0, 1, 0) + jnp.where(z < depth - 1, 1, 0)
    pl.semaphore_wait(barrier, count)


def gather_region(depth, npd, rows, base, ranges, swaps, duals, src, dst, hold, local_sem, recv_sem, send_sem):
    b, me, z, y, c = place()
    (a0, a1), (b0, b1) = ranges
    q0 = jnp.where(b == 0, a0, b0)
    q1 = jnp.where(b == 0, a1, b1)
    swap = jnp.where(b == 0, swaps[0], swaps[1])
    core_peer, y_peer = (b, me + 1 - 2 * c), (b, me + 2 - 4 * y)

    def chunk(ref, index):
        return ref.at[pl.ds(pl.multiple_of(index * rows, 8), rows), :]

    def own(i):
        return src.at[pl.ds(pl.multiple_of(base + i * rows, 8), rows), :]

    def remote(kind, q, device, from_own=False):
        k = q - q0
        return pltpu.make_async_remote_copy(
            own(q - me * npd) if from_own else chunk(dst, k), chunk(dst, k), send_sem.at[kind, k], recv_sem.at[k],
            device_id=device, device_id_type=MESH,
        )

    def each_own(what):
        for i in range(npd):
            q = me * npd + i

            @pl.when(jnp.logical_and(q >= q0, q < q1))
            def _():
                what(q, i)

    def kept(i):
        return hold.at[i, pl.ds(0, rows), :]

    def take(q, i):
        return pltpu.make_async_copy(own(i), kept(i), local_sem.at[0, i])

    def put(q, i):
        return pltpu.make_async_copy(kept(i), chunk(dst, q - q0), local_sem.at[1, i])

    def column(j):
        ys = (j // 2) % 2
        return jnp.where(j == swap, 1 - ys, ys)

    def each(core, what):
        def over(zs, t, s):
            for ys in (y, 1 - y):
                j = (zs * 2 + ys) * 2 + core
                col = column(j)
                i = s - t - jnp.where(ys != col, 1, 0) - jnp.where(y != col, 1, 0)
                i = jnp.where(jnp.logical_and(t == 0, ys == y), s, i)
                q = j * npd + i

                @pl.when(jnp.logical_and(jnp.logical_and(i >= 0, i < npd), jnp.logical_and(q >= q0, q < q1)))
                def _():
                    what(q, j)

        def over_step(s):
            def over_far(t, inner):
                @pl.when(z >= t)
                def _():
                    over(z - t, t, s)

                @pl.when(jnp.logical_and(z + t < depth, t > 0))
                def _():
                    over(z + t, t, s)

                return inner

            lax.fori_loop(0, depth, over_far, 0)

        return over_step

    def sends(q, j, act, from_own=False):
        zs, ys = j // 4, (j // 2) % 2
        col, dual = column(j), listed(j, b, duals)
        chain = y == col
        along = jnp.logical_or(chain, dual)

        @pl.when(jnp.logical_and(along, jnp.logical_and(z >= zs, z < depth - 1)))
        def _():
            act(remote(0, q, (b, me + 4), from_own))

        @pl.when(jnp.logical_and(along, jnp.logical_and(z <= zs, z > 0)))
        def _():
            act(remote(1, q, (b, me - 4), from_own))

        start_here = jnp.logical_and(z == zs, ys != col)

        @pl.when(jnp.logical_and(chain != start_here, jnp.logical_or(jnp.logical_not(dual), me == j)))
        def _():
            act(remote(2, q, y_peer, from_own))

        act(remote(3, q, core_peer, from_own))

    def forward(q, j):
        @pl.when(me == j)
        def _():
            sends(q, j, lambda copy: copy.start(), True)

        @pl.when(me != j)
        def _():
            remote(3, q, core_peer).wait_recv()
            sends(q, j, lambda copy: copy.start())

    def begin():
        each_own(lambda q, i: take(q, i).start())

    def swap_own(q, i):
        take(q, i).wait()
        put(q, i).start()

    work = each(c, forward)

    def finish(q, carry):
        j = q // npd

        @pl.when(c == j % 2)
        def _():
            sends(q, j, lambda copy: copy.wait_send())

        @pl.when(c != j % 2)
        def _():
            remote(3, q, core_peer).wait_recv()

        return carry

    def end():
        each_own(swap_own)
        lax.fori_loop(q0, q1, finish, 0)
        each_own(lambda q, i: put(q, i).wait())

    return begin, work, end, npd + depth + 1


def by_branch(b, regions, run):
    if all(rows[0] == rows[1] for _, rows, *_ in regions):
        run(0)
        return
    for which in range(2):
        pl.when(b == which)(lambda which=which: run(which))


def gather_body(depth, regions, *refs):
    count = len(regions)
    src, dsts, scratch = refs[0], refs[1 : 1 + count], refs[1 + count :]
    b, me, z, y, c = place()
    meet(depth, b, me, z)

    def run(which):
        phases = [
            gather_region(depth, npd, rows[which], *rest, src, dsts[r], *scratch[4 * r : 4 * r + 4])
            for r, (npd, rows, *rest) in enumerate(regions)
        ]
        for begin, *_ in phases:
            begin()

        def step(s, carry):
            for phase in phases:
                phase[1](s)
            return carry

        lax.fori_loop(0, max(phase[3] for phase in phases), step, 0)
        for phase in phases:
            phase[2]()

    by_branch(b, regions, run)


def gather_rows(mesh, src, regions, collective_id):
    depth, width = mesh.shape["dp"] // 4, src.shape[1]
    shapes, scratch = [], []
    for npd, rows, _, ranges, *_ in regions:
        count = max(r[1] - r[0] for r in ranges)
        shapes.append(jax.ShapeDtypeStruct((count * max(rows), width), src.dtype))
        scratch += [
            pltpu.VMEM((npd, max(rows), width), src.dtype),
            pltpu.SemaphoreType.DMA((2, npd)),
            pltpu.SemaphoreType.DMA((count,)),
            pltpu.SemaphoreType.DMA((4, count)),
        ]
    return pl.pallas_call(
        functools.partial(gather_body, depth, regions),
        out_shape=shapes,
        in_specs=[ANY],
        out_specs=[ANY] * len(shapes),
        scratch_shapes=scratch,
        compiler_params=pltpu.CompilerParams(collective_id=collective_id, has_side_effects=True),
        cost_estimate=pl.CostEstimate(flops=5 * 10**10, bytes_accessed=2**24, transcendentals=0),
    )(src)


def reduce_region(depth, npd, rows, ranges, swaps, duals, lag, src, out, own, rc, ry, rz, acc, own_sem, rc_sem, ry_sem, rz_sem, send_sem):
    b, me, z, y, c = place()
    (a0, a1), (b0, b1) = ranges
    q0 = jnp.where(b == 0, a0, b0)
    q1 = jnp.where(b == 0, a1, b1)
    swap = jnp.where(b == 0, swaps[0], swaps[1])
    pair0 = q0 // npd // 2
    core_peer, y_peer = (b, me + 1 - 2 * c), (b, me + 2 - 4 * y)
    up, down = (b, jnp.minimum(me + 4, 4 * depth - 1)), (b, jnp.maximum(me - 4, 0))

    def column(j):
        ys = (j // 2) % 2
        return jnp.where(j == swap, 1 - ys, ys)

    def at(ref, *index):
        return ref.at[(*index, pl.ds(0, rows), slice(None))]

    def slot(j, i):
        return (j // 2 - pair0) * npd + i

    def part(j, i):
        return src.at[pl.ds(pl.multiple_of((j * npd + i - q0) * rows, 8), rows), :]

    def keep(j, i):
        return pltpu.make_async_copy(part(j, i), at(own, slot(j, i)), own_sem.at[slot(j, i)])

    def remote(kind, frm, to, sem, k, device):
        return pltpu.make_async_remote_copy(
            frm, to, send_sem.at[kind, k], sem, device_id=device, device_id_type=MESH
        )

    def to_core(j, i):
        k = slot(j, i)
        return remote(0, part(j, i), at(rc, k), rc_sem.at[k], k, core_peer)

    def to_y(j, i):
        k = slot(j, i)
        return remote(1, at(own, k), at(ry, k), ry_sem.at[k], k, y_peer)

    def to_z(j, i, way):
        k = slot(j, i)
        return remote(2, at(own, k), at(rz, way, k), rz_sem.at[way, k], k, (up, down)[way])

    def to_owner(j, i):
        k = slot(j, i)
        return remote(2, at(own, k), at(ry, k), ry_sem.at[k], k, y_peer)

    def owners(n, core, what):
        pos, i = n // npd, n % npd
        rising = pos + jnp.where(pos >= z, 1, 0)
        falling = depth - 1 - pos
        falling = falling - jnp.where(falling <= z, 1, 0)
        zs = jnp.where(pos == depth - 1, z, jnp.where(z >= depth // 2, rising, falling))
        for ys in (0, 1):
            j = (zs * 2 + ys) * 2 + core
            q = j * npd + i

            @pl.when(jnp.logical_and(q >= q0, q < q1))
            def _():
                what(j, i, zs, ys)

    total = depth * npd

    def first(n, carry):
        owners(n, 1 - c, lambda j, i, zs, ys: to_core(j, i).start())
        owners(n, c, lambda j, i, zs, ys: keep(j, i).start())
        return carry

    def cross(j, i, zs, ys):
        @pl.when(jnp.logical_and(column(j) != y, jnp.logical_not(listed(j, b, duals))))
        def _():
            k = slot(j, i)
            keep(j, i).wait()
            to_core(j, i).wait_recv()
            own[k, :rows] = (own[k, :rows].astype(jnp.float32) + rc[k, :rows].astype(jnp.float32)).astype(own.dtype)
            to_y(j, i).start()

    def chain(j, i, zs, ys):
        dual = listed(j, b, duals)

        @pl.when(jnp.logical_or(column(j) == y, dual))
        def _():
            k = slot(j, i)
            keep(j, i).wait()
            to_core(j, i).wait_recv()
            acc[:rows] = own[k, :rows].astype(jnp.float32) + rc[k, :rows].astype(jnp.float32)

            @pl.when(jnp.logical_or(jnp.logical_not(dual), jnp.logical_and(z == zs, ys == y)))
            def _():
                to_y(j, i).wait_recv()
                acc[:rows] += ry[k, :rows].astype(jnp.float32)

            @pl.when(jnp.logical_and(z >= zs, z < depth - 1))
            def _():
                to_z(j, i, 1).wait_recv()
                acc[:rows] += rz[1, k, :rows].astype(jnp.float32)

            @pl.when(jnp.logical_and(z <= zs, z > 0))
            def _():
                to_z(j, i, 0).wait_recv()
                acc[:rows] += rz[0, k, :rows].astype(jnp.float32)

            @pl.when(jnp.logical_and(z == zs, ys == y))
            def _():
                out[i, :rows] = acc[:rows].astype(out.dtype)

            @pl.when(jnp.logical_not(jnp.logical_and(z == zs, ys == y)))
            def _():
                own[k, :rows] = acc[:rows].astype(own.dtype)

            @pl.when(z > zs)
            def _():
                to_z(j, i, 1).start()

            @pl.when(z < zs)
            def _():
                to_z(j, i, 0).start()

            @pl.when(jnp.logical_and(z == zs, ys != y))
            def _():
                @pl.when(dual)
                def _():
                    to_y(j, i).start()

                @pl.when(jnp.logical_not(dual))
                def _():
                    to_owner(j, i).start()

    def step(s):
        @pl.when(s < total)
        def _():
            owners(s, c, cross)

        @pl.when(jnp.logical_and(s >= lag, s < total + lag))
        def _():
            owners(s - lag, c, chain)

    def sent(j, i, zs, ys):
        dual = listed(j, b, duals)

        @pl.when(jnp.logical_and(column(j) != y, jnp.logical_not(dual)))
        def _():
            to_y(j, i).wait_send()

            @pl.when(me == j)
            def _():
                to_owner(j, i).wait_recv()
                out[i, :rows] = ry[slot(j, i), :rows].astype(out.dtype)

        @pl.when(jnp.logical_or(column(j) == y, dual))
        def _():
            @pl.when(z != zs)
            def _():
                to_z(j, i, 0).wait_send()

            @pl.when(jnp.logical_and(z == zs, ys != y))
            def _():
                @pl.when(dual)
                def _():
                    to_y(j, i).wait_send()

                @pl.when(jnp.logical_not(dual))
                def _():
                    to_owner(j, i).wait_send()

    def last(n, carry):
        owners(n, 1 - c, lambda j, i, zs, ys: to_core(j, i).wait_send())
        owners(n, c, sent)
        return carry

    return (
        lambda: lax.fori_loop(0, total, first, 0),
        step,
        lambda: lax.fori_loop(0, total, last, 0),
        total + lag,
    )


def total_steps(depth, values, out, pair, come, far, sent_sem, come_sem, far_sent, far_come):
    b, me, z, y, c = place()
    peers = ((b, me + 1 - 2 * c), (b, me + 2 - 4 * y), (1 - b, me))

    def swap(at, frm):
        return pltpu.make_async_remote_copy(
            pair.at[frm], come.at[at], sent_sem.at[at], come_sem.at[at], device_id=peers[at], device_id_type=MESH
        )

    def to_row(other, landing):
        return pltpu.make_async_remote_copy(
            pair.at[2], far.at[landing], far_sent.at[other], far_come.at[landing],
            device_id=(b, me + 4 * (other - z)), device_id_type=MESH,
        )

    def start():
        pair[0] = values[...]
        swap(0, 0).start()

    def step(s):
        @pl.when(s == 4)
        def _():
            swap(0, 0).wait()
            pair[1] = pair[0] + come[0]
            swap(1, 1).start()

        @pl.when(s == 12)
        def _():
            swap(1, 1).wait()
            pair[2] = pair[1] + come[1]
            each_other_row(depth, z, lambda other: to_row(other, z).start())
            far[z] = pair[2]

        @pl.when(s == 22)
        def _():
            each_other_row(depth, z, lambda other: to_row(other, z).wait_send())
            each_other_row(depth, z, lambda other: to_row(other, other).wait_recv())
            pair[3] = far[0]

            def add(other, carry):
                pair[3] += far[other]
                return carry

            lax.fori_loop(1, depth, add, 0)
            swap(2, 3).start()

    def end():
        swap(2, 3).wait()
        out[...] = pair[3] + come[2]

    return start, step, end


def reduce_body(depth, regions, extra, *refs):
    count, size = len(regions), 10
    many = count + extra
    srcs, outs, scratch = refs[:many], refs[many : 2 * many], refs[2 * many :]
    b, me, z, y, c = place()
    meet(depth, b, me, z, extra)
    side = [total_steps(depth, srcs[count], outs[count], *scratch[size * count :])] if extra else []

    def run(which):
        phases = [
            reduce_region(depth, npd, rows[which], *rest, srcs[r], outs[r], *scratch[size * r : size * (r + 1)])
            for r, (npd, rows, *rest) in enumerate(regions)
        ]
        for begin, *_ in (*phases, *side):
            begin()

        def step(s, carry):
            for phase in (*phases, *side):
                phase[1](s)
            return carry

        lax.fori_loop(0, max(phase[3] for phase in phases), step, 0)
        for phase in (*phases, *side):
            phase[2]()

    by_branch(b, regions, run)


def reduce_rows(mesh, srcs, regions, collective_id, dtype, lag=2, small=None):
    depth, width = mesh.shape["dp"] // 4, srcs[0].shape[1]
    kind = srcs[0].dtype
    shapes, scratch = [], []
    for npd, rows, ranges, *_ in regions:
        pairs = max((r[1] + npd - 1) // npd // 2 + (r[1] + npd - 1) // npd % 2 - r[0] // npd // 2 for r in ranges)
        held = pairs * npd
        block = (held, max(rows), width)
        shapes.append(jax.ShapeDtypeStruct((npd, max(rows), width), dtype))
        scratch += [
            pltpu.VMEM(block, kind),
            pltpu.VMEM(block, kind),
            pltpu.VMEM(block, kind),
            pltpu.VMEM((2, *block), kind),
            pltpu.VMEM((max(rows), width), jnp.float32),
            pltpu.SemaphoreType.DMA((held,)),
            pltpu.SemaphoreType.DMA((held,)),
            pltpu.SemaphoreType.DMA((held,)),
            pltpu.SemaphoreType.DMA((2, held)),
            pltpu.SemaphoreType.DMA((3, held)),
        ]
    vmem = pl.BlockSpec(memory_space=pltpu.VMEM)
    in_specs, out_specs = [ANY] * len(srcs), [vmem] * len(shapes)
    if small is not None:
        shapes.append(jax.ShapeDtypeStruct(small.shape, jnp.float32))
        in_specs.append(vmem)
        out_specs.append(vmem)
        scratch += [pltpu.VMEM((lead, *small.shape), jnp.float32) for lead in (4, 3, depth)]
        scratch += [pltpu.SemaphoreType.DMA((lead,)) for lead in (3, 3, depth, depth)]
        srcs = [*srcs, small]
    return pl.pallas_call(
        functools.partial(reduce_body, depth, tuple((*region, lag) for region in regions), small is not None),
        out_shape=shapes,
        in_specs=in_specs,
        out_specs=out_specs,
        scratch_shapes=scratch,
        compiler_params=pltpu.CompilerParams(
            collective_id=collective_id, has_side_effects=True, vmem_limit_bytes=60 * 2**20
        ),
        cost_estimate=pl.CostEstimate(flops=5 * 10**10, bytes_accessed=2**24, transcendentals=0),
    )(*srcs)
SCALES = (12, 16)
MICRO = 3
GROUPS = 2
EPSILON = 1e-05
BF, F32 = jnp.bfloat16, jnp.float32
MIB = 2**20


def up_to(value, step):
    return (value + step - 1) // step * step


def dot(a, b):
    return jnp.dot(a, b, preferred_element_type=F32)


def dot_bt(a, b):
    return lax.dot_general(a, b, (((1,), (1,)), ((), ())), preferred_element_type=F32)


def dot_at(a, b):
    return lax.dot_general(a, b, (((0,), (0,)), ((), ())), preferred_element_type=F32)


def mean(values):
    return jnp.mean(values, axis=-1, keepdims=True)


def normalise(values):
    centre = values - mean(values)
    rho = lax.rsqrt(mean(centre * centre) + EPSILON)
    return centre * rho, rho


def norm_back(q_gain, xhat, rho):
    return rho * (q_gain - mean(q_gain) - xhat * mean(q_gain * xhat))


def column_sum(values):
    return jnp.sum(values, axis=0, keepdims=True)


VMEM = pl.BlockSpec(memory_space=pltpu.VMEM)


LANES = 128


def panels(ref, lead, rows):
    return jnp.concatenate([ref[(*lead, p, rows, slice(None))] for p in range(ref.shape[-3])], axis=1)


def set_panels(ref, lead, rows, values):
    for p in range(ref.shape[-3]):
        ref[(*lead, p, rows, slice(None))] = values[:, p * LANES : (p + 1) * LANES]


def stride_of(k):
    return k if k % 8 else k + 1


def put_rows(ref, lead, k, values):
    stride = stride_of(k)
    if stride == k:
        set_panels(ref, lead, slice(0, values.shape[0]), values)
        return
    for t in range(values.shape[0] // k):
        set_panels(ref, lead, slice(t * stride, t * stride + k), values[t * k : (t + 1) * k])


def get_rows(ref, lead, k, length):
    stride = stride_of(k)
    if stride == k:
        return panels(ref, lead, slice(0, length))
    return jnp.concatenate([panels(ref, lead, slice(t * stride, t * stride + k)) for t in range(length // k)], axis=0)


def tap_rows(k, r, pitch):
    return pl.ds(r, pitch, stride=stride_of(k))


def at_window(w, pitch):
    return pl.ds(pl.multiple_of(w * pitch, 16), pitch)


def block_of(r, width, off=0):
    return pl.ds(pl.multiple_of(off + r * width, 16), width)


def fit(values, tall):
    rows = values.shape[0]
    if rows >= tall:
        return values[:tall]
    return jnp.concatenate([values, jnp.zeros((tall - rows, values.shape[1]), values.dtype)], axis=0)


def iso_of(n, pitch, pre_iso, bias):
    rows = fit(jnp.tanh(pre_iso + bias[1:2, :]), pitch)
    step = lax.broadcasted_iota(jnp.int32, rows.shape, 0)
    return jnp.where(step < n, rows, 0.0)


def window_of(ref, tall, slots, w):
    per = slots // ref.shape[0]
    return ref[w // per, w % per * tall : (w % per + 1) * tall, :]


def set_iso_rows(n, pitch, tall, slots, live, pre_iso, bias, iso_rows):
    for w in range(slots):
        iso = iso_of(n, pitch, window_of(pre_iso, tall, slots, w), bias)
        iso_rows[w * pitch : (w + 1) * pitch, :] = jnp.where(w < live[0], iso, 0.0).astype(BF)


def each_of(count, what):
    def step(at, carry):
        what(at)
        return carry

    lax.fori_loop(0, count, step, 0)


def down_body(k, n, pitch, tall, off, live, x, weight, bias, pre, act, taps, x_held, w_held, t_held, total, spread, x_sem, w_sem, t_sem):
    slots, length, width = x.shape

    def window(w):
        return pltpu.make_async_copy(x.at[w], x_held.at[w], x_sem.at[w])

    def block(r):
        return pltpu.make_async_copy(weight.at[block_of(r, width, off), :], w_held.at[r], w_sem.at[r])

    def out(w):
        rows = at_window(w, pitch)
        return pltpu.make_async_copy(t_held.at[:, rows, :], taps.at[pl.ds(0, k), rows, :], t_sem.at[w])

    each_of(slots, lambda w: window(w).start())
    each_of(k, lambda r: block(r).start())
    used = n * stride_of(k)
    spread[:, used:, :] = jnp.zeros((spread.shape[0], spread.shape[1] - used, LANES), F32)

    def lay(w):
        window(w).wait()
        put_rows(spread, (), k, x_held[w].astype(F32))
        for r in range(k):
            t_held[r, at_window(w, pitch), :] = panels(spread, (), tap_rows(k, r, pitch)).astype(BF)
        out(w).start()

    each_of(slots, lay)
    total[...] = jnp.zeros_like(total)

    def tap(r):
        block(r).wait()
        total[...] += dot(t_held[r], w_held[r])

    each_of(k, tap)
    for w in range(slots):
        rows = fit(total[w * pitch : (w + 1) * pitch, :] + bias[0:1, :], tall)
        pre[w, :tall] = rows
        step = lax.broadcasted_iota(jnp.int32, rows.shape, 0)
        flag = jnp.where(step == tall - 1, jnp.where(w < live[0], 1.0, 0.0), 0.0)
        act[w * tall : (w + 1) * tall, :] = jnp.where(step < n, jnp.tanh(rows), flag).astype(BF)
    each_of(slots, lambda w: out(w).wait())


def up_body(k, n, pitch, tall, off, live, half, pre_iso, weight, x, gain, bias, own, send, x_held, w_held, o_held, iso_rows, spread,
            x_sem, w_sem, o_sem):
    slots, length, width = x.shape

    def window(w):
        return pltpu.make_async_copy(x.at[w], x_held.at[w], x_sem.at[w])

    def block(r):
        return pltpu.make_async_copy(weight.at[block_of(r, width, off), :], w_held.at[r], w_sem.at[r])

    def out(which, m):
        return pltpu.make_async_copy(o_held.at[which, m], (send, own)[which].at[m], o_sem.at[which, m])

    each_of(k, lambda r: block(r).start())
    each_of(slots, lambda w: window(w).start())
    set_iso_rows(n, pitch, tall, slots, live, pre_iso, bias, iso_rows)

    def tap(r):
        block(r).wait()
        rows = dot(iso_rows[...], w_held[r])
        for w in range(slots):
            set_panels(spread, (w,), tap_rows(k, r, pitch), rows[w * pitch : (w + 1) * pitch])

    each_of(k, tap)

    def finish(m):
        for which, w in enumerate((2 * m + 1 - half[0], 2 * m + half[0])):
            window(w).wait()
            values = get_rows(spread, (w,), k, length) + bias[2:3, :] + x_held[w].astype(F32)
            xhat, _ = normalise(values)
            o_held[which, m] = (xhat * gain[0:1, :] + bias[3:4, :]).astype(BF)
            out(which, m).start()

    each_of(slots // 2, finish)
    for which in range(2):
        each_of(slots // 2, lambda m, which=which: out(which, m).wait())


def up_back_body(k, n, pitch, tall, off, live, half, grad_own, grad_arrived, pre_iso, weight, taps, gain, bias, grad_iso, vectors,
                 grad_taps, part, g_held, w_held, t_held, q_held, p_held, iso_rows, total, spread, g_sem, w_sem, t_sem, q_sem, p_sem):
    (half_slots, length, width), slots = grad_own.shape, 2 * grad_own.shape[0]
    many = slots * pitch

    def window(which, m):
        return pltpu.make_async_copy((grad_own, grad_arrived)[which].at[m], g_held.at[which, m], g_sem.at[which, m])

    def block(r):
        return pltpu.make_async_copy(weight.at[block_of(r, width, off), :], w_held.at[r], w_sem.at[r])

    def tap_in(r):
        return pltpu.make_async_copy(taps.at[r, pl.ds(0, many), :], t_held.at[r], t_sem.at[r])

    def tap_out(r):
        return pltpu.make_async_copy(q_held.at[r], grad_taps.at[r, pl.ds(0, many), :], q_sem.at[r])

    def part_out(r):
        return pltpu.make_async_copy(p_held.at[r % 2], part.at[block_of(r, width, off), :], p_sem.at[r % 2])

    for which in range(2):
        each_of(half_slots, lambda m, which=which: window(which, m).start())

    def fetch(r):
        block(r).start()
        tap_in(r).start()

    each_of(k, fetch)
    set_iso_rows(n, pitch, tall, slots, live, pre_iso, bias, iso_rows)
    used = n * stride_of(k)
    spread[:, used:, :] = jnp.zeros((spread.shape[0], spread.shape[1] - used, LANES), F32)

    def lay(m):
        for which, w in enumerate((2 * m + half[0], 2 * m + 1 - half[0])):
            window(which, m).wait()
            put_rows(spread, (), k, g_held[which, m].astype(F32))
            for r in range(k):
                q_held[r, at_window(w, pitch), :] = panels(spread, (), tap_rows(k, r, pitch)).astype(BF)

    each_of(half_slots, lay)
    vectors[...] = jnp.zeros_like(vectors)
    total[...] = jnp.zeros_like(total)

    def tap(r):
        block(r).wait()
        tap_in(r).wait()
        values = dot(iso_rows[...], w_held[r]) + bias[2:3, :] + t_held[r].astype(F32)
        xhat, rho = normalise(values)
        q = q_held[r].astype(F32)
        residual = norm_back(q * gain[0:1, :], xhat, rho).astype(BF)
        q_held[r] = residual
        tap_out(r).start()
        vectors[0:1, :] += column_sum(q * xhat)
        vectors[3:4, :] += column_sum(residual.astype(F32))
        vectors[4:5, :] += column_sum(q)
        total[...] += dot_bt(residual, w_held[r])

        @pl.when(r >= 2)
        def _():
            part_out(r - 2).wait()

        p_held[r % 2] = dot_at(iso_rows[...], residual).astype(BF)
        part_out(r).start()

    each_of(k, tap)
    for w in range(slots):
        iso = iso_of(n, pitch, window_of(pre_iso, tall, slots, w), bias)
        slope = jnp.where(lax.broadcasted_iota(jnp.int32, iso.shape, 0) < n, 1.0 - iso * iso, 0.0)
        back = jnp.where(w < live[0], total[w * pitch : (w + 1) * pitch, :] * slope, 0.0).astype(BF)
        vectors[2:3, :] += column_sum(back.astype(F32))
        grad_iso[w * tall : (w + 1) * tall, :] = fit(back.astype(F32), tall).astype(BF)
    part_out(k - 2).wait()
    part_out(k - 1).wait()
    each_of(k, lambda r: tap_out(r).wait())


def down_back_body(k, n, pitch, tall, off, live, half, grad_act, pre, grad_taps, taps, weight, keep, send, vector, part, g_held, w_held,
                   t_held, p_held, o_held, rows, spread, g_sem, w_sem, t_sem, p_sem, o_sem):
    slots, (half_slots, length, width) = pre.shape[0], keep.shape
    many = slots * pitch

    def block(r):
        return pltpu.make_async_copy(weight.at[block_of(r, width, off), :], w_held.at[r], w_sem.at[r])

    def grad_in(r):
        return pltpu.make_async_copy(grad_taps.at[r, pl.ds(0, many), :], g_held.at[r], g_sem.at[r])

    def tap_in(r):
        return pltpu.make_async_copy(taps.at[r, pl.ds(0, many), :], t_held.at[r], t_sem.at[r])

    def part_out(r):
        return pltpu.make_async_copy(p_held.at[r % 2], part.at[block_of(r, width, off), :], p_sem.at[r % 2])

    def out(which, m):
        return pltpu.make_async_copy(o_held.at[which, m], (send, keep)[which].at[m], o_sem.at[which, m])

    def fetch(r):
        block(r).start()
        grad_in(r).start()
        tap_in(r).start()

    each_of(k, fetch)
    vector[...] = jnp.zeros_like(vector)
    for w in range(slots):
        act = jnp.tanh(fit(pre[w, :tall], pitch))
        step = lax.broadcasted_iota(jnp.int32, act.shape, 0)
        back = fit(window_of(grad_act, tall, slots, w), pitch) * (1.0 - act * act)
        back = jnp.where(jnp.logical_and(step < n, w < live[0]), back, 0.0).astype(BF)
        vector[...] += column_sum(back.astype(F32))
        rows[w * pitch : (w + 1) * pitch, :] = back

    def tap(r):
        block(r).wait()
        grad_in(r).wait()
        tap_in(r).wait()
        back = dot_bt(rows[...], w_held[r]) + g_held[r].astype(F32)
        for w in range(slots):
            set_panels(spread, (w,), tap_rows(k, r, pitch), back[w * pitch : (w + 1) * pitch])

        @pl.when(r >= 2)
        def _():
            part_out(r - 2).wait()

        p_held[r % 2] = dot_at(t_held[r], rows[...]).astype(BF)
        part_out(r).start()

    each_of(k, tap)

    def finish(m):
        for which, w in enumerate((2 * m + 1 - half[0], 2 * m + half[0])):
            o_held[which, m] = get_rows(spread, (w,), k, length).astype(BF)
            out(which, m).start()

    each_of(half_slots, finish)
    part_out(k - 2).wait()
    part_out(k - 1).wait()
    for which in range(2):
        each_of(half_slots, lambda m, which=which: out(which, m).wait())


SUBLANES = 8


def shifted(ref, start, tall):
    width = ref.shape[1]
    first = pl.multiple_of(start // SUBLANES * SUBLANES, SUBLANES)
    ahead = start % SUBLANES
    tiles = ref[pl.ds(first, tall + SUBLANES), :].reshape(tall // SUBLANES + 1, SUBLANES, width)
    turned = pltpu.roll(tiles, (SUBLANES - ahead) % SUBLANES, 1)
    row = lax.broadcasted_iota(jnp.int32, (tall // SUBLANES, SUBLANES, width), 1)
    return jnp.where(row < SUBLANES - ahead, turned[:-1], turned[1:]).reshape(tall, width).astype(BF)


PACK = 8


def iso_specs(tall, width, pieces):
    def spec(e):
        def at(step, order, count, shift):
            last = jnp.maximum(count[0] - 1, 0) // PACK
            return order[jnp.minimum(step, last) * PACK + e], 0

        return pl.BlockSpec((tall, width), at)

    return [spec(e) for e in range(PACK)]


def scatter_out(order, count, slots_ref, sem, out, tall, step, steps):
    def copy(at, e):
        where = jnp.minimum(at * PACK + e, order.shape[0] - 1)
        return pltpu.make_async_copy(
            slots_ref.at[at % 2, e], out.at[pl.ds(pl.multiple_of(order[where] * tall, SUBLANES), tall), :], sem.at[at % 2, e]
        )

    live = pl.cdiv(count[0], PACK)

    @pl.when(step < live)
    def _():
        for e in range(PACK):
            @pl.when(step * PACK + e < count[0])
            def _():
                copy(step, e).start()

    @pl.when(jnp.logical_and(step >= 1, step <= live))
    def _():
        for e in range(PACK):
            @pl.when((step - 1) * PACK + e < count[0])
            def _():
                copy(step - 1, e).wait()

    @pl.when(jnp.logical_and(step == steps - 1, live == steps))
    def _():
        for e in range(PACK):
            @pl.when(step * PACK + e < count[0])
            def _():
                copy(step, e).wait()


PARTS = 2


def iso_forward_body(tall, pitch, blocks, steps, order, count, shift, *refs):
    acts, (weight, out), rest = refs[:PACK], refs[PACK : PACK + 2], refs[PACK + 2 :]
    buffers, columns, (ready, sem) = rest[:PACK], rest[PACK : PACK + PARTS], rest[PACK + PARTS :]
    step = pl.program_id(0)
    width = weight.shape[1]
    group = PACK // PARTS

    @pl.when(step == 0)
    def _():
        for ref in (*buffers, *columns):
            ref[...] = jnp.zeros_like(ref)

    @pl.when(step * PACK < count[0])
    def _():
        for p in range(PARTS):
            for at in range(group):
                e = p * group + at
                buffers[e][tall : 2 * tall, :] = jnp.where(step * PACK + e < count[0], acts[e][...].astype(F32), 0.0)
                for m in range(blocks):
                    columns[p][at * pitch : at * pitch + tall, m * width : (m + 1) * width] = shifted(
                        buffers[e], tall - shift[m], tall
                    )
            total = dot(columns[p][...], weight[...])
            for at in range(group):
                ready[step % 2, p * group + at] = total[at * pitch : at * pitch + tall].astype(BF)

    scatter_out(order, count, ready, sem, out, tall, step, steps)


def iso_back_body(tall, pitch, blocks, steps, order, count, shift, *refs):
    acts, grads = refs[:PACK], refs[PACK : 2 * PACK]
    (weight, out, kernel_grad), rest = refs[2 * PACK : 2 * PACK + 3], refs[2 * PACK + 3 :]
    buffers, ahead, rest = rest[:PACK], rest[PACK : 2 * PACK], rest[2 * PACK :]
    columns, later, (gathered, ready, sem) = rest[0], rest[1 : 1 + PARTS], rest[1 + PARTS :]
    step = pl.program_id(0)
    width = weight.shape[1]
    group = PACK // PARTS

    @pl.when(step == 0)
    def _():
        for ref in (*buffers, *ahead, columns, *later, gathered, kernel_grad):
            ref[...] = jnp.zeros_like(ref)

    @pl.when(step * PACK < count[0])
    def _():
        for e in range(PACK):
            alive = step * PACK + e < count[0]
            grad = jnp.where(alive, grads[e][...].astype(F32), 0.0)
            ahead[e][:tall, :] = grad
            gathered[e * pitch : e * pitch + tall, :] = grad.astype(BF)
        for p in range(PARTS):
            for at in range(group):
                e = p * group + at
                for m in range(blocks):
                    later[p][at * pitch : at * pitch + tall, m * width : (m + 1) * width] = shifted(ahead[e], shift[m], tall)
            total = dot_bt(later[p][:, :width], weight[:width, :])
            for m in range(1, blocks):
                total += dot_bt(later[p][:, m * width : (m + 1) * width], weight[m * width : (m + 1) * width, :])
            for at in range(group):
                ready[step % 2, p * group + at] = total[at * pitch : at * pitch + tall].astype(BF)
        for e in range(PACK):
            alive = step * PACK + e < count[0]
            buffers[e][tall : 2 * tall, :] = jnp.where(alive, acts[e][...].astype(F32), 0.0)
        for m in range(blocks):
            for e in range(PACK):
                columns[e * pitch : e * pitch + tall, m * width : (m + 1) * width] = shifted(buffers[e], tall - shift[m], tall)
            kernel_grad[m * width : (m + 1) * width, :] += dot_at(columns[:, m * width : (m + 1) * width], gathered[...])

    scatter_out(order, count, ready, sem, out, tall, step, steps)


def iso_call(back, tall, order, count, shift, weight, *windows):
    many, (rows, width) = order.shape[0], windows[0].shape
    blocks = weight.shape[0] // width
    pitch = up_to(tall, 16)
    steps = many // PACK
    held = pl.BlockSpec(weight.shape, lambda step, *_: (0, 0))
    out_shape = [jax.ShapeDtypeStruct((rows, width), BF)]
    out_specs = [ANY]
    copies = [pltpu.VMEM((2 * tall + SUBLANES, width), F32)] * PACK
    halves = [pltpu.VMEM((PACK // PARTS * pitch, blocks * width), BF)] * PARTS
    if back:
        out_shape.append(jax.ShapeDtypeStruct(weight.shape, F32))
        out_specs.append(held)
        scratch = [*copies, *copies, pltpu.VMEM((PACK * pitch, blocks * width), BF), *halves, pltpu.VMEM((PACK * pitch, width), BF)]
    else:
        scratch = [*copies, *halves]
    scratch += [pltpu.VMEM((2, PACK, tall, width), BF), pltpu.SemaphoreType.DMA((2, PACK))]
    body = iso_back_body if back else iso_forward_body
    flops = 2 * many * tall * weight.size * (2 if back else 1) // 3
    return pl.pallas_call(
        functools.partial(body, tall, pitch, blocks, steps),
        out_shape=out_shape,
        grid_spec=pltpu.PrefetchScalarGridSpec(
            num_scalar_prefetch=3,
            grid=(steps,),
            in_specs=[s for _ in windows for s in iso_specs(tall, width, steps)] + [held],
            out_specs=out_specs,
            scratch_shapes=scratch,
        ),
        compiler_params=pltpu.CompilerParams(vmem_limit_bytes=56 * MIB),
        cost_estimate=pl.CostEstimate(flops=flops, bytes_accessed=4 * MIB, transcendentals=0),
    )(order, count, shift, *[v for v in windows for _ in range(PACK)], weight)


def feed_body(per_window, tile, live, own, bo_send, d_out, merge_weight, ff_in, ff_in_bias, ff_out, biases, gains,
              layer_out, grad_own, arrived, merge_grad, in_grad, out_grad, bias_grad, sums,
              slope, hidden_kept, other_slots, grad_slots, merge_sum, in_sum, out_sum, bo_sent, bo_come, back_sent, back_come):
    step, steps = pl.program_id(0), pl.num_programs(0)
    branch, me = lax.axis_index("branch"), lax.axis_index("dp")
    partner = (1 - branch, me)
    block, width = own.shape

    def forth(at):
        return pltpu.make_async_remote_copy(
            bo_send.at[pl.ds(pl.multiple_of(at * block, 8), block), :], other_slots.at[at], bo_sent.at[at], bo_come.at[at],
            device_id=partner, device_id_type=MESH,
        )

    def back_copy(at):
        return pltpu.make_async_remote_copy(
            grad_slots.at[at], arrived.at[pl.ds(pl.multiple_of(at * block, 8), block), :], back_sent.at[at], back_come.at[at],
            device_id=partner, device_id_type=MESH,
        )

    @pl.when(step == 0)
    def _():
        barrier = pltpu.get_barrier_semaphore()
        pl.semaphore_signal(barrier, 1, device_id=partner, device_id_type=MESH)
        pl.semaphore_wait(barrier, 1)
        forth(0).start()
        forth(1).start()
        forth(2).start()
        forth(3).start()
        bias_grad[...] = jnp.zeros_like(bias_grad)
        sums[...] = jnp.zeros_like(sums)
        merge_sum[...] = jnp.zeros_like(merge_sum)
        in_sum[...] = jnp.zeros_like(in_sum)
        out_sum[...] = jnp.zeros_like(out_sum)

    forth(step).wait_recv()

    @pl.when(step + 4 < steps)
    def _():
        forth(step + 4).start()

    alive = jnp.where(2 * (step // per_window) + branch < live[0], 1.0, 0.0)
    own_rows, other_rows = own[...], other_slots[step]
    own_at = pl.ds(pl.multiple_of(branch * width, width), width)
    other_at = pl.ds(pl.multiple_of((1 - branch) * width, width), width)
    merged = dot(own_rows, merge_weight[own_at, :]) + dot(other_rows, merge_weight[other_at, :]) + biases[0:1, :]
    xhat_one, rho_one = normalise(merged)
    normed = (xhat_one * gains[0:1, :] + biases[1:2, :]).astype(BF)
    units = ff_in.shape[1]
    total = merged + biases[2:3, :]
    for u in range(0, units, tile):
        inner = dot(normed, ff_in[:, u : u + tile]) + ff_in_bias[:, u : u + tile]
        phi_total = 0.5 * (1.0 + lax.erf(inner * 0.7071067811865476))
        hidden = (inner * phi_total).astype(BF)
        slope[:, u : u + tile] = phi_total + inner * (jnp.exp(-0.5 * inner * inner) * 0.3989422804014327)
        hidden_kept[:, u : u + tile] = hidden
        total += dot(hidden, ff_out[u : u + tile, :])
    xhat_two, rho_two = normalise(total)
    layer_out[...] = ((xhat_two * gains[1:2, :] + biases[3:4, :]) * alive).astype(BF)
    q = d_out[...].astype(F32) * alive
    grad_sum = norm_back(q * gains[1:2, :], xhat_two, rho_two)
    grad_outer = grad_sum.astype(BF)
    back = jnp.zeros_like(merged)
    for u in range(0, units, tile):
        grad_inner = (dot_bt(grad_outer, ff_out[u : u + tile, :]) * slope[:, u : u + tile]).astype(BF)
        bias_grad[:, u : u + tile] += column_sum(grad_inner.astype(F32))
        back += dot_bt(grad_inner, ff_in[:, u : u + tile])
        in_sum[:, u : u + tile] += dot_at(normed, grad_inner)
        out_sum[u : u + tile, :] += dot_at(hidden_kept[:, u : u + tile], grad_outer)
    grad_merged = (grad_sum + norm_back(back * gains[0:1, :], xhat_one, rho_one)).astype(BF)
    grad_slots[step] = dot_bt(grad_merged, merge_weight[other_at, :]).astype(BF)
    back_copy(step).start()
    grad_own[...] = dot_bt(grad_merged, merge_weight[own_at, :]).astype(BF)
    merge_sum[own_at, :] += dot_at(own_rows, grad_merged)
    merge_sum[other_at, :] += dot_at(other_rows, grad_merged)
    sums[0:1, :] += column_sum(grad_merged.astype(F32))
    sums[1:2, :] += column_sum(back)
    sums[2:3, :] += column_sum(grad_outer.astype(F32))
    sums[3:4, :] += column_sum(q)
    sums[4:5, :] += column_sum(back * xhat_one)
    sums[5:6, :] += column_sum(q * xhat_two)

    @pl.when(step == steps - 1)
    def _():
        merge_grad[...] = merge_sum[...].astype(BF)
        in_grad[...] = in_sum[...].astype(BF)
        out_grad[...] = out_sum[...].astype(BF)

        def finish(at, carry):
            forth(at).wait_send()
            back_copy(at).wait_send()
            back_copy(at).wait_recv()
            return carry

        lax.fori_loop(0, steps, finish, 0)


def feed_call(live, own, bo_send, d_out, merge_weight, ff_in, ff_in_bias, ff_out, biases, gains, per_window, collective_id):
    rows, width = own.shape
    units = ff_in.shape[1]
    steps = MICRO * per_window
    block = rows // steps

    def rowed(columns):
        return pl.BlockSpec((block, columns), lambda step, *_: (step, 0))

    def held(shape):
        return pl.BlockSpec(shape, lambda step, *_: (0, 0), pipeline_mode=pl.Buffered(1))

    def shaped(*shape):
        return jax.ShapeDtypeStruct(shape, BF)

    weights = (merge_weight, ff_in, ff_in_bias, ff_out, biases, gains)
    outs = [(rows, width), (rows, width), (rows, width), merge_weight.shape, ff_in.shape, ff_out.shape]
    return pl.pallas_call(
        functools.partial(feed_body, per_window, 512),
        out_shape=[shaped(*s) for s in outs] + [jax.ShapeDtypeStruct((1, units), F32), jax.ShapeDtypeStruct((8, width), F32)],
        grid_spec=pltpu.PrefetchScalarGridSpec(
            num_scalar_prefetch=1,
            grid=(steps,),
            in_specs=[rowed(width), ANY, rowed(width)] + [held(v.shape) for v in weights],
            out_specs=[rowed(width), rowed(width), ANY] + [held(s) for s in outs[3:]] + [held((1, units)), held((8, width))],
            scratch_shapes=[
                pltpu.VMEM((block, units), F32), pltpu.VMEM((block, units), BF), pltpu.VMEM((steps, block, width), BF),
                pltpu.VMEM((steps, block, width), BF), pltpu.VMEM(merge_weight.shape, F32), pltpu.VMEM(ff_in.shape, F32),
                pltpu.VMEM(ff_out.shape, F32), pltpu.SemaphoreType.DMA((steps,)), pltpu.SemaphoreType.DMA((steps,)),
                pltpu.SemaphoreType.DMA((steps,)), pltpu.SemaphoreType.DMA((steps,)),
            ],
        ),
        compiler_params=pltpu.CompilerParams(vmem_limit_bytes=58 * MIB, collective_id=collective_id, has_side_effects=True),
        cost_estimate=pl.CostEstimate(flops=rows * width * units * 2 * 8, bytes_accessed=40 * MIB, transcendentals=rows * units),
    )(live, own, bo_send, d_out, *weights)


def branch_index_pair(branch, first, second, *operands):
    return lax.cond(branch == 0, first, second, *operands)


def solution(mesh):
    def per_device(inputs, window_count, branch_blocks, branch_gains, branch_biases, merge_weight, ff_in, ff_in_bias, ff_out,
                   shared_biases, shared_gains, d_out):
        members = mesh.shape["dp"]
        branch, me = lax.axis_index("branch"), lax.axis_index("dp")
        slots, length, width = inputs.shape
        group_rows = branch_blocks.shape[2] * members
        share = branch_blocks.shape[2]
        taps_of = [length // k for k in SCALES]
        members = mesh.shape["dp"]
        tall = up_to(max(taps_of) + 1, 8)
        talls = [up_to(n + 1, 8) if members <= 32 else tall for n in taps_of]
        pitches = [up_to(n, 16) for n in taps_of]
        reach = max(SCALES)
        most = slots * max(pitches)
        live = window_count.astype(jnp.int32)
        half = branch.astype(jnp.int32)[None]
        gain, bias = branch_gains, branch_biases[0]

        npd = 8 if share % 64 == 0 else 1
        chunk = share // npd
        down_ranges = tuple((0, -(-k * width // chunk)) for k in SCALES)
        up_starts = [(k + n) * width - group_rows for k, n in zip(SCALES, taps_of)]
        up_ranges = tuple((s // chunk, -(-(s + k * width) // chunk)) for s, k in zip(up_starts, SCALES))
        up_offs = [s - r[0] * chunk for s, r in zip(up_starts, up_ranges)]
        swaps = (-1, 1) if members == 16 else (-1, -1)
        none = ((), ())
        own_rows = branch_blocks.reshape(GROUPS * share, width)
        down_weight, up_weight = gather_rows(
            mesh, own_rows, ((npd, (chunk, chunk), 0, down_ranges, swaps, none), (npd, (chunk, chunk), share, up_ranges, (-1, -1), none)), 1
        )

        blocks = (share + width - 1) // width + 1
        k_of = jnp.where(branch == 0, SCALES[0], SCALES[1])
        n_of = jnp.where(branch == 0, taps_of[0], taps_of[1])
        rows_at = jnp.arange(share)
        padded, shifts, insides, lead = [], [], [], []
        for g in range(GROUPS):
            first = g * group_rows + me * share - k_of * width
            inside = jnp.logical_and(first + rows_at >= 0, first + rows_at < n_of * width)
            start = first // width
            shifts.append(jnp.clip(n_of - 1 - start - jnp.arange(blocks), 0, jnp.where(branch == 0, talls[0], talls[1])))
            lead.append(first - start * width)
            insides.append(inside)
            kept = jnp.where(inside[:, None], own_rows[g * share : (g + 1) * share], 0)
            padded.append(lax.dynamic_update_slice(jnp.zeros((blocks * width, width), BF), kept, (lead[g], 0)))
        iso_weight = jnp.concatenate(padded, axis=0)
        shift = jnp.concatenate(shifts).astype(jnp.int32)

        def windows_shape(kind):
            return jax.ShapeDtypeStruct((slots, tall, width), kind)

        flat_shape = jax.ShapeDtypeStruct((slots * tall, width), BF)
        full = jax.ShapeDtypeStruct((slots // 2, length, width), BF)
        taps_shape = jax.ShapeDtypeStruct((reach, most, width), BF)
        part_shape = jax.ShapeDtypeStruct((max(r[1] - r[0] for r in down_ranges) * chunk, width), BF)
        up_part_shape = jax.ShapeDtypeStruct((max(r[1] - r[0] for r in up_ranges) * chunk, width), BF)
        sm = pl.BlockSpec(memory_space=pltpu.SMEM)

        def call(body, index, off, outs, held, kinds, *operands):
            k, n, pitch = SCALES[index], taps_of[index], pitches[index]
            spec = {"s": sm, "v": VMEM, "h": ANY}
            scratch = {
                "w": pltpu.VMEM((k, width, width), BF), "t": pltpu.VMEM((k, slots * pitch, width), BF),
                "x": pltpu.VMEM((slots, length, width), BF), "o": pltpu.VMEM((2, slots // 2, length, width), BF),
                "p": pltpu.VMEM((2, width, width), BF), "i": pltpu.VMEM((slots * pitch, width), BF),
                "f": pltpu.VMEM((slots * pitch, width), F32),
                "1": pltpu.VMEM((width // LANES, pitch * stride_of(k), LANES), F32),
                "6": pltpu.VMEM((slots, width // LANES, pitch * stride_of(k), LANES), F32),
                "K": pltpu.SemaphoreType.DMA((k,)), "S": pltpu.SemaphoreType.DMA((slots,)),
                "H": pltpu.SemaphoreType.DMA((2, slots // 2)), "P": pltpu.SemaphoreType.DMA((2,)),
            }
            return pl.pallas_call(
                functools.partial(body, k, n, pitch, talls[index], off),
                out_shape=outs,
                in_specs=[spec[s] for s in kinds[: len(operands)]],
                out_specs=tuple(spec[s] for s in kinds[len(operands) :]),
                scratch_shapes=[scratch[s] for s in held],
                compiler_params=pltpu.CompilerParams(vmem_limit_bytes=60 * MIB),
                cost_estimate=pl.CostEstimate(flops=2 * 10**10, bytes_accessed=2**24, transcendentals=0),
            )(*operands)

        def down_of(index):
            def run(*operands):
                return call(down_body, index, 0, (windows_shape(F32), flat_shape, taps_shape), "xwtf1SKS", "shhvvvh",
                            *operands)
            return run

        pre, act, taps = branch_index_pair(branch, down_of(0), down_of(1), live, inputs, down_weight, bias)

        passes = 1 if members <= 32 else slots
        per = slots // passes
        pieces = 2 if per % 2 == 0 else 1

        def spread_windows(values, collective_id):
            rows = tuple(slots * t // 2 for t in talls)
            [every] = gather_rows(mesh, values, ((2, rows, 0, ((0, 2 * members),) * 2, (-1, -1), none),), collective_id)
            return every

        def sum_windows(values, collective_id):
            rows = tuple(per * t // pieces for t in talls)
            parts = values.reshape(members, passes, per * tall, width)
            results = [
                reduce_rows(mesh, [parts[:, p].reshape(-1, width)],
                            ((pieces, rows, ((0, pieces * members),) * 2, (-1, -1), none),), collective_id + p, F32)[0]
                for p in range(passes)
            ]
            return jnp.concatenate(results, axis=0)

        def iso_of_branch(back):
            return [lambda *operands, t=t: iso_call(back, t, *operands) for t in talls]

        acts = spread_windows(act, 3)
        alive = branch_index_pair(
            branch, *[lambda rows, t=t: rows[t - 1 : members * slots * t : t, 0] > 0.5 for t in talls], acts
        )
        places = jnp.arange(members * slots)
        rank = jnp.sum(jnp.logical_and(alive[None, :], places[None, :] < places[:, None]).astype(jnp.int32), axis=1)
        order = jnp.sum(
            jnp.where(jnp.logical_and(alive[:, None], rank[:, None] == places[None, :]), places[:, None], 0), axis=0
        ).astype(jnp.int32)
        count = jnp.sum(alive.astype(jnp.int32))[None]
        [terms] = branch_index_pair(branch, *iso_of_branch(False), order, count, shift, iso_weight, acts)
        pre_iso = sum_windows(terms, 16)

        def up_of(index):
            def run(*operands):
                return call(up_body, index, up_offs[index], (full, full), "xwoi6SKH", "ssvhhvvhh", *operands)
            return run

        bo_own, bo_send = branch_index_pair(branch, up_of(0), up_of(1), live, half, pre_iso, up_weight, inputs, gain, bias)
        (layer_out, grad_own, arrived, merge_grad, ff_in_grad, ff_out_grad, bias_grad, sums) = feed_call(
            live, bo_own.reshape(-1, width), bo_send.reshape(-1, width), d_out.reshape(-1, width), merge_weight, ff_in,
            ff_in_bias[None], ff_out, shared_biases, shared_gains, 3, 7,
        )
        wide = lax.psum((merge_grad, ff_in_grad, ff_out_grad), ("branch", "dp"))

        def up_back_of(index):
            def run(*operands):
                return call(up_back_body, index, up_offs[index],
                            (flat_shape, jax.ShapeDtypeStruct((8, width), F32), taps_shape, up_part_shape),
                            "owttpif1HKKKP", "sshhvhhvvvvhh", *operands)
            return run

        grad_iso, vectors, grad_taps, up_part = branch_index_pair(
            branch, up_back_of(0), up_back_of(1), live, half, grad_own.reshape(full.shape), arrived.reshape(full.shape), pre_iso, up_weight, taps, gain, bias
        )
        grads = spread_windows(grad_iso, 4)
        back_terms, kernel_grad = branch_index_pair(branch, *iso_of_branch(True), order, count, shift, iso_weight, acts, grads)
        grad_act = sum_windows(back_terms, 32)
        grad_act, wide = lax.optimization_barrier((grad_act, wide))

        def down_back_of(index):
            def run(*operands):
                return call(down_back_body, index, 0, (full, full, jax.ShapeDtypeStruct((1, width), F32), part_shape),
                            "twtpoi6KKKPH", "ssvvhhhhhvh", *operands)
            return run

        values_keep, values_send, down_vector, down_part = branch_index_pair(
            branch, down_back_of(0), down_back_of(1), live, half, grad_act, pre, grad_taps, taps, down_weight
        )
        vectors = jnp.concatenate([vectors[:1], down_vector, vectors[2:5]], axis=0)
        both = jnp.where((jnp.arange(2) == branch)[:, None, None], vectors[None], 0.0).reshape(10, width)
        pieces_of = bias_grad.shape[1] // width
        small = jnp.concatenate([sums, bias_grad.reshape(pieces_of, width), both, jnp.zeros((2, width), F32)])
        arrived_values = lax.ppermute(values_send, "branch", [(0, 1), (1, 0)])
        grad_inputs = (values_keep.astype(F32) + arrived_values.astype(F32)).astype(BF)
        up_sum, down_sum, small = reduce_rows(
            mesh, [up_part, down_part],
            ((npd, (chunk, chunk), up_ranges, (-1, -1), none), (npd, (chunk, chunk), down_ranges, swaps, none)), 5, BF, 6, small,
        )
        up_sum, down_sum = up_sum.reshape(share, width), down_sum.reshape(share, width)
        own_vectors = lax.dynamic_slice_in_dim(small[8 + pieces_of :], 5 * branch, 5, 0)[None]
        bias_total = small[8 : 8 + pieces_of].reshape(-1)

        group_grads = []
        for g, side in enumerate((down_sum, up_sum)):
            at = g * group_rows + me * share + rows_at
            low, high = (0, k_of * width) if g == 0 else ((k_of + n_of) * width, (2 * k_of + n_of) * width)
            iso_rows = lax.dynamic_slice(kernel_grad, (g * blocks * width + lead[g], 0), (share, width))
            outside = jnp.where(jnp.logical_and(at >= low, at < high)[:, None], side.astype(F32), 0.0)
            group_grads.append(jnp.where(insides[g][:, None], iso_rows, outside))
        grad_blocks = jnp.stack(group_grads)[None]
        return (
            layer_out.reshape(MICRO, 1, 1, length, width), grad_inputs[:, None, None], grad_blocks,
            own_vectors[:, 0], own_vectors[:, 1:], wide[0].astype(F32), wide[1].astype(F32), bias_total,
            wide[2].astype(F32), small[:4], small[4:6],
        )

    from jax.sharding import PartitionSpec as P

    placed = (P("dp", None, None), P("dp"), P("branch", None, "dp", None), P("branch", None), P("branch", None, None), P(), P(), P(),
              P(), P(), P(), P("dp", "branch", None, None, None))
    return jax.shard_map(
        per_device, mesh=mesh, in_specs=placed,
        out_specs=(P("dp", "branch", None, None, None), P("dp", "branch", None, None, None), P("branch", None, "dp", None),
                   P("branch", None), P("branch", None, None), P(), P(), P(), P(), P(), P()),
        check_vma=False,
    )
```
